256 devices in a mesh: seq: 16 (over z_lo, x, core), exp: 16 (over y, z_hi).
Axes of the slice: x: 4, y: 4, z: 8 (z_hi: 4, z_lo: 2; z = z_hi * 2 + z_lo), core: 2. Of those that a mesh axis runs over, the one named last changes fastest.
Arguments:
- tokens: bfloat16 [2, 16, 2048, 1024], P(None, 'exp', 'seq'), may hold values from -3 to 3
- queries: bfloat16 [2, 16, 2048, 1024], P(None, 'exp', 'seq'), may hold values from -6 to 6
- key_rows: bfloat16 [2, 16, 2048, 1024], P(None, 'exp', 'seq'), may hold values from -6 to 6
- value_rows: bfloat16 [2, 16, 2048, 1024], P(None, 'exp', 'seq'), may hold values from -6 to 6
- segments: int32 [2, 16, 2048], P(None, 'exp', 'seq'), may hold values from 0 to 3, never falling along the last dimension, each value on 1 to 1024 neighbouring positions
- bias_table: float32 [16, 32], replicated, may hold values from -3 to 5
- out_proj: bfloat16 [1024, 1024], replicated, may hold values from -0.75 to 0.75
- router: bfloat16 [1024, 16], replicated, may hold values from -0.1875 to 0.1875
- gate_weight: bfloat16 [16, 1024, 1408], P('exp'), may hold values from -0.1875 to 0.1875
- up_weight: bfloat16 [16, 1024, 1408], P('exp'), may hold values from -0.1875 to 0.1875
- down_weight: bfloat16 [16, 1408, 1024], P('exp'), may hold values from -0.15625 to 0.15625
- old_table: int32 [16], replicated, may hold values from 0 to 15, each once
- new_table: int32 [16], replicated, may hold values from 0 to 15, as said below
- routes_one: int32 [16, 2048, 2], P('exp', 'seq'), may hold values from 0 to 15, all different within a row; in each aligned block of 128 rows (0 to 127, 128 to 255, ..., all dimensions but the last counted through in order) at most 20 rows name the same one
- routes_two: int32 [16, 2048, 2], P('exp', 'seq'), may hold values from 0 to 15, all different within a row; in each aligned block of 128 rows (0 to 127, 128 to 255, ..., all dimensions but the last counted through in order) at most 20 rows name the same one
Outputs:
- layer_out: bfloat16 [2, 16, 2048, 1024], P(None, 'exp', 'seq')
The draws below stay inside these ranges and needn't reach their ends.
Inputs may be any that keep to these rules, and one draw needn't show every extreme that they name: `old_table`: each position holds a different expert. `new_table`: no expert is served at more than 2 slots, and at least one expert at exactly 2. `routes_one`: the 2 entries of a token differ; in the rows of one device no expert is named more than 20 times, and in some device's rows one is named exactly 20 times. `routes_two`: the 2 entries of a token differ; in the rows of one device no slot is named more than 20 times, and in some device's rows one is named exactly 20 times.
All inputs are finite; a program needn't handle non-finite values.
Results may differ from the reference program's by a relative error of at most 0.006.
Values may be sent and summed in bfloat16 or wider, within the bound.
A program may use at most 128 MiB of HBM per device.

```python
import math
import jax
import jax.numpy as jnp
import numpy as np
from jax import lax

D = 1024
HEADS = 16
HEAD_DIM = 64
FFW = 1408
TOP = 2
WIN_BLOCKS = 4
NBUCK = 32
DOCS = 4
TOK_DEV = 128
EXPERTS = 16
GROUPS = 16
SEQLEN = 2048
CAP = 20
N_SEQ = 16
N_EXP = 16


def query_key_pair(key):
    shape = (2, GROUPS, SEQLEN, HEADS * HEAD_DIM)
    queries = jnp.clip(jax.random.normal(jax.random.fold_in(key, 101), shape, jnp.float32), -5.0, 5.0)
    key_rows = jnp.clip(jax.random.normal(jax.random.fold_in(key, 102), shape, jnp.float32), -5.0, 5.0)
    return (queries, key_rows)


def draw_queries(key, part):
    return query_key_pair(key)[0].astype(jnp.bfloat16)


def draw_key_rows(key, part):
    return query_key_pair(key)[1].astype(jnp.bfloat16)


def draw_new_table(key, part):
    ordering = jax.random.permutation(jax.random.fold_in(key, 201), EXPERTS).astype(jnp.int32)
    chosen_spots = jax.random.permutation(jax.random.fold_in(key, 202), EXPERTS).astype(jnp.int32)
    doubled = max(1, EXPERTS // 4)
    return ordering.at[chosen_spots[:doubled]].set(ordering[chosen_spots[doubled:2 * doubled]])


def steps_of(rng, extent, cuts, low, high):
    factor_of, own = 1.0, jax.random.fold_in(rng, 6)
    for dim, blocks in cuts:
        heights = jnp.exp(jax.random.uniform(jax.random.fold_in(own, dim), (blocks,), jnp.float32, low / len(cuts), high / len(cuts)))
        factor_of = factor_of * jnp.repeat(heights, extent[dim] // blocks).reshape([-1 if axis == dim else 1 for axis in range(len(extent))])
    return factor_of


def split_up(count, total, bound, lean):
    loads = [(1 << 20) // math.isqrt(standing ** lean) + 1 for standing in range(2, count + 1)]
    rest, holding = total - bound - (count - 1), [1] * (count - 1)
    while rest > 0:
        movable = [i for i in range(count - 1) if holding[i] < bound]
        pool, budget = sum([loads[i] for i in movable]), rest
        for i in movable:
            addition = min(bound - holding[i], max(1, budget * loads[i] // pool), rest)
            holding[i] = holding[i] + addition
            rest = rest - addition
    return np.array([bound] + holding)


def uneven_parts(rng, amount, total, bound, slope):
    if amount == 2:
        one = jax.random.randint(rng, (), max(1, total - bound), min(bound, total - 1) + 1)
        return jnp.stack([one, total - one])
    tallies = jnp.asarray(split_up(amount, total, bound, slope), jnp.int32)
    couples = (amount - 1) // 2
    giver, receiver = tallies[1:1 + 2 * couples:2], tallies[2:2 + 2 * couples:2]
    margin = jnp.minimum(giver - 1, bound - receiver)
    moved = jax.random.randint(jax.random.fold_in(rng, 1), (couples,), 0, 1 << 20) % (margin + 1)
    tallies = tallies.at[1:1 + 2 * couples:2].set(giver - moved).at[2:2 + 2 * couples:2].set(receiver + moved)
    return tallies[jax.random.permutation(jax.random.fold_in(rng, 2), amount)]


def assign_block(key, own, number, rows, count, top, reach, skew):
    sequence = jax.random.permutation(key, count)
    crowded, common = portions_of(count, rows * top, reach, skew, True), portions_of(count, rows * top, reach, skew, False)
    places = jnp.arange(count)

    def named(lengths, offset_by):
        used = int((lengths > 0).sum())
        fixed = max(1, used // 4)
        moved = fixed + (places - fixed + offset_by * (used - fixed)) % max(1, count - fixed)
        return jnp.zeros((count,), jnp.int32).at[sequence[jnp.where(places < fixed, places, moved)]].set(jnp.asarray(lengths, jnp.int32))

    lengths = jnp.where(number % 4 == 0, named(crowded, number // 4), named(common, number - number // 4 - 1))
    mixed = jax.random.permutation(jax.random.fold_in(own, 3), count)
    donor, taker = mixed[0:count // 2 * 2:2], mixed[1:count // 2 * 2:2]
    margin = jnp.minimum(lengths[donor] - 1, reach - lengths[taker]) // 2
    margin = jnp.where((donor == sequence[0]) | (taker == sequence[0]) | (lengths[taker] == 0), 0, jnp.maximum(margin, 0))
    moved = jax.random.randint(jax.random.fold_in(own, 4), (count // 2,), 0, 1 << 20) % (margin + 1)
    lengths = lengths.at[donor].add(-moved).at[taker].add(moved)
    items = jnp.searchsorted(jnp.cumsum(lengths), jnp.arange(rows * top), side="right").astype(jnp.int32)
    grid = items.reshape(top, rows).T
    grid = grid[jax.random.permutation(jax.random.fold_in(own, 1), rows)]
    offset_by = jax.random.randint(jax.random.fold_in(own, 2), (rows, 1), 0, top)
    return jnp.take_along_axis(grid, (jnp.arange(top)[None, :] + offset_by) % top, axis=1)


def portions_of(number_of, total, most, skew, full):
    weights = [(1 << 20) // math.isqrt(grade ** skew) + 1 for grade in range(1, number_of + 1)]
    largest = most if full else min(most, max(-(-total // number_of), total * weights[0] // sum(weights)))
    least = 1 if total - largest >= number_of - 1 else 0
    counts, rest = [largest] + [least] * (number_of - 1), total - largest - least * (number_of - 1)
    while rest > 0:
        free = [i for i in range(1, number_of) if counts[i] < largest] or [i for i in range(1, number_of) if counts[i] < most]
        mass, budget = sum([weights[i] for i in free]), rest
        for i in free:
            addition = min(most - counts[i], max(1, budget * weights[i] // mass), rest)
            counts[i] = counts[i] + addition
            rest = rest - addition
    return np.array(counts)


def gaussian(own_key, shape, width, most, pieces=(), kind=jnp.bfloat16):
    drawn = jax.random.normal(own_key, shape, jnp.float32) * width
    if len(pieces) > 0:
        drawn = steps_of(own_key, shape, pieces, -0.22, 0.18) * drawn
    return jnp.clip(drawn, min=-most, max=most).astype(kind)


def setup_inputs(seed: int = 0) -> dict:
    splits = jax.random.split(jax.random.key(seed), 16)
    tokens = gaussian(splits[0], (2, GROUPS, SEQLEN, D), 0.5, 3.0, ((1, 16), (2, 16)))
    queries = draw_queries(jax.random.fold_in(splits[15], 71), 0)
    key_rows = draw_key_rows(jax.random.fold_in(splits[15], 71), 0)
    value_rows = gaussian(splits[3], (2, GROUPS, SEQLEN, HEADS * HEAD_DIM), 1.0, 6.0, ((1, 16), (2, 16)))
    segments = jax.vmap(lambda own: jnp.searchsorted(jnp.cumsum(uneven_parts(own, DOCS, SEQLEN, SEQLEN // 2, 2)), jnp.arange(SEQLEN), side="right"))(jax.random.split(splits[4], 2 * GROUPS)).reshape((2, GROUPS, SEQLEN)).astype(jnp.int32)
    bias_table = jnp.clip(jax.random.uniform(splits[5], (HEADS, NBUCK), jnp.float32, -3.0, 5.0), -3.0, 5.0)
    out_proj = gaussian(splits[6], (HEADS * HEAD_DIM, D), HEAD_DIM ** -0.5, 0.75)
    router = gaussian(splits[7], (D, EXPERTS), D ** -0.5, 0.1875)
    gate_weight = gaussian(splits[8], (EXPERTS, D, FFW), D ** -0.5, 0.1875, ((0, 16),))
    up_weight = gaussian(splits[9], (EXPERTS, D, FFW), D ** -0.5, 0.1875, ((0, 16),))
    down_weight = gaussian(splits[10], (EXPERTS, FFW, D), FFW ** -0.5, 0.15625, ((0, 16),))
    old_table = jax.random.permutation(splits[11], EXPERTS).astype(jnp.int32)
    new_table = draw_new_table(jax.random.fold_in(splits[15], 71), 0)
    routes_one_keys = jax.random.split(jax.random.fold_in(splits[13], 1), GROUPS * SEQLEN // TOK_DEV)
    routes_one_turns = jax.random.permutation(jax.random.fold_in(splits[13], 3), GROUPS * SEQLEN // TOK_DEV)
    routes_one = jax.vmap(lambda own, number: assign_block(jax.random.fold_in(splits[13], 2), own, number, TOK_DEV, EXPERTS, TOP, CAP, 2))(routes_one_keys, routes_one_turns).reshape((GROUPS, SEQLEN, TOP))
    routes_two_keys = jax.random.split(jax.random.fold_in(splits[14], 1), GROUPS * SEQLEN // TOK_DEV)
    routes_two_turns = jax.random.permutation(jax.random.fold_in(splits[14], 3), GROUPS * SEQLEN // TOK_DEV)
    routes_two = jax.vmap(lambda own, number: assign_block(jax.random.fold_in(splits[14], 2), own, number, TOK_DEV, EXPERTS, TOP, CAP, 1))(routes_two_keys, routes_two_turns).reshape((GROUPS, SEQLEN, TOP))
    return dict(tokens=tokens, queries=queries, key_rows=key_rows, value_rows=value_rows, segments=segments, bias_table=bias_table, out_proj=out_proj, router=router, gate_weight=gate_weight, up_weight=up_weight, down_weight=down_weight, old_table=old_table, new_table=new_table, routes_one=routes_one, routes_two=routes_two)


score_scale = 0.125
epsilon = 1e-06
masked_score = -1e+30

def bit_length(distance):
    counted = jnp.zeros_like(distance)
    for exponent in range(NBUCK - 2):
        counted = counted + (distance >= 1 << exponent).astype(jnp.int32)
    return counted

def attend_rows(queries, key_rows, value_rows, segments, bias_table):
    window_len = WIN_BLOCKS * TOK_DEV
    model_width = HEADS * HEAD_DIM

    def one_group(group_args):
        group_queries, group_keys, group_values, group_segments = group_args
        row_starts = jnp.searchsorted(group_segments, group_segments, side='left').astype(jnp.int32)
        padded_keys = jnp.concatenate([jnp.zeros((window_len, model_width), group_keys.dtype), group_keys], axis=0)
        padded_values = jnp.concatenate([jnp.zeros((window_len, model_width), group_values.dtype), group_values], axis=0)

        def one_block(block_index):
            block_start = block_index * TOK_DEV
            query_block = lax.dynamic_slice_in_dim(group_queries, block_start, TOK_DEV, 0)
            key_block = lax.dynamic_slice_in_dim(padded_keys, block_start, window_len + TOK_DEV, 0)
            value_block = lax.dynamic_slice_in_dim(padded_values, block_start, window_len + TOK_DEV, 0)
            block_starts = lax.dynamic_slice_in_dim(row_starts, block_start, TOK_DEV, 0)
            positions = block_start + jnp.arange(TOK_DEV, dtype=jnp.int32)
            key_pos = block_start - window_len + jnp.arange(window_len + TOK_DEV, dtype=jnp.int32)
            distance = positions[:, None] - key_pos[None, :]
            query_heads = query_block.reshape(TOK_DEV, HEADS, HEAD_DIM).astype(jnp.float32)
            key_heads = key_block.reshape(window_len + TOK_DEV, HEADS, HEAD_DIM).astype(jnp.float32)
            value_heads = value_block.reshape(window_len + TOK_DEV, HEADS, HEAD_DIM).astype(jnp.float32)
            sink_key = group_keys[block_starts].reshape(TOK_DEV, HEADS, HEAD_DIM).astype(jnp.float32)
            sink_value = group_values[block_starts].reshape(TOK_DEV, HEADS, HEAD_DIM).astype(jnp.float32)
            window_bias = jnp.take(bias_table, bit_length(jnp.maximum(distance, 0)), axis=1)
            scores = jnp.einsum('qhd,khd->hqk', query_heads, key_heads) * score_scale + window_bias
            visible = (key_pos[None, :] >= block_starts[:, None]) & (distance >= 0) & (distance < window_len)
            scores = jnp.where(visible[None], scores, masked_score)
            sink_scores = jnp.einsum('qhd,qhd->hq', query_heads, sink_key) * score_scale + bias_table[:, NBUCK - 1][:, None]
            sink_visible = positions - block_starts >= window_len
            sink_scores = jnp.where(sink_visible[None], sink_scores, masked_score)
            row_peak = jnp.maximum(lax.optimization_barrier(jnp.max(scores, axis=2)), sink_scores)
            weights = jnp.exp(scores - row_peak[:, :, None])
            sink_weight = jnp.exp(sink_scores - row_peak)
            row_total = lax.optimization_barrier(jnp.sum(weights, axis=2)) + sink_weight
            attn_probs = (weights / row_total[:, :, None]).astype(jnp.bfloat16)
            sink_prob = (sink_weight / row_total).astype(jnp.bfloat16)
            context = jnp.einsum('hqk,khd->qhd', attn_probs.astype(jnp.float32), value_heads)
            context = context + jnp.einsum('hq,qhd->qhd', sink_prob.astype(jnp.float32), sink_value)
            return context.reshape(TOK_DEV, model_width).astype(jnp.bfloat16)
        blocks = lax.map(one_block, jnp.arange(N_SEQ, dtype=jnp.int32))
        return blocks.reshape(SEQLEN, model_width)
    return lax.map(one_group, (queries, key_rows, value_rows, segments))

def mixture(normed, logits, chosen, weight_rows, multiple, gate_weight, up_weight, down_weight):
    picked = jnp.take_along_axis(logits, chosen, axis=1)
    first_gate = jax.nn.sigmoid(picked[:, 0] - picked[:, 1])
    gate_pair = jnp.stack([first_gate, 1.0 - first_gate], axis=1)
    pair_rows = weight_rows.reshape(-1)
    pair_count = pair_rows.shape[0]
    limit = multiple * N_SEQ * N_EXP * CAP
    token_of_pair = jnp.arange(pair_count, dtype=jnp.int32) // TOP
    padded_normed = jnp.concatenate([normed, jnp.zeros((1, D), normed.dtype)], axis=0)
    token_pad = jnp.concatenate([token_of_pair, jnp.full((1,), normed.shape[0], jnp.int32)])

    def one_expert(expert_index, outputs):
        picks = jnp.nonzero(pair_rows == expert_index, size=limit, fill_value=pair_count)[0].astype(jnp.int32)
        rows_in = padded_normed[token_pad[picks]]
        gate_part = jnp.dot(rows_in, gate_weight[expert_index], preferred_element_type=jnp.float32)
        up_part = jnp.dot(rows_in, up_weight[expert_index], preferred_element_type=jnp.float32)
        active = (jax.nn.gelu(gate_part, approximate=True) * up_part).astype(jnp.bfloat16)
        expert_out = jnp.dot(active, down_weight[expert_index], preferred_element_type=jnp.float32).astype(jnp.bfloat16)
        return outputs.at[picks].set(expert_out)
    outputs = lax.fori_loop(0, EXPERTS, one_expert, jnp.zeros((pair_count + 1, D), jnp.bfloat16))
    values = outputs[:pair_count].reshape(-1, TOP, D).astype(jnp.float32)
    return lax.optimization_barrier(jnp.sum(values * gate_pair[:, :, None], axis=1))

def reference(tokens, queries, key_rows, value_rows, segments, bias_table, out_proj, router, gate_weight, up_weight, down_weight, old_table, new_table, routes_one, routes_two):
    holder_of = jnp.zeros((EXPERTS,), jnp.int32).at[old_table].set(jnp.arange(EXPERTS, dtype=jnp.int32))
    second_expert = new_table[routes_two]
    batch_plans = ((routes_one, 1), (second_expert, 2))
    results = []
    for batch_index in range(2):
        context = attend_rows(queries[batch_index], key_rows[batch_index], value_rows[batch_index], segments[batch_index], bias_table)
        flat_context = context.reshape(GROUPS * SEQLEN, HEADS * HEAD_DIM)
        hidden = tokens[batch_index].reshape(GROUPS * SEQLEN, D).astype(jnp.float32) + jnp.dot(flat_context, out_proj, preferred_element_type=jnp.float32)
        normed = (hidden * lax.rsqrt(lax.optimization_barrier(jnp.mean(hidden * hidden, axis=1, keepdims=True)) + epsilon)).astype(jnp.bfloat16)
        logits = jnp.dot(normed, router, preferred_element_type=jnp.float32)
        chosen = batch_plans[batch_index][0].reshape(GROUPS * SEQLEN, TOP)
        weight_rows = holder_of[chosen]
        mixed_out = mixture(normed, logits, chosen, weight_rows, batch_plans[batch_index][1], gate_weight, up_weight, down_weight)
        results.append((hidden + mixed_out).astype(jnp.bfloat16).reshape(GROUPS, SEQLEN, D))
    return jnp.stack(results)
```

```python
import jax
import jax.numpy as jnp
from jax import lax
from jax.experimental import pallas as pl
from jax.experimental.pallas import tpu as pltpu
from jax.sharding import PartitionSpec as P

MESH = pl.DeviceIdType.MESH
BF16 = jnp.bfloat16
F32 = jnp.float32
I32 = jnp.int32

N_SEQ = 16
N_EXP = 16
EXP_Y = 4
EXP_Z = 4
TOK = 128
D = 1024
FFW = 1408
NBUCK = 32
WIN = 4
PAIRS = 8
LANES = 128
HALF = 64
CAP = 20
ROWS = 64
FIRST_ROWS = 24
SINK_BUCKET = 31

EPSILON = 1e-06
MASKED = -1e30


def iota(shape, dim):
    return lax.broadcasted_iota(I32, shape, dim)


def dot(a, b):
    return jnp.dot(a, b, preferred_element_type=F32)


def dot_t(a, b):
    return lax.dot_general(a, b, (((1,), (1,)), ((), ())), preferred_element_type=F32)


def greet(axis, count):
    me = lax.axis_index(axis)
    barrier = pltpu.get_barrier_semaphore()
    for step in range(1, count):
        pl.semaphore_signal(
            barrier, inc=1, device_id={axis: lax.rem(me + step, count)}, device_id_type=MESH
        )
    pl.semaphore_wait(barrier, count - 1)


def bias_of_distance(distance, values):
    result = jnp.full(distance.shape, values[0], F32)
    for bucket in range(1, 10):
        result = jnp.where(distance >= (1 << (bucket - 1)), values[bucket], result)
    return result


def attention_kernel(
    table,
    q_hbm,
    k_hbm,
    v_hbm,
    seg_hbm,
    out_hbm,
    qb,
    kb,
    vb,
    segs,
    segcol,
    bias,
    sink_rows,
    ctx,
    send_sem,
    recv_sem,
    local_sem,
    out_send,
    out_recv,
    out_local,
):
    me = lax.axis_index("seq")
    greet("seq", N_SEQ)

    def parts(target, spot):
        batch = target // PAIRS
        lanes = pl.ds(pl.multiple_of(lax.rem(target, PAIRS) * LANES, LANES), LANES)
        return (
            (k_hbm.at[batch, 0, :, lanes], kb.at[spot + WIN]),
            (v_hbm.at[batch, 0, :, lanes], vb.at[spot + WIN]),
            (q_hbm.at[batch, 0, :, lanes], qb.at[spot]),
            (seg_hbm.at[batch], segs.at[spot + WIN]),
        )

    copies = []
    for step in range(1, N_SEQ):
        target = lax.rem(me + step, N_SEQ)
        for kind, (src, dst) in enumerate(parts(target, me)):
            copy = pltpu.make_async_remote_copy(
                src_ref=src,
                dst_ref=dst,
                send_sem=send_sem.at[kind, step],
                recv_sem=recv_sem.at[kind, step],
                device_id={"seq": target},
                device_id_type=MESH,
            )
            copy.start()
            copies.append(copy)
    own = []
    for kind, (src, dst) in enumerate(parts(me, me)):
        copy = pltpu.make_async_copy(src, dst, local_sem.at[kind])
        copy.start()
        own.append(copy)

    kb[0:WIN] = jnp.zeros((WIN, TOK, LANES), BF16)
    vb[0:WIN] = jnp.zeros((WIN, TOK, LANES), BF16)
    segs[0:WIN] = jnp.full((WIN, 1, TOK), -1, I32)
    first_head = 2 * lax.rem(me, PAIRS)
    qi = iota((TOK, TOK), 0)
    kj = iota((TOK, TOK), 1)
    for head in range(2):
        values = [table[first_head + head, bucket] for bucket in range(10)]
        rows = slice(head * TOK, (head + 1) * TOK)
        merged = jnp.where(kj <= qi, qi - kj, qi - kj + WIN * TOK)
        bias[0, rows, :] = bias_of_distance(merged, values)
        for block in range(1, WIN):
            bias[block, rows, :] = bias_of_distance(qi - kj + (WIN - block) * TOK, values)
    sink_bias = jnp.where(
        iota((2 * TOK, 1), 0) < TOK,
        table[first_head, SINK_BUCKET],
        table[first_head + 1, SINK_BUCKET],
    )

    for copy in own:
        copy.wait()
    for copy in copies:
        copy.wait()

    def columns(block, before):
        row = segs[block]
        segcol[block] = jnp.transpose(jnp.broadcast_to(row, (TOK, TOK)))
        document = iota((8, TOK), 0)
        return before + jnp.where((row < document) & (row >= 0), 1, 0)

    ahead = lax.fori_loop(0, N_SEQ + WIN, columns, jnp.zeros((8, TOK), I32))
    starts = jnp.sum(ahead, axis=1, keepdims=True)

    def sinks(block, sums):
        k_sum, v_sum = sums
        spot = block * TOK + iota((8, TOK), 1)
        pick = jnp.where(spot == starts, 1.0, 0.0).astype(BF16)
        return (k_sum + dot(pick, kb[block + WIN]), v_sum + dot(pick, vb[block + WIN]))

    zero = jnp.zeros((8, LANES), F32)
    k_sink, v_sink = lax.fori_loop(0, N_SEQ, sinks, (zero, zero))
    sink_rows[0] = k_sink
    sink_rows[1] = v_sink

    lane_head = iota((2 * TOK, LANES), 1) // HALF
    row_head = iota((2 * TOK, LANES), 0) // TOK
    own_half = lane_head == row_head
    causal = lax.rem(iota((2 * TOK, TOK), 0), TOK) >= iota((2 * TOK, TOK), 1)

    def twice(value):
        return jnp.concatenate([value, value], axis=0)

    def attend(block, carry):
        query = twice(qb[block].astype(F32) * 0.125)
        query = jnp.where(own_half, query, 0.0)
        query_rows = query.astype(BF16)
        mine = segcol[block + WIN]
        pieces = []
        for near in range(WIN + 1):
            raw = dot_t(query_rows, kb[block + near])
            same = twice(mine == segs[block + near])
            pieces.append((raw, same))
        merged = jnp.where(causal, pieces[WIN][0], pieces[0][0])
        merged_same = jnp.where(
            causal, pieces[WIN][1].astype(I32), pieces[0][1].astype(I32)
        )
        scores = [jnp.where(merged_same > 0, merged + bias[0], MASKED)]
        for near in range(1, WIN):
            raw, same = pieces[near]
            scores.append(jnp.where(same, raw + bias[near], MASKED))
        chosen_doc = iota((8, LANES), 0) == segs[block + WIN][:, 0:1]
        k_row = jnp.sum(jnp.where(chosen_doc, sink_rows[0], 0.0), axis=0, keepdims=True)
        v_row = jnp.sum(jnp.where(chosen_doc, sink_rows[1], 0.0), axis=0, keepdims=True)
        sink_seen = twice(mine[:, 0:1] == segcol[block][:, 0:1])
        sink = jnp.sum(query * k_row, axis=1, keepdims=True) + sink_bias
        sink = jnp.where(sink_seen, sink, MASKED)
        peak = jnp.maximum(jnp.maximum(scores[0], scores[1]), jnp.maximum(scores[2], scores[3]))
        peak = jnp.maximum(jnp.max(peak, axis=1, keepdims=True), sink)
        weights = [jnp.exp(score - peak) for score in scores]
        sink_weight = jnp.exp(sink - peak)
        total = (weights[0] + weights[1]) + (weights[2] + weights[3])
        total = jnp.sum(total, axis=1, keepdims=True) + sink_weight
        mixed = sink_weight * v_row
        mixed = mixed + dot(jnp.where(causal, 0.0, weights[0]).astype(BF16), vb[block])
        mixed = mixed + dot(jnp.where(causal, weights[0], 0.0).astype(BF16), vb[block + WIN])
        for near in range(1, WIN):
            mixed = mixed + dot(weights[near].astype(BF16), vb[block + near])
        mixed = mixed / total
        ctx[block] = jnp.where(
            lane_head[:TOK] == 0, mixed[:TOK], mixed[TOK:]
        ).astype(BF16)
        return carry

    lax.fori_loop(0, N_SEQ, attend, 0)

    batch = me // PAIRS
    lanes = pl.ds(pl.multiple_of(lax.rem(me, PAIRS) * LANES, LANES), LANES)
    outgoing = []
    for step in range(1, N_SEQ):
        target = lax.rem(me + step, N_SEQ)
        copy = pltpu.make_async_remote_copy(
            src_ref=ctx.at[target],
            dst_ref=out_hbm.at[batch, :, lanes],
            send_sem=out_send.at[step],
            recv_sem=out_recv.at[step],
            device_id={"seq": target},
            device_id_type=MESH,
        )
        copy.start()
        outgoing.append(copy)
    mine = pltpu.make_async_copy(ctx.at[me], out_hbm.at[batch, :, lanes], out_local)
    mine.start()
    mine.wait()
    for copy in outgoing:
        copy.wait()


def attention(bias_table, queries, key_rows, value_rows, segments):
    any_spec = pl.BlockSpec(memory_space=pl.ANY)
    return pl.pallas_call(
        attention_kernel,
        out_shape=jax.ShapeDtypeStruct((2, TOK, D), BF16),
        in_specs=[pl.BlockSpec(memory_space=pltpu.SMEM)] + [any_spec] * 4,
        out_specs=any_spec,
        scratch_shapes=[
            pltpu.VMEM((N_SEQ, TOK, LANES), BF16),
            pltpu.VMEM((N_SEQ + WIN, TOK, LANES), BF16),
            pltpu.VMEM((N_SEQ + WIN, TOK, LANES), BF16),
            pltpu.VMEM((N_SEQ + WIN, 1, TOK), I32),
            pltpu.VMEM((N_SEQ + WIN, TOK, TOK), I32),
            pltpu.VMEM((WIN, 2 * TOK, TOK), F32),
            pltpu.VMEM((2, 8, LANES), F32),
            pltpu.VMEM((N_SEQ, TOK, LANES), BF16),
            pltpu.SemaphoreType.DMA((4, N_SEQ)),
            pltpu.SemaphoreType.DMA((4, N_SEQ)),
            pltpu.SemaphoreType.DMA((4,)),
            pltpu.SemaphoreType.DMA((N_SEQ,)),
            pltpu.SemaphoreType.DMA((N_SEQ,)),
            pltpu.SemaphoreType.DMA(()),
        ],
        compiler_params=pltpu.CompilerParams(
            collective_id=0, has_side_effects=True, vmem_limit_bytes=32 << 20
        ),
        name="attention",
    )(bias_table, queries, key_rows, value_rows, segments)


def plane_step(group):
    return group + (group // 2) * (1 - 2 * lax.rem(group, 2))


def expert_kernel(
    ctx,
    tokens,
    out_proj,
    router,
    routes_one,
    routes_two,
    bases,
    serving,
    gate_hbm,
    up_hbm,
    down_hbm,
    out_ref,
    gate_w,
    up_w,
    down_w,
    hidden,
    normed,
    sbuf,
    rbuf,
    ybuf,
    back,
    active,
    w_sem,
    send_sem,
    recv_sem,
    back_send,
    back_recv,
):
    me = lax.axis_index("exp")
    me_y, me_z = me // EXP_Z, lax.rem(me, EXP_Z)
    loads = [
        pltpu.make_async_copy(gate_hbm.at[0], gate_w, w_sem.at[0]),
        pltpu.make_async_copy(up_hbm.at[0], up_w, w_sem.at[1]),
        pltpu.make_async_copy(down_hbm.at[0], down_w, w_sem.at[2]),
    ]
    for load in loads:
        load.start()

    context = ctx[...].reshape(2 * TOK, D)
    for part in range(2):
        cols = slice(part * 512, (part + 1) * 512)
        hidden[:, cols] = tokens[:, 0, :, cols].reshape(2 * TOK, 512).astype(F32) + dot(
            context, out_proj[:, cols]
        )
    rows_value = hidden[...]
    scale = lax.rsqrt(jnp.mean(rows_value * rows_value, axis=1, keepdims=True) + EPSILON)
    normed[...] = (rows_value * scale).astype(BF16)
    logits = dot(normed[...], router[...])

    lane = iota((TOK, LANES), 1)
    lower = jnp.where(iota((TOK, TOK), 0) > lane, 1.0, 0.0).astype(BF16)
    places, weights = [], []
    for batch, routes in enumerate((routes_one, routes_two)):
        named = [routes[0, :, c : c + 1] == lane for c in range(2)]
        member = [jnp.where(hit, 1.0, 0.0) for hit in named]
        member_b = [m.astype(BF16) for m in member]
        counts = [dot(lower, m) for m in member_b]
        counts[1] = counts[1] + jnp.sum(member[0], axis=0, keepdims=True)
        base = bases[batch : batch + 1, :]
        places.append(
            [
                jnp.sum(m * (c + base), axis=1, keepdims=True)
                for m, c in zip(member, counts)
            ]
        )
        difference = member[0] - member[1]
        if batch == 1:
            difference = dot(difference.astype(BF16), serving[...])
        picked = jnp.sum(
            difference[:, :N_EXP] * logits[batch * TOK : (batch + 1) * TOK], axis=1, keepdims=True
        )
        first = jax.nn.sigmoid(picked)
        weights.append([first, 1.0 - first])
    place_rows = [
        jnp.concatenate(
            [
                jnp.transpose(jnp.broadcast_to(places[batch][c], (TOK, TOK)))[0:1, :]
                for batch in range(2)
            ],
            axis=1,
        )
        for c in range(2)
    ]

    greet("exp", N_EXP)

    def target_of(group, dy, sign):
        y = lax.rem(me_y + EXP_Y + sign * dy, EXP_Y)
        z = lax.rem(me_z + EXP_Z + sign * plane_step(group), EXP_Z)
        return y * EXP_Z + z

    outgoing = []
    for group in (3, 1, 2, 0):
        spot = (iota((EXP_Y * ROWS, 2 * TOK), 0) + group * EXP_Y * ROWS).astype(F32)
        plan = jnp.where((spot == place_rows[0]) | (spot == place_rows[1]), 1.0, 0.0).astype(BF16)
        for part in range(2):
            cols = slice(part * 512, (part + 1) * 512)
            sbuf[group * EXP_Y : (group + 1) * EXP_Y, :, cols] = (
                dot(plan, normed[:, cols]).astype(BF16).reshape(EXP_Y, ROWS, 512)
            )
        for dy in range(EXP_Y):
            slot = group * EXP_Y + dy
            if slot == 0:
                continue
            copy = pltpu.make_async_remote_copy(
                src_ref=sbuf.at[slot],
                dst_ref=rbuf.at[slot],
                send_sem=send_sem.at[slot],
                recv_sem=recv_sem.at[slot],
                device_id={"exp": target_of(group, dy, 1)},
                device_id_type=MESH,
            )
            copy.start()
            outgoing.append(copy)
    rbuf[0] = sbuf[0]
    for load in loads:
        load.wait()

    def answer(slot, group, dy):
        return pltpu.make_async_remote_copy(
            src_ref=ybuf.at[slot],
            dst_ref=back.at[slot],
            send_sem=back_send.at[slot],
            recv_sem=back_recv.at[slot],
            device_id={"exp": target_of(group, dy, -1)},
            device_id_type=MESH,
        )

    def arrival(slot, group, dy):
        return pltpu.make_async_remote_copy(
            src_ref=sbuf.at[slot],
            dst_ref=rbuf.at[slot],
            send_sem=send_sem.at[slot],
            recv_sem=recv_sem.at[slot],
            device_id={"exp": target_of(group, dy, 1)},
            device_id_type=MESH,
        )

    def serve(group, carry):
        for dy in range(EXP_Y):
            slot = group * EXP_Y + dy
            if dy == 0:

                @pl.when(group > 0)
                def _():
                    arrival(slot, group, dy).wait_recv()

            else:
                arrival(slot, group, dy).wait_recv()
        inputs = rbuf[pl.ds(group * EXP_Y, EXP_Y)].reshape(EXP_Y * ROWS, D)
        for low, high in ((0, 512), (512, 1024), (1024, FFW)):
            gate = dot(inputs, gate_w[:, low:high])
            up = dot(inputs, up_w[:, low:high])
            inner = 0.7978845608028654 * (gate + 0.044715 * (gate * gate * gate))
            active[:, low:high] = (0.5 * gate * (1.0 + jnp.tanh(inner)) * up).astype(BF16)
        for part in range(2):
            cols = slice(part * 512, (part + 1) * 512)
            ybuf[pl.ds(group * EXP_Y, EXP_Y), :, cols] = (
                dot(active[...], down_w[:, cols]).astype(BF16).reshape(EXP_Y, ROWS, 512)
            )
        for dy in range(EXP_Y):
            slot = group * EXP_Y + dy
            if dy == 0:

                @pl.when(group > 0)
                def _():
                    answer(slot, group, dy).start()

            else:
                answer(slot, group, dy).start()
        return carry

    lax.fori_loop(0, EXP_Z, serve, 0)
    back[0] = ybuf[0]

    result = hidden[...]
    for group in range(EXP_Z):
        for dy in range(EXP_Y):
            if group + dy > 0:
                answer(group * EXP_Y + dy, group, dy).wait_recv()
        spot = (iota((TOK, EXP_Y * ROWS), 1) + group * EXP_Y * ROWS).astype(F32)
        mixes = []
        for batch in range(2):
            mixes.append(
                jnp.where(spot == places[batch][0], weights[batch][0], 0.0)
                + jnp.where(spot == places[batch][1], weights[batch][1], 0.0)
            )
        mix = jnp.concatenate(mixes, axis=0)
        coarse = mix.astype(BF16)
        fine = (mix - coarse.astype(F32)).astype(BF16)
        rows = back[group * EXP_Y : (group + 1) * EXP_Y].reshape(EXP_Y * ROWS, D)
        result = result + dot(coarse, rows) + dot(fine, rows)
    out_ref[...] = result.astype(BF16).reshape(2, 1, TOK, D)
    for copy in outgoing:
        copy.wait_send()
    for group in range(EXP_Z):
        for dy in range(EXP_Y):
            if group + dy > 0:
                answer(group * EXP_Y + dy, group, dy).wait_send()


def experts(
    ctx, tokens, out_proj, router, routes_one, routes_two, bases, serving, gate_w, up_w, down_w
):
    vmem = pl.BlockSpec(memory_space=pltpu.VMEM)
    any_spec = pl.BlockSpec(memory_space=pl.ANY)
    buffer = pltpu.VMEM((N_EXP, ROWS, D), BF16)
    sems = pltpu.SemaphoreType.DMA((N_EXP,))
    return pl.pallas_call(
        expert_kernel,
        out_shape=jax.ShapeDtypeStruct((2, 1, TOK, D), BF16),
        in_specs=[vmem] * 8 + [any_spec] * 3,
        out_specs=vmem,
        scratch_shapes=[
            pltpu.VMEM((D, FFW), BF16),
            pltpu.VMEM((D, FFW), BF16),
            pltpu.VMEM((FFW, D), BF16),
            pltpu.VMEM((2 * TOK, D), F32),
            pltpu.VMEM((2 * TOK, D), BF16),
            buffer,
            buffer,
            buffer,
            buffer,
            pltpu.VMEM((EXP_Y * ROWS, FFW), BF16),
            pltpu.SemaphoreType.DMA((3,)),
            sems,
            sems,
            sems,
            sems,
        ],
        compiler_params=pltpu.CompilerParams(
            collective_id=1, has_side_effects=True, vmem_limit_bytes=56 << 20
        ),
        name="experts",
    )(ctx, tokens, out_proj, router, routes_one, routes_two, bases, serving, gate_w, up_w, down_w)


def slot_tables(old_table, new_table):
    ids = jnp.arange(N_EXP, dtype=I32)
    me = lax.axis_index("exp")
    steps_y = lax.rem(ids // EXP_Z - me // EXP_Z + EXP_Y, EXP_Y)
    steps_z = lax.rem(lax.rem(ids, EXP_Z) - lax.rem(me, EXP_Z) + EXP_Z, EXP_Z)
    start_of = (plane_step(steps_z) * EXP_Y + steps_y) * ROWS
    held = old_table[:, None] == ids[None, :]
    first = jnp.sum(jnp.where(held, start_of[:, None], 0), axis=0)
    serving = new_table[:, None] == ids[None, :]
    second = jnp.sum(jnp.where(serving, first[None, :], 0), axis=1)
    repeated = (new_table[:, None] == new_table[None, :]) & (ids[None, :] < ids[:, None])
    second = second + FIRST_ROWS + CAP * jnp.sum(repeated.astype(I32), axis=1)
    bases = jnp.stack([first, second]).astype(F32)
    bases = jnp.pad(bases, ((0, 6), (0, LANES - N_EXP)))
    table = jnp.pad(serving.astype(BF16), ((0, LANES - N_EXP), (0, LANES - N_EXP)))
    return bases, table


def local(
    tokens,
    queries,
    key_rows,
    value_rows,
    segments,
    bias_table,
    out_proj,
    router,
    gate_weight,
    up_weight,
    down_weight,
    old_table,
    new_table,
    routes_one,
    routes_two,
):
    bases, serving = slot_tables(old_table, new_table)
    ctx = attention(bias_table, queries, key_rows, value_rows, segments)
    return experts(
        ctx,
        tokens,
        out_proj,
        router,
        routes_one,
        routes_two,
        bases,
        serving,
        gate_weight,
        up_weight,
        down_weight,
    )


def solution(mesh):
    placed = (
        P(None, "exp", "seq", None),
        P(None, "exp", "seq", None),
        P(None, "exp", "seq", None),
        P(None, "exp", "seq", None),
        P(None, "exp", "seq"),
        P(),
        P(),
        P(),
        P("exp", None, None),
        P("exp", None, None),
        P("exp", None, None),
        P(),
        P(),
        P("exp", "seq", None),
        P("exp", "seq", None),
    )
    return jax.shard_map(
        local, mesh=mesh, in_specs=placed, out_specs=P(None, "exp", "seq", None), check_vma=False
    )
```

```python
import jax
import jax.numpy as jnp
from jax import lax
from jax.experimental import pallas as pl
from jax.experimental.pallas import tpu as pltpu
from jax.sharding import PartitionSpec as P

MESH = pl.DeviceIdType.MESH
BF16 = jnp.bfloat16
F32 = jnp.float32
I32 = jnp.int32

N_SEQ = 16
N_EXP = 16
EXP_Y = 4
EXP_Z = 4
TOK = 128
D = 1024
FFW = 1408
NBUCK = 32
WIN = 4
PAIRS = 8
LANES = 128
HALF = 64
CAP = 20
STRIDE = (32, 48)
SENT = (24, 40)
SINK_BUCKET = 31
ORDER = (1, 0)

EPSILON = 1e-06
MASKED = -1e30


def iota(shape, dim):
    return lax.broadcasted_iota(I32, shape, dim)


def dot(a, b):
    return jnp.dot(a, b, preferred_element_type=F32)


def dot_t(a, b):
    return lax.dot_general(a, b, (((1,), (1,)), ((), ())), preferred_element_type=F32)


def turned(row):
    return jnp.transpose(jnp.broadcast_to(row, (LANES, LANES)))


def remote(src, dst, send, recv, **device):
    return pltpu.make_async_remote_copy(
        src_ref=src,
        dst_ref=dst,
        send_sem=send,
        recv_sem=recv,
        device_id=device,
        device_id_type=MESH,
    )


def bias_of_distance(distance, values):
    result = jnp.broadcast_to(values[0], distance.shape)
    for bucket in range(1, 10):
        result = jnp.where(distance >= (1 << (bucket - 1)), values[bucket], result)
    return result


def plane_step(group):
    return group + (group // 2) * (1 - 2 * lax.rem(group, 2))


def layer_kernel(
    bias_hbm,
    seg_hbm,
    q_hbm,
    k_hbm,
    v_hbm,
    tok_hbm,
    proj_hbm,
    router_hbm,
    one_hbm,
    two_hbm,
    old_hbm,
    new_hbm,
    gate_hbm,
    up_hbm,
    down_hbm,
    out_ref,
    table,
    routes,
    held,
    tabs,
    router,
    tok,
    proj,
    gate_w,
    up_w,
    down_w,
    segs,
    qb,
    kb,
    vb,
    segcol,
    bias,
    sink_out,
    sink_in,
    sink_rows,
    ctx_out,
    ctx_in,
    hidden,
    normed,
    sbuf_one,
    sbuf_two,
    rbuf_one,
    rbuf_two,
    ybuf_one,
    ybuf_two,
    back_one,
    back_two,
    active,
    load_sem,
    qkv_send,
    qkv_recv,
    qkv_own,
    seg_send,
    seg_recv,
    seg_own,
    hop_send,
    hop_recv,
    sink_send,
    sink_recv,
    ctx_send,
    ctx_recv,
    ctx_own,
    go_send,
    go_recv,
    back_send,
    back_recv,
):
    me = lax.axis_index("seq")
    my_exp = lax.axis_index("exp")
    upper, pair = me // PAIRS, lax.rem(me, PAIRS)
    me_y, me_z = my_exp // EXP_Z, lax.rem(my_exp, EXP_Z)
    first_of_half = upper * PAIRS
    across = lax.rem(me + PAIRS, N_SEQ)
    sbuf, rbuf = (sbuf_one, sbuf_two), (rbuf_one, rbuf_two)
    ybuf, back = (ybuf_one, ybuf_two), (back_one, back_two)

    early = [
        pltpu.make_async_copy(src, dst, load_sem.at[i])
        for i, (src, dst) in enumerate(
            (
                (old_hbm, held.at[0]),
                (new_hbm, held.at[1]),
                (one_hbm.at[0], routes.at[0]),
                (two_hbm.at[0], routes.at[1]),
                (bias_hbm, table),
            )
        )
    ]
    late = [
        pltpu.make_async_copy(src, dst, load_sem.at[i + 5])
        for i, (src, dst) in enumerate(
            (
                (router_hbm, router),
                (tok_hbm, tok),
                (proj_hbm, proj),
                (gate_hbm.at[0], gate_w),
                (up_hbm.at[0], up_w),
                (down_hbm.at[0], down_w),
            )
        )
    ]
    for copy in early:
        copy.start()

    for batch in range(2):
        low = STRIDE[batch] - 16
        back[batch][:, low:, :] = jnp.zeros((N_EXP, 16, D), BF16)

    @pl.when(upper == 0)
    def _():
        for batch in range(2):
            kb[batch, 0:WIN] = jnp.zeros((WIN, TOK, LANES), BF16)
            vb[batch, 0:WIN] = jnp.zeros((WIN, TOK, LANES), BF16)
            segs[batch, 0:PAIRS] = jnp.full((PAIRS, 1, TOK), -1, I32)
            sink_in[batch] = jnp.zeros((2, 8, LANES), F32)

    barrier = pltpu.get_barrier_semaphore()
    for step in range(1, PAIRS):
        pl.semaphore_signal(
            barrier,
            inc=1,
            device_id={"seq": first_of_half + lax.rem(pair + step, PAIRS)},
            device_id_type=MESH,
        )
    pl.semaphore_signal(barrier, inc=1, device_id={"seq": across}, device_id_type=MESH)
    for step in range(1, N_EXP):
        pl.semaphore_signal(
            barrier,
            inc=1,
            device_id={"exp": lax.rem(my_exp + step, N_EXP)},
            device_id_type=MESH,
        )
    pl.semaphore_wait(barrier, PAIRS + N_EXP - 1)

    def lanes_of(which):
        return pl.ds(pl.multiple_of(which * LANES, LANES), LANES)

    def qkv_parts(batch, target):
        lanes = lanes_of(target)
        return (
            (k_hbm.at[batch, 0, :, lanes], kb.at[batch, pair + WIN]),
            (v_hbm.at[batch, 0, :, lanes], vb.at[batch, pair + WIN]),
            (q_hbm.at[batch, 0, :, lanes], qb.at[batch, pair]),
        )

    def qkv_copies(batch):
        copies = []
        for step in range(1, PAIRS):
            target = lax.rem(pair + step, PAIRS)
            for kind, (src, dst) in enumerate(qkv_parts(batch, target)):
                copies.append(
                    remote(
                        src,
                        dst,
                        qkv_send.at[batch, kind, step],
                        qkv_recv.at[batch, kind, step],
                        seq=first_of_half + target,
                    )
                )
        for kind, (src, dst) in enumerate(qkv_parts(batch, pair)):
            copies.append(pltpu.make_async_copy(src, dst, qkv_own.at[batch, kind]))
        return copies

    qkv = [qkv_copies(batch) for batch in range(2)]
    seg_copies = [
        remote(
            seg_hbm,
            segs.at[:, PAIRS + pair],
            seg_send.at[step],
            seg_recv.at[step],
            seq=first_of_half + lax.rem(pair + step, PAIRS),
        )
        for step in range(1, PAIRS)
    ]
    seg_copies.append(pltpu.make_async_copy(seg_hbm, segs.at[:, PAIRS + pair], seg_own))
    seg_hop = remote(
        segs.at[:, PAIRS : 2 * PAIRS],
        segs.at[:, 0:PAIRS],
        hop_send.at[4],
        hop_recv.at[4],
        seq=across,
    )

    def halo_hop(batch, kind):
        block = (kb, vb)[kind]
        return remote(
            block.at[batch, PAIRS : PAIRS + WIN],
            block.at[batch, 0:WIN],
            hop_send.at[2 * batch + kind],
            hop_recv.at[2 * batch + kind],
            seq=across,
        )

    def sink_hop(batch):
        return remote(
            sink_out.at[batch],
            sink_in.at[batch],
            sink_send.at[batch],
            sink_recv.at[batch],
            seq=across,
        )

    for copy in seg_copies:
        copy.start()
    for copy in qkv[ORDER[0]]:
        copy.start()
    for copy in late:
        copy.start()
    for copy in early:
        copy.wait()

    qi = iota((TOK, TOK), 0)
    kj = iota((TOK, TOK), 1)
    for head in range(2):
        head_row = table[pl.ds(2 * pair + head, 1), :]
        values = [head_row[:, bucket : bucket + 1] for bucket in range(10)]
        rows = slice(head * TOK, (head + 1) * TOK)
        merged = jnp.where(kj <= qi, qi - kj, qi - kj + WIN * TOK)
        bias[0, rows, :] = bias_of_distance(merged, values)
        for block in range(1, WIN):
            bias[block, rows, :] = bias_of_distance(qi - kj + (WIN - block) * TOK, values)
    sink_bias = jnp.where(
        iota((2 * TOK, 1), 0) < TOK,
        table[pl.ds(2 * pair, 1), :][:, SINK_BUCKET : SINK_BUCKET + 1],
        table[pl.ds(2 * pair + 1, 1), :][:, SINK_BUCKET : SINK_BUCKET + 1],
    )

    lane = iota((LANES, LANES), 1)
    row = iota((LANES, LANES), 0)
    tabs[...] = jnp.full((2, LANES), -1, I32)
    tabs[0:1, 0:N_EXP] = held[0]
    tabs[1:2, 0:N_EXP] = held[1]
    steps_y = lax.rem(row // EXP_Z - me_y + 2 * EXP_Y * EXP_Y, EXP_Y)
    steps_z = lax.rem(lax.rem(row, EXP_Z) - me_z + EXP_Z, EXP_Z)
    groups = steps_z + (steps_z // 2) * (1 - 2 * lax.rem(steps_z, 2))
    slot_of_row = (groups * EXP_Y + steps_y).astype(F32)
    holds = turned(tabs[0:1, :]) == lane
    slot_of_expert = jnp.sum(jnp.where(holds, slot_of_row, 0.0), axis=0, keepdims=True)
    new_row = tabs[1:2, :]
    new_col = turned(new_row)
    served = new_col == lane
    serving = jnp.where(served, 1.0, 0.0).astype(BF16)
    slot_two = jnp.sum(jnp.where(served, slot_of_expert, 0.0), axis=1, keepdims=True)
    again = jnp.where((new_col == new_row) & (lane < row), 1.0, 0.0)
    again = jnp.sum(again, axis=1, keepdims=True)
    base_two = jnp.transpose(
        jnp.broadcast_to(slot_two * STRIDE[1] + again * CAP, (LANES, LANES))
    )[0:1, :]
    bases = (slot_of_expert * STRIDE[0], base_two)
    lower = jnp.where(row > lane, 1.0, 0.0).astype(BF16)
    place_cols, place_rows, differences = [], [], []
    for batch in range(2):
        member = [
            jnp.where(turned(routes[batch, c : c + 1, :]) == lane, 1.0, 0.0) for c in range(2)
        ]
        counts = [dot(lower, m.astype(BF16)) for m in member]
        counts[1] = counts[1] + jnp.sum(member[0], axis=0, keepdims=True)
        cols = [
            jnp.sum(m * (c + bases[batch]), axis=1, keepdims=True)
            for m, c in zip(member, counts)
        ]
        place_cols.append(cols)
        place_rows.append(
            [jnp.transpose(jnp.broadcast_to(col, (TOK, TOK)))[0:1, :] for col in cols]
        )
        difference = member[0] - member[1]
        if batch == 1:
            difference = dot(difference.astype(BF16), serving)
        differences.append(difference)

    lane_head = iota((2 * TOK, LANES), 1) // HALF
    row_head = iota((2 * TOK, LANES), 0) // TOK
    own_half = lane_head == row_head
    causal = lax.rem(iota((2 * TOK, TOK), 0), TOK) >= iota((2 * TOK, TOK), 1)

    def twice(value):
        return jnp.concatenate([value, value], axis=0)

    def context_copy(batch, block):
        return remote(
            ctx_out.at[batch, block],
            ctx_in.at[batch, :, lanes_of(pair)],
            ctx_send.at[batch, block],
            ctx_recv.at[batch, pair],
            seq=first_of_half + block,
        )

    def context_own(batch):
        return pltpu.make_async_copy(
            ctx_out.at[batch, pair], ctx_in.at[batch, :, lanes_of(pair)], ctx_own.at[batch]
        )

    def attention(batch, opening):
        if opening:
            for copy in seg_copies:
                copy.wait()

            @pl.when(upper == 0)
            def _():
                seg_hop.start()

        for copy in qkv[batch]:
            copy.wait()

        @pl.when(upper == 0)
        def _():
            for kind in range(2):
                halo_hop(batch, kind).start()

        if opening:
            for copy in qkv[ORDER[1]]:
                copy.start()

            @pl.when(upper == 1)
            def _():
                seg_hop.wait_recv()

        def columns(block, before):
            line = segs[batch, block]
            segcol[block] = turned(line)
            document = iota((8, TOK), 0)
            return before + jnp.where((line < document) & (line >= 0), 1, 0)

        ahead = lax.fori_loop(0, 2 * PAIRS, columns, jnp.zeros((8, TOK), I32))
        starts = jnp.sum(ahead, axis=1, keepdims=True)

        def sinks(block, sums):
            k_sum, v_sum = sums
            spot = (upper * PAIRS + block) * TOK + iota((8, TOK), 1)
            pick = jnp.where(spot == starts, 1.0, 0.0).astype(BF16)
            return (
                k_sum + dot(pick, kb[batch, block + WIN]),
                v_sum + dot(pick, vb[batch, block + WIN]),
            )

        zero = jnp.zeros((8, LANES), F32)
        k_sink, v_sink = lax.fori_loop(0, PAIRS, sinks, (zero, zero))
        sink_out[batch, 0] = k_sink
        sink_out[batch, 1] = v_sink

        @pl.when(upper == 0)
        def _():
            sink_hop(batch).start()

        @pl.when(upper == 1)
        def _():
            sink_hop(batch).wait_recv()

        sink_rows[0] = k_sink + sink_in[batch, 0]
        sink_rows[1] = v_sink + sink_in[batch, 1]

        def attend(block):
            query = twice(qb[batch, block].astype(F32) * 0.125)
            query = jnp.where(own_half, query, 0.0)
            query_rows = query.astype(BF16)
            mine = segcol[block + PAIRS]
            pieces = []
            for near in range(WIN + 1):
                raw = dot_t(query_rows, kb[batch, block + near])
                same = twice(mine == segs[batch, block + near + WIN])
                pieces.append((raw, same))
            merged = jnp.where(causal, pieces[WIN][0], pieces[0][0])
            merged_same = jnp.where(
                causal, pieces[WIN][1].astype(I32), pieces[0][1].astype(I32)
            )
            scores = [jnp.where(merged_same > 0, merged + bias[0], MASKED)]
            for near in range(1, WIN):
                raw, same = pieces[near]
                scores.append(jnp.where(same, raw + bias[near], MASKED))
            chosen_doc = iota((8, LANES), 0) == segs[batch, block + PAIRS][:, 0:1]
            k_row = jnp.sum(jnp.where(chosen_doc, sink_rows[0], 0.0), axis=0, keepdims=True)
            v_row = jnp.sum(jnp.where(chosen_doc, sink_rows[1], 0.0), axis=0, keepdims=True)
            sink_seen = twice(mine[:, 0:1] == segcol[block + WIN][:, 0:1])
            sink = jnp.sum(query * k_row, axis=1, keepdims=True) + sink_bias
            sink = jnp.where(sink_seen, sink, MASKED)
            peak = jnp.maximum(
                jnp.maximum(scores[0], scores[1]), jnp.maximum(scores[2], scores[3])
            )
            peak = jnp.maximum(jnp.max(peak, axis=1, keepdims=True), sink)
            weights = [jnp.exp(score - peak) for score in scores]
            sink_weight = jnp.exp(sink - peak)
            total = (weights[0] + weights[1]) + (weights[2] + weights[3])
            total = jnp.sum(total, axis=1, keepdims=True) + sink_weight
            mixed = sink_weight * v_row
            mixed = mixed + dot(jnp.where(causal, 0.0, weights[0]).astype(BF16), vb[batch, block])
            mixed = mixed + dot(
                jnp.where(causal, weights[0], 0.0).astype(BF16), vb[batch, block + WIN]
            )
            for near in range(1, WIN):
                mixed = mixed + dot(weights[near].astype(BF16), vb[batch, block + near])
            mixed = mixed / total
            ctx_out[batch, block] = jnp.where(
                lane_head[:TOK] == 0, mixed[:TOK], mixed[TOK:]
            ).astype(BF16)

            @pl.when(block == pair)
            def _():
                context_own(batch).start()

            @pl.when(block != pair)
            def _():
                context_copy(batch, block).start()

        def attend_late(turn, carry):
            attend(WIN + lax.rem(pair + turn, WIN))
            return carry

        def attend_early(turn, carry):
            attend(lax.rem(pair + turn, WIN))
            return carry

        lax.fori_loop(0, WIN, attend_late, 0)

        @pl.when(upper == 1)
        def _():
            for kind in range(2):
                halo_hop(batch, kind).wait_recv()

        lax.fori_loop(0, WIN, attend_early, 0)

    def target_of(group, dy, sign):
        y = lax.rem(me_y + EXP_Y + sign * dy, EXP_Y)
        z = lax.rem(me_z + EXP_Z + sign * plane_step(group), EXP_Z)
        return y * EXP_Z + z

    def dispatch(batch, group, dy):
        slot = group * EXP_Y + dy
        rows = slice(0, SENT[batch])
        return remote(
            sbuf[batch].at[slot, rows],
            rbuf[batch].at[slot, rows],
            go_send.at[batch, slot],
            go_recv.at[batch, slot],
            exp=target_of(group, dy, 1),
        )

    def answer(batch, group, dy):
        slot = group * EXP_Y + dy
        rows = slice(0, SENT[batch])
        return remote(
            ybuf[batch].at[slot, rows],
            back[batch].at[slot, rows],
            back_send.at[batch, slot],
            back_recv.at[batch, slot],
            exp=target_of(group, dy, -1),
        )

    gates = [None, None]

    def front(batch, opening):
        for step in range(1, PAIRS):
            source = lax.rem(pair + step, PAIRS)
            remote(
                ctx_out.at[batch, source],
                ctx_in.at[batch, :, lanes_of(source)],
                ctx_send.at[batch, source],
                ctx_recv.at[batch, source],
                seq=first_of_half + source,
            ).wait_recv()
        context_own(batch).wait()
        if opening:
            for copy in late[:3]:
                copy.wait()
        context = ctx_in[batch]
        for part in range(2):
            cols = slice(part * 512, (part + 1) * 512)
            hidden[batch, :, cols] = tok[batch, 0, :, cols].astype(F32) + dot(
                context, proj[:, cols]
            )
        value = hidden[batch]
        scale = lax.rsqrt(jnp.mean(value * value, axis=1, keepdims=True) + EPSILON)
        normed[...] = (value * scale).astype(BF16)
        stride = STRIDE[batch]
        for group in (3, 1, 2, 0):
            spot = (iota((EXP_Y * stride, TOK), 0) + group * EXP_Y * stride).astype(F32)
            hit = (spot == place_rows[batch][0]) | (spot == place_rows[batch][1])
            plan = jnp.where(hit, 1.0, 0.0).astype(BF16)
            for part in range(2):
                cols = slice(part * 512, (part + 1) * 512)
                sbuf[batch][group * EXP_Y : (group + 1) * EXP_Y, :, cols] = (
                    dot(plan, normed[:, cols]).astype(BF16).reshape(EXP_Y, stride, 512)
                )
            for dy in range(EXP_Y):
                if group + dy > 0:
                    dispatch(batch, group, dy).start()
        rbuf[batch][0] = sbuf[batch][0]
        logits = dot_t(normed[...], router[...])
        picked = jnp.sum(differences[batch][:, :N_EXP] * logits, axis=1, keepdims=True)
        first = jax.nn.sigmoid(picked)
        gates[batch] = (first, 1.0 - first)

    def serve_all(batch):
        stride = STRIDE[batch]
        count = EXP_Y * stride

        def serve(group, carry):
            for dy in range(EXP_Y):
                if dy == 0:

                    @pl.when(group > 0)
                    def _():
                        dispatch(batch, group, dy).wait_recv()

                else:
                    dispatch(batch, group, dy).wait_recv()
            inputs = rbuf[batch][pl.ds(group * EXP_Y, EXP_Y)].reshape(count, D)
            for low, high in ((0, 512), (512, 1024), (1024, FFW)):
                gate = dot(inputs, gate_w[:, low:high])
                up = dot(inputs, up_w[:, low:high])
                inner = 0.7978845608028654 * (gate + 0.044715 * (gate * gate * gate))
                active[0:count, low:high] = (0.5 * gate * (1.0 + jnp.tanh(inner)) * up).astype(
                    BF16
                )
            for part in range(2):
                cols = slice(part * 512, (part + 1) * 512)
                ybuf[batch][pl.ds(group * EXP_Y, EXP_Y), :, cols] = (
                    dot(active[0:count], down_w[:, cols])
                    .astype(BF16)
                    .reshape(EXP_Y, stride, 512)
                )
            for dy in range(EXP_Y):
                if dy == 0:

                    @pl.when(group > 0)
                    def _():
                        answer(batch, group, dy).start()

                else:
                    answer(batch, group, dy).start()
            return carry

        lax.fori_loop(0, EXP_Z, serve, 0)
        back[batch][0] = ybuf[batch][0]

    def combine(batch):
        stride = STRIDE[batch]
        result = hidden[batch]
        for group in range(EXP_Z):
            for dy in range(EXP_Y):
                if group + dy > 0:
                    answer(batch, group, dy).wait_recv()
            spot = (iota((TOK, EXP_Y * stride), 1) + group * EXP_Y * stride).astype(F32)
            mix = jnp.where(spot == place_cols[batch][0], gates[batch][0], 0.0) + jnp.where(
                spot == place_cols[batch][1], gates[batch][1], 0.0
            )
            coarse = mix.astype(BF16)
            fine = (mix - coarse.astype(F32)).astype(BF16)
            rows = back[batch][group * EXP_Y : (group + 1) * EXP_Y].reshape(EXP_Y * stride, D)
            both = dot(jnp.concatenate([coarse, fine], axis=0), rows)
            result = result + both[:TOK] + both[TOK:]
        out_ref[batch, 0] = result.astype(BF16)

    for turn, batch in enumerate(ORDER):
        attention(batch, turn == 0)
        front(batch, turn == 0)
    for copy in late[3:]:
        copy.wait()
    for batch in ORDER:
        serve_all(batch)
    for batch in ORDER:
        combine(batch)

    for batch in range(2):
        for group in range(EXP_Z):
            for dy in range(EXP_Y):
                if group + dy > 0:
                    dispatch(batch, group, dy).wait_send()
                    answer(batch, group, dy).wait_send()
        for step in range(1, PAIRS):
            context_copy(batch, lax.rem(pair + step, PAIRS)).wait_send()

    @pl.when(upper == 0)
    def _():
        seg_hop.wait_send()
        for batch in range(2):
            sink_hop(batch).wait_send()
            for kind in range(2):
                halo_hop(batch, kind).wait_send()


def local(
    tokens,
    queries,
    key_rows,
    value_rows,
    segments,
    bias_table,
    out_proj,
    router,
    gate_weight,
    up_weight,
    down_weight,
    old_table,
    new_table,
    routes_one,
    routes_two,
):
    any_spec = pl.BlockSpec(memory_space=pl.ANY)
    vmem = pltpu.VMEM
    dma = pltpu.SemaphoreType.DMA
    buffers = [vmem((N_EXP, stride, D), BF16) for stride in STRIDE]
    return pl.pallas_call(
        layer_kernel,
        out_shape=jax.ShapeDtypeStruct((2, 1, TOK, D), BF16),
        in_specs=[any_spec] * 15,
        out_specs=pl.BlockSpec(memory_space=pltpu.VMEM),
        scratch_shapes=[
            vmem((N_EXP, NBUCK), F32),
            vmem((2, 2, TOK), I32),
            vmem((2, 1, N_EXP), I32),
            vmem((2, LANES), I32),
            vmem((N_EXP, D), BF16),
            vmem((2, 1, TOK, D), BF16),
            vmem((D, D), BF16),
            vmem((D, FFW), BF16),
            vmem((D, FFW), BF16),
            vmem((FFW, D), BF16),
            vmem((2, N_SEQ, 1, TOK), I32),
            vmem((2, PAIRS, TOK, LANES), BF16),
            vmem((2, PAIRS + WIN, TOK, LANES), BF16),
            vmem((2, PAIRS + WIN, TOK, LANES), BF16),
            vmem((N_SEQ, TOK, TOK), I32),
            vmem((WIN, 2 * TOK, TOK), F32),
            vmem((2, 2, 8, LANES), F32),
            vmem((2, 2, 8, LANES), F32),
            vmem((2, 8, LANES), F32),
            vmem((2, PAIRS, TOK, LANES), BF16),
            vmem((2, TOK, D), BF16),
            vmem((2, TOK, D), F32),
            vmem((TOK, D), BF16),
            *buffers,
            *buffers,
            *buffers,
            *buffers,
            vmem((EXP_Y * STRIDE[1], FFW), BF16),
            dma((11,)),
            dma((2, 3, PAIRS)),
            dma((2, 3, PAIRS)),
            dma((2, 3)),
            dma((PAIRS,)),
            dma((PAIRS,)),
            dma(()),
            dma((5,)),
            dma((5,)),
            dma((2,)),
            dma((2,)),
            dma((2, PAIRS)),
            dma((2, PAIRS)),
            dma((2,)),
            dma((2, N_EXP)),
            dma((2, N_EXP)),
            dma((2, N_EXP)),
            dma((2, N_EXP)),
        ],
        compiler_params=pltpu.CompilerParams(
            collective_id=0, has_side_effects=True, vmem_limit_bytes=56 << 20
        ),
        name="layer",
    )(
        bias_table,
        segments,
        queries,
        key_rows,
        value_rows,
        tokens,
        out_proj,
        router.T,
        jnp.swapaxes(routes_one, 1, 2),
        jnp.swapaxes(routes_two, 1, 2),
        old_table[None],
        new_table[None],
        gate_weight,
        up_weight,
        down_weight,
    )


def solution(mesh):
    placed = (
        P(None, "exp", "seq", None),
        P(None, "exp", "seq", None),
        P(None, "exp", "seq", None),
        P(None, "exp", "seq", None),
        P(None, "exp", "seq"),
        P(),
        P(),
        P(),
        P("exp", None, None),
        P("exp", None, None),
        P("exp", None, None),
        P(),
        P(),
        P("exp", "seq", None),
        P("exp", "seq", None),
    )
    return jax.shard_map(
        local, mesh=mesh, in_specs=placed, out_specs=P(None, "exp", "seq", None), check_vma=False
    )
```

```python
import jax
import jax.numpy as jnp
from jax import lax
from jax.experimental import pallas as pl
from jax.experimental.pallas import tpu as pltpu
from jax.sharding import PartitionSpec as P

MESH = pl.DeviceIdType.MESH
BF16 = jnp.bfloat16
F32 = jnp.float32
I32 = jnp.int32

N_SEQ = 16
N_EXP = 16
EXP_Y = 4
EXP_Z = 4
TOK = 128
D = 1024
FFW = 1408
NBUCK = 32
WIN = 4
PAIRS = 8
LANES = 128
HALF = 64
CAP = 20
STRIDE = (32, 48)
SENT = (24, 40)
SINK_BUCKET = 31
ORDER = (1, 0)

EPSILON = 1e-06
MASKED = -1e30


def iota(shape, dim):
    return lax.broadcasted_iota(I32, shape, dim)


def dot(a, b):
    return jnp.dot(a, b, preferred_element_type=F32)


def dot_t(a, b):
    return lax.dot_general(a, b, (((1,), (1,)), ((), ())), preferred_element_type=F32)


def turned(row):
    return jnp.transpose(jnp.broadcast_to(row, (LANES, LANES)))


def remote(src, dst, send, recv, **device):
    return pltpu.make_async_remote_copy(
        src_ref=src,
        dst_ref=dst,
        send_sem=send,
        recv_sem=recv,
        device_id=device,
        device_id_type=MESH,
    )


def bias_of_distance(distance, values):
    result = jnp.broadcast_to(values[0], distance.shape)
    for bucket in range(1, 10):
        result = jnp.where(distance >= (1 << (bucket - 1)), values[bucket], result)
    return result


def plane_step(group):
    return group + (group // 2) * (1 - 2 * lax.rem(group, 2))


def layer_kernel(
    bias_hbm,
    seg_hbm,
    q_hbm,
    k_hbm,
    v_hbm,
    tok_hbm,
    proj_hbm,
    router_hbm,
    one_hbm,
    two_hbm,
    old_hbm,
    new_hbm,
    gate_hbm,
    up_hbm,
    down_hbm,
    out_ref,
    table,
    routes,
    held,
    tabs,
    router,
    tok,
    proj,
    gate_w,
    up_w,
    down_w,
    segs,
    qb,
    kb,
    vb,
    segcol,
    bias,
    sink_out,
    sink_in,
    sink_rows,
    ctx_out,
    ctx_in,
    hidden,
    normed,
    sbuf_one,
    sbuf_two,
    rbuf_one,
    rbuf_two,
    ybuf_one,
    ybuf_two,
    back_one,
    back_two,
    active,
    load_sem,
    qkv_send,
    qkv_recv,
    qkv_own,
    seg_send,
    seg_recv,
    seg_own,
    hop_send,
    hop_recv,
    sink_send,
    sink_recv,
    ctx_send,
    ctx_recv,
    ctx_own,
    go_send,
    go_recv,
    back_send,
    back_recv,
    tok_in,
    place_in,
    place_out,
    tok_send,
    tok_recv,
    place_send,
    place_recv,
):
    me = lax.axis_index("seq")
    my_exp = lax.axis_index("exp")
    upper, pair = me // PAIRS, lax.rem(me, PAIRS)
    me_y, me_z = my_exp // EXP_Z, lax.rem(my_exp, EXP_Z)
    first_of_half = upper * PAIRS
    across = lax.rem(me + PAIRS, N_SEQ)
    sbuf, rbuf = (sbuf_one, sbuf_two), (rbuf_one, rbuf_two)
    ybuf, back = (ybuf_one, ybuf_two), (back_one, back_two)

    early = [
        pltpu.make_async_copy(src, dst, load_sem.at[i])
        for i, (src, dst) in enumerate(
            (
                (old_hbm, held.at[0]),
                (new_hbm, held.at[1]),
                (one_hbm.at[0], routes.at[0]),
                (two_hbm.at[0], routes.at[1]),
                (bias_hbm, table),
            )
        )
    ]
    late = [
        pltpu.make_async_copy(src, dst, load_sem.at[i + 5])
        for i, (src, dst) in enumerate(
            (
                (router_hbm, router),
                (tok_hbm, tok),
                (proj_hbm, proj),
                (gate_hbm.at[0], gate_w),
                (up_hbm.at[0], up_w),
                (down_hbm.at[0], down_w),
            )
        )
    ]
    for copy in early:
        copy.start()

    for batch in range(2):
        low = STRIDE[batch] - 16
        back[batch][:, low:, :] = jnp.zeros((N_EXP, 16, D), BF16)

    @pl.when(upper == 0)
    def _():
        for batch in range(2):
            kb[batch, 0:WIN] = jnp.zeros((WIN, TOK, LANES), BF16)
            vb[batch, 0:WIN] = jnp.zeros((WIN, TOK, LANES), BF16)
            segs[batch, 0:PAIRS] = jnp.full((PAIRS, 1, TOK), -1, I32)
            sink_in[batch] = jnp.zeros((2, 8, LANES), F32)

    barrier = pltpu.get_barrier_semaphore()
    for step in range(1, PAIRS):
        pl.semaphore_signal(
            barrier,
            inc=1,
            device_id={"seq": first_of_half + lax.rem(pair + step, PAIRS)},
            device_id_type=MESH,
        )
    pl.semaphore_signal(barrier, inc=1, device_id={"seq": across}, device_id_type=MESH)
    for step in range(1, N_EXP):
        pl.semaphore_signal(
            barrier,
            inc=1,
            device_id={"exp": lax.rem(my_exp + step, N_EXP)},
            device_id_type=MESH,
        )
    pl.semaphore_wait(barrier, PAIRS + N_EXP - 1)

    def lanes_of(which):
        return pl.ds(pl.multiple_of(which * LANES, LANES), LANES)

    def qkv_parts(batch, target):
        lanes = lanes_of(target)
        return (
            (k_hbm.at[batch, 0, :, lanes], kb.at[batch, pair + WIN]),
            (v_hbm.at[batch, 0, :, lanes], vb.at[batch, pair + WIN]),
            (q_hbm.at[batch, 0, :, lanes], qb.at[batch, pair]),
        )

    def qkv_copies(batch):
        copies = []
        for step in range(1, PAIRS):
            target = lax.rem(pair + step, PAIRS)
            for kind, (src, dst) in enumerate(qkv_parts(batch, target)):
                copies.append(
                    remote(
                        src,
                        dst,
                        qkv_send.at[batch, kind, step],
                        qkv_recv.at[batch, kind, step],
                        seq=first_of_half + target,
                    )
                )
        for kind, (src, dst) in enumerate(qkv_parts(batch, pair)):
            copies.append(pltpu.make_async_copy(src, dst, qkv_own.at[batch, kind]))
        return copies

    qkv = [qkv_copies(batch) for batch in range(2)]
    seg_copies = [
        remote(
            seg_hbm,
            segs.at[:, PAIRS + pair],
            seg_send.at[step],
            seg_recv.at[step],
            seq=first_of_half + lax.rem(pair + step, PAIRS),
        )
        for step in range(1, PAIRS)
    ]
    seg_copies.append(pltpu.make_async_copy(seg_hbm, segs.at[:, PAIRS + pair], seg_own))
    seg_hop = remote(
        segs.at[:, PAIRS : 2 * PAIRS],
        segs.at[:, 0:PAIRS],
        hop_send.at[4],
        hop_recv.at[4],
        seq=across,
    )

    def halo_hop(batch, kind):
        block = (kb, vb)[kind]
        return remote(
            block.at[batch, PAIRS : PAIRS + WIN],
            block.at[batch, 0:WIN],
            hop_send.at[2 * batch + kind],
            hop_recv.at[2 * batch + kind],
            seq=across,
        )

    def sink_hop(batch):
        return remote(
            sink_out.at[batch],
            sink_in.at[batch],
            sink_send.at[batch],
            sink_recv.at[batch],
            seq=across,
        )

    for copy in seg_copies:
        copy.start()
    for copy in qkv[ORDER[0]]:
        copy.start()
    for copy in late:
        copy.start()
    for copy in early:
        copy.wait()

    qi = iota((TOK, TOK), 0)
    kj = iota((TOK, TOK), 1)
    for head in range(2):
        head_row = table[pl.ds(2 * pair + head, 1), :]
        values = [head_row[:, bucket : bucket + 1] for bucket in range(10)]
        rows = slice(head * TOK, (head + 1) * TOK)
        merged = jnp.where(kj <= qi, qi - kj, qi - kj + WIN * TOK)
        bias[0, rows, :] = bias_of_distance(merged, values)
        for block in range(1, WIN):
            bias[block, rows, :] = bias_of_distance(qi - kj + (WIN - block) * TOK, values)
    sink_bias = jnp.where(
        iota((2 * TOK, 1), 0) < TOK,
        table[pl.ds(2 * pair, 1), :][:, SINK_BUCKET : SINK_BUCKET + 1],
        table[pl.ds(2 * pair + 1, 1), :][:, SINK_BUCKET : SINK_BUCKET + 1],
    )

    lane = iota((LANES, LANES), 1)
    row = iota((LANES, LANES), 0)
    tabs[...] = jnp.full((2, LANES), -1, I32)
    tabs[0:1, 0:N_EXP] = held[0]
    tabs[1:2, 0:N_EXP] = held[1]
    steps_y = lax.rem(row // EXP_Z - me_y + 2 * EXP_Y * EXP_Y, EXP_Y)
    steps_z = lax.rem(lax.rem(row, EXP_Z) - me_z + EXP_Z, EXP_Z)
    groups = steps_z + (steps_z // 2) * (1 - 2 * lax.rem(steps_z, 2))
    slot_of_row = (groups * EXP_Y + steps_y).astype(F32)
    holds = turned(tabs[0:1, :]) == lane
    slot_of_expert = jnp.sum(jnp.where(holds, slot_of_row, 0.0), axis=0, keepdims=True)
    new_row = tabs[1:2, :]
    new_col = turned(new_row)
    served = new_col == lane
    serving = jnp.where(served, 1.0, 0.0).astype(BF16)
    slot_two = jnp.sum(jnp.where(served, slot_of_expert, 0.0), axis=1, keepdims=True)
    again = jnp.where((new_col == new_row) & (lane < row), 1.0, 0.0)
    again = jnp.sum(again, axis=1, keepdims=True)
    base_two = jnp.transpose(
        jnp.broadcast_to(slot_two * STRIDE[1] + again * CAP, (LANES, LANES))
    )[0:1, :]
    bases = (slot_of_expert * STRIDE[0], base_two)
    lower = jnp.where(row > lane, 1.0, 0.0).astype(BF16)
    place_cols, place_rows, differences = [], [], []
    for batch in range(2):
        member = [
            jnp.where(turned(routes[batch, c : c + 1, :]) == lane, 1.0, 0.0) for c in range(2)
        ]
        counts = [dot(lower, m.astype(BF16)) for m in member]
        counts[1] = counts[1] + jnp.sum(member[0], axis=0, keepdims=True)
        cols = [
            jnp.sum(m * (c + bases[batch]), axis=1, keepdims=True)
            for m, c in zip(member, counts)
        ]
        place_cols.append(cols)
        place_rows.append(
            [jnp.transpose(jnp.broadcast_to(col, (TOK, TOK)))[0:1, :] for col in cols]
        )
        difference = member[0] - member[1]
        if batch == 1:
            difference = dot(difference.astype(BF16), serving)
        differences.append(difference)
    for c in range(2):
        place_out[c : c + 1, :] = place_rows[1][c]
    place_in[0] = place_out[...]

    def plane(step):
        return me_y * EXP_Z + lax.rem(me_z + step, EXP_Z)

    place_copies = [
        remote(
            place_out,
            place_in.at[group],
            place_send.at[group],
            place_recv.at[group],
            exp=plane(step),
        )
        for group, step in ((1, 1), (2, 3), (3, 2))
    ]
    for copy in place_copies:
        copy.start()

    def token_copy(group, half):
        rows = slice(half * (TOK // 2), (half + 1) * (TOK // 2))
        origin = 1 + half if group == 3 else 0
        step = (1, 3)[half] if group == 3 else (1, 3)[group - 1]
        return remote(
            tok_in.at[origin, rows],
            tok_in.at[group, rows],
            tok_send.at[group, half],
            tok_recv.at[group, half],
            exp=plane(step),
        )

    def relay():
        for half in range(2):
            token_copy(1 + half, half).wait_recv()
            token_copy(3, half).start()

    lane_head = iota((2 * TOK, LANES), 1) // HALF
    row_head = iota((2 * TOK, LANES), 0) // TOK
    own_half = lane_head == row_head
    causal = lax.rem(iota((2 * TOK, TOK), 0), TOK) >= iota((2 * TOK, TOK), 1)

    def twice(value):
        return jnp.concatenate([value, value], axis=0)

    def context_copy(batch, block):
        return remote(
            ctx_out.at[batch, block],
            ctx_in.at[batch, :, lanes_of(pair)],
            ctx_send.at[batch, block],
            ctx_recv.at[batch, pair],
            seq=first_of_half + block,
        )

    def context_own(batch):
        return pltpu.make_async_copy(
            ctx_out.at[batch, pair], ctx_in.at[batch, :, lanes_of(pair)], ctx_own.at[batch]
        )

    def attention(batch, opening):
        if opening:
            for copy in seg_copies:
                copy.wait()

            @pl.when(upper == 0)
            def _():
                seg_hop.start()

        for copy in qkv[batch]:
            copy.wait()

        @pl.when(upper == 0)
        def _():
            for kind in range(2):
                halo_hop(batch, kind).start()

        if opening:
            for copy in qkv[ORDER[1]]:
                copy.start()

            @pl.when(upper == 1)
            def _():
                seg_hop.wait_recv()

        def columns(block, before):
            line = segs[batch, block]
            segcol[block] = turned(line)
            document = iota((8, TOK), 0)
            return before + jnp.where((line < document) & (line >= 0), 1, 0)

        ahead = lax.fori_loop(0, 2 * PAIRS, columns, jnp.zeros((8, TOK), I32))
        starts = jnp.sum(ahead, axis=1, keepdims=True)

        def sinks(block, sums):
            k_sum, v_sum = sums
            spot = (upper * PAIRS + block) * TOK + iota((8, TOK), 1)
            pick = jnp.where(spot == starts, 1.0, 0.0).astype(BF16)
            return (
                k_sum + dot(pick, kb[batch, block + WIN]),
                v_sum + dot(pick, vb[batch, block + WIN]),
            )

        zero = jnp.zeros((8, LANES), F32)
        k_sink, v_sink = lax.fori_loop(0, PAIRS, sinks, (zero, zero))
        sink_out[batch, 0] = k_sink
        sink_out[batch, 1] = v_sink

        @pl.when(upper == 0)
        def _():
            sink_hop(batch).start()

        @pl.when(upper == 1)
        def _():
            sink_hop(batch).wait_recv()

        sink_rows[0] = k_sink + sink_in[batch, 0]
        sink_rows[1] = v_sink + sink_in[batch, 1]

        def attend(block):
            query = twice(qb[batch, block].astype(F32) * 0.125)
            query = jnp.where(own_half, query, 0.0)
            query_rows = query.astype(BF16)
            mine = segcol[block + PAIRS]
            pieces = []
            for near in range(WIN + 1):
                raw = dot_t(query_rows, kb[batch, block + near])
                same = twice(mine == segs[batch, block + near + WIN])
                pieces.append((raw, same))
            merged = jnp.where(causal, pieces[WIN][0], pieces[0][0])
            merged_same = jnp.where(
                causal, pieces[WIN][1].astype(I32), pieces[0][1].astype(I32)
            )
            scores = [jnp.where(merged_same > 0, merged + bias[0], MASKED)]
            for near in range(1, WIN):
                raw, same = pieces[near]
                scores.append(jnp.where(same, raw + bias[near], MASKED))
            chosen_doc = iota((8, LANES), 0) == segs[batch, block + PAIRS][:, 0:1]
            k_row = jnp.sum(jnp.where(chosen_doc, sink_rows[0], 0.0), axis=0, keepdims=True)
            v_row = jnp.sum(jnp.where(chosen_doc, sink_rows[1], 0.0), axis=0, keepdims=True)
            sink_seen = twice(mine[:, 0:1] == segcol[block + WIN][:, 0:1])
            sink = jnp.sum(query * k_row, axis=1, keepdims=True) + sink_bias
            sink = jnp.where(sink_seen, sink, MASKED)
            peak = jnp.maximum(
                jnp.maximum(scores[0], scores[1]), jnp.maximum(scores[2], scores[3])
            )
            peak = jnp.maximum(jnp.max(peak, axis=1, keepdims=True), sink)
            weights = [jnp.exp(score - peak) for score in scores]
            sink_weight = jnp.exp(sink - peak)
            total = (weights[0] + weights[1]) + (weights[2] + weights[3])
            total = jnp.sum(total, axis=1, keepdims=True) + sink_weight
            mixed = sink_weight * v_row
            mixed = mixed + dot(jnp.where(causal, 0.0, weights[0]).astype(BF16), vb[batch, block])
            mixed = mixed + dot(
                jnp.where(causal, weights[0], 0.0).astype(BF16), vb[batch, block + WIN]
            )
            for near in range(1, WIN):
                mixed = mixed + dot(weights[near].astype(BF16), vb[batch, block + near])
            mixed = mixed / total
            ctx_out[batch, block] = jnp.where(
                lane_head[:TOK] == 0, mixed[:TOK], mixed[TOK:]
            ).astype(BF16)

            @pl.when(block == pair)
            def _():
                context_own(batch).start()

            @pl.when(block != pair)
            def _():
                context_copy(batch, block).start()

        def attend_late(turn, carry):
            attend(WIN + lax.rem(pair + turn, WIN))
            return carry

        def attend_early(turn, carry):
            attend(lax.rem(pair + turn, WIN))
            return carry

        lax.fori_loop(0, WIN, attend_late, 0)
        if not opening:
            relay()

        @pl.when(upper == 1)
        def _():
            for kind in range(2):
                halo_hop(batch, kind).wait_recv()

        lax.fori_loop(0, WIN, attend_early, 0)

    def target_of(group, dy, sign):
        y = lax.rem(me_y + EXP_Y + sign * dy, EXP_Y)
        z = lax.rem(me_z + EXP_Z + sign * plane_step(group), EXP_Z)
        return y * EXP_Z + z

    def beside(dy):
        return lax.rem(me_y + dy, EXP_Y) * EXP_Z + me_z

    def dispatch(batch, group, dy):
        slot = group * EXP_Y + dy
        rows = slice(0, SENT[batch])
        return remote(
            sbuf[batch].at[slot, rows],
            rbuf[batch].at[slot, rows],
            go_send.at[batch, slot],
            go_recv.at[batch, slot],
            exp=beside(dy) if batch == 1 else target_of(group, dy, 1),
        )

    def answer(batch, group, dy):
        slot = group * EXP_Y + dy
        rows = slice(0, SENT[batch])
        return remote(
            ybuf[batch].at[slot, rows],
            back[batch].at[slot, rows],
            back_send.at[batch, slot],
            back_recv.at[batch, slot],
            exp=target_of(group, dy, -1),
        )

    gates = [None, None]

    def pick(batch, group, places, source):
        stride = STRIDE[batch]
        spot = (iota((EXP_Y * stride, TOK), 0) + group * EXP_Y * stride).astype(F32)
        hit = (spot == places[0]) | (spot == places[1])
        plan = jnp.where(hit, 1.0, 0.0).astype(BF16)
        for part in range(2):
            cols = slice(part * 512, (part + 1) * 512)
            sbuf[batch][group * EXP_Y : (group + 1) * EXP_Y, :, cols] = (
                dot(plan, source[:, cols]).astype(BF16).reshape(EXP_Y, stride, 512)
            )

    def spread(group):
        if group > 0:
            place_copies[group - 1].wait_recv()
            for half in range(2):
                if (group, half) not in ((1, 0), (2, 1)):
                    token_copy(group, half).wait_recv()
        places = [place_in[group, c : c + 1, :] for c in range(2)]
        pick(1, group, places, tok_in.at[group])
        for dy in range(1, EXP_Y):
            dispatch(1, group, dy).start()
        rbuf[1][group * EXP_Y] = sbuf[1][group * EXP_Y]

    def front(batch, opening):
        for step in range(1, PAIRS):
            source = lax.rem(pair + step, PAIRS)
            remote(
                ctx_out.at[batch, source],
                ctx_in.at[batch, :, lanes_of(source)],
                ctx_send.at[batch, source],
                ctx_recv.at[batch, source],
                seq=first_of_half + source,
            ).wait_recv()
        context_own(batch).wait()
        if opening:
            for copy in late[:3]:
                copy.wait()
        context = ctx_in[batch]
        for part in range(2):
            cols = slice(part * 512, (part + 1) * 512)
            hidden[batch, :, cols] = tok[batch, 0, :, cols].astype(F32) + dot(
                context, proj[:, cols]
            )
        value = hidden[batch]
        scale = lax.rsqrt(jnp.mean(value * value, axis=1, keepdims=True) + EPSILON)
        rows_value = (value * scale).astype(BF16)
        if batch == 1:
            tok_in[0] = rows_value
            for group, half in ((1, 0), (2, 1), (1, 1), (2, 0)):
                token_copy(group, half).start()
            spread(0)
            source = tok_in[0]
        else:
            normed[...] = rows_value
            for group in (3, 1, 2, 0):
                pick(batch, group, place_rows[0], normed)
                for dy in range(EXP_Y):
                    if group + dy > 0:
                        dispatch(batch, group, dy).start()
            rbuf[batch][0] = sbuf[batch][0]
            source = normed[...]
        logits = dot_t(source, router[...])
        picked = jnp.sum(differences[batch][:, :N_EXP] * logits, axis=1, keepdims=True)
        first = jax.nn.sigmoid(picked)
        gates[batch] = (first, 1.0 - first)

    def serve_all(batch):
        stride = STRIDE[batch]
        count = EXP_Y * stride

        def serve(group, carry):
            for dy in range(EXP_Y):
                if dy == 0 and batch == 1:
                    continue
                if dy == 0:

                    @pl.when(group > 0)
                    def _():
                        dispatch(batch, group, dy).wait_recv()

                else:
                    dispatch(batch, group, dy).wait_recv()
            inputs = rbuf[batch][pl.ds(group * EXP_Y, EXP_Y)].reshape(count, D)
            for low, high in ((0, 512), (512, 1024), (1024, FFW)):
                gate = dot(inputs, gate_w[:, low:high])
                up = dot(inputs, up_w[:, low:high])
                inner = 0.7978845608028654 * (gate + 0.044715 * (gate * gate * gate))
                active[0:count, low:high] = (0.5 * gate * (1.0 + jnp.tanh(inner)) * up).astype(
                    BF16
                )
            for part in range(2):
                cols = slice(part * 512, (part + 1) * 512)
                ybuf[batch][pl.ds(group * EXP_Y, EXP_Y), :, cols] = (
                    dot(active[0:count], down_w[:, cols])
                    .astype(BF16)
                    .reshape(EXP_Y, stride, 512)
                )
            for dy in range(EXP_Y):
                if dy == 0:

                    @pl.when(group > 0)
                    def _():
                        answer(batch, group, dy).start()

                else:
                    answer(batch, group, dy).start()
            return carry

        lax.fori_loop(0, EXP_Z, serve, 0)
        back[batch][0] = ybuf[batch][0]

    def combine(batch):
        stride = STRIDE[batch]
        result = hidden[batch]
        for group in range(EXP_Z):
            for dy in range(EXP_Y):
                if group + dy > 0:
                    answer(batch, group, dy).wait_recv()
            spot = (iota((TOK, EXP_Y * stride), 1) + group * EXP_Y * stride).astype(F32)
            mix = jnp.where(spot == place_cols[batch][0], gates[batch][0], 0.0) + jnp.where(
                spot == place_cols[batch][1], gates[batch][1], 0.0
            )
            coarse = mix.astype(BF16)
            fine = (mix - coarse.astype(F32)).astype(BF16)
            rows = back[batch][group * EXP_Y : (group + 1) * EXP_Y].reshape(EXP_Y * stride, D)
            both = dot(jnp.concatenate([coarse, fine], axis=0), rows)
            result = result + both[:TOK] + both[TOK:]
        out_ref[batch, 0] = result.astype(BF16)

    attention(1, True)
    front(1, True)
    attention(0, False)
    spread(1)
    spread(2)
    front(0, False)
    spread(3)
    for copy in late[3:]:
        copy.wait()
    for batch in ORDER:
        serve_all(batch)
    for batch in ORDER:
        combine(batch)

    for batch in range(2):
        for group in range(EXP_Z):
            for dy in range(EXP_Y):
                if dy > 0 or (batch == 0 and group > 0):
                    dispatch(batch, group, dy).wait_send()
                if group + dy > 0:
                    answer(batch, group, dy).wait_send()
        for step in range(1, PAIRS):
            context_copy(batch, lax.rem(pair + step, PAIRS)).wait_send()

    for group in range(1, EXP_Z):
        place_copies[group - 1].wait_send()
        for half in range(2):
            token_copy(group, half).wait_send()

    @pl.when(upper == 0)
    def _():
        seg_hop.wait_send()
        for batch in range(2):
            sink_hop(batch).wait_send()
            for kind in range(2):
                halo_hop(batch, kind).wait_send()


def local(
    tokens,
    queries,
    key_rows,
    value_rows,
    segments,
    bias_table,
    out_proj,
    router,
    gate_weight,
    up_weight,
    down_weight,
    old_table,
    new_table,
    routes_one,
    routes_two,
):
    any_spec = pl.BlockSpec(memory_space=pl.ANY)
    vmem = pltpu.VMEM
    dma = pltpu.SemaphoreType.DMA
    buffers = [vmem((N_EXP, stride, D), BF16) for stride in STRIDE]
    return pl.pallas_call(
        layer_kernel,
        out_shape=jax.ShapeDtypeStruct((2, 1, TOK, D), BF16),
        in_specs=[any_spec] * 15,
        out_specs=pl.BlockSpec(memory_space=pltpu.VMEM),
        scratch_shapes=[
            vmem((N_EXP, NBUCK), F32),
            vmem((2, 2, TOK), I32),
            vmem((2, 1, N_EXP), I32),
            vmem((2, LANES), I32),
            vmem((N_EXP, D), BF16),
            vmem((2, 1, TOK, D), BF16),
            vmem((D, D), BF16),
            vmem((D, FFW), BF16),
            vmem((D, FFW), BF16),
            vmem((FFW, D), BF16),
            vmem((2, N_SEQ, 1, TOK), I32),
            vmem((2, PAIRS, TOK, LANES), BF16),
            vmem((2, PAIRS + WIN, TOK, LANES), BF16),
            vmem((2, PAIRS + WIN, TOK, LANES), BF16),
            vmem((N_SEQ, TOK, TOK), I32),
            vmem((WIN, 2 * TOK, TOK), F32),
            vmem((2, 2, 8, LANES), F32),
            vmem((2, 2, 8, LANES), F32),
            vmem((2, 8, LANES), F32),
            vmem((2, PAIRS, TOK, LANES), BF16),
            vmem((2, TOK, D), BF16),
            vmem((2, TOK, D), F32),
            vmem((TOK, D), BF16),
            *buffers,
            *buffers,
            *buffers,
            *buffers,
            vmem((EXP_Y * STRIDE[1], FFW), BF16),
            dma((11,)),
            dma((2, 3, PAIRS)),
            dma((2, 3, PAIRS)),
            dma((2, 3)),
            dma((PAIRS,)),
            dma((PAIRS,)),
            dma(()),
            dma((5,)),
            dma((5,)),
            dma((2,)),
            dma((2,)),
            dma((2, PAIRS)),
            dma((2, PAIRS)),
            dma((2,)),
            dma((2, N_EXP)),
            dma((2, N_EXP)),
            dma((2, N_EXP)),
            dma((2, N_EXP)),
            vmem((EXP_Z, TOK, D), BF16),
            vmem((EXP_Z, 2, TOK), F32),
            vmem((2, TOK), F32),
            dma((EXP_Z, 2)),
            dma((EXP_Z, 2)),
            dma((EXP_Z,)),
            dma((EXP_Z,)),
        ],
        compiler_params=pltpu.CompilerParams(
            collective_id=0, has_side_effects=True, vmem_limit_bytes=56 << 20
        ),
        name="layer",
    )(
        bias_table,
        segments,
        queries,
        key_rows,
        value_rows,
        tokens,
        out_proj,
        router.T,
        jnp.swapaxes(routes_one, 1, 2),
        jnp.swapaxes(routes_two, 1, 2),
        old_table[None],
        new_table[None],
        gate_weight,
        up_weight,
        down_weight,
    )


def solution(mesh):
    placed = (
        P(None, "exp", "seq", None),
        P(None, "exp", "seq", None),
        P(None, "exp", "seq", None),
        P(None, "exp", "seq", None),
        P(None, "exp", "seq"),
        P(),
        P(),
        P(),
        P("exp", None, None),
        P("exp", None, None),
        P("exp", None, None),
        P(),
        P(),
        P("exp", "seq", None),
        P("exp", "seq", None),
    )
    return jax.shard_map(
        local, mesh=mesh, in_specs=placed, out_specs=P(None, "exp", "seq", None), check_vma=False
    )
```

```python
import jax
import jax.numpy as jnp
from jax import lax
from jax.experimental import pallas as pl
from jax.experimental.pallas import tpu as pltpu
from jax.sharding import PartitionSpec as P

MESH = pl.DeviceIdType.MESH
BF16 = jnp.bfloat16
F32 = jnp.float32
I32 = jnp.int32

N_SEQ = 16
N_EXP = 16
EXP_Y = 4
EXP_Z = 4
TOK = 128
D = 1024
FFW = 1408
NBUCK = 32
WIN = 4
PAIRS = 8
LANES = 128
HALF = 64
CAP = 20
STRIDE = (32, 48)
SENT = (24, 40)
SINK_BUCKET = 31

EPSILON = 1e-06
MASKED = -1e30


def iota(shape, dim):
    return lax.broadcasted_iota(I32, shape, dim)


def dot(a, b):
    return jnp.dot(a, b, preferred_element_type=F32)


def dot_t(a, b):
    return lax.dot_general(a, b, (((1,), (1,)), ((), ())), preferred_element_type=F32)


def turned(row):
    return jnp.transpose(jnp.broadcast_to(row, (LANES, LANES)))


def remote(src, dst, send, recv, **device):
    return pltpu.make_async_remote_copy(
        src_ref=src,
        dst_ref=dst,
        send_sem=send,
        recv_sem=recv,
        device_id=device,
        device_id_type=MESH,
    )


def bias_of_distance(distance, values):
    result = jnp.broadcast_to(values[0], distance.shape)
    for bucket in range(1, 10):
        result = jnp.where(distance >= (1 << (bucket - 1)), values[bucket], result)
    return result


def plane_step(group):
    return group + (group // 2) * (1 - 2 * lax.rem(group, 2))


def layer_kernel(
    bias_hbm,
    seg_hbm,
    q_hbm,
    k_hbm,
    v_hbm,
    tok_hbm,
    proj_hbm,
    router_hbm,
    one_hbm,
    two_hbm,
    old_hbm,
    new_hbm,
    gate_hbm,
    up_hbm,
    down_hbm,
    out_ref,
    table,
    routes,
    held,
    tabs,
    router,
    tok,
    proj,
    gate_w,
    up_w,
    down_w,
    segs,
    qb,
    kb,
    vb,
    segcol,
    bias,
    sink_out,
    sink_in,
    sink_rows,
    ctx_out,
    ctx_in,
    hidden,
    normed,
    sbuf_one,
    sbuf_two,
    rbuf_one,
    rbuf_two,
    ybuf_one,
    ybuf_two,
    back_one,
    back_two,
    active,
    load_sem,
    qkv_send,
    qkv_recv,
    qkv_own,
    seg_send,
    seg_recv,
    seg_own,
    hop_send,
    hop_recv,
    sink_send,
    sink_recv,
    ctx_send,
    ctx_recv,
    ctx_own,
    go_send,
    go_recv,
    back_send,
    back_recv,
    tok_in,
    place_in,
    place_out,
    tok_send,
    tok_recv,
    place_send,
    place_recv,
    gate_in,
    gate_out,
    gate_send,
    gate_recv,
    part_out,
    part_in,
    red_in,
    part_send,
    part_recv,
    red_send,
    red_recv,
    hidden_part,
):
    me = lax.axis_index("seq")
    my_exp = lax.axis_index("exp")
    upper, pair = me // PAIRS, lax.rem(me, PAIRS)
    me_y, me_z = my_exp // EXP_Z, lax.rem(my_exp, EXP_Z)
    first_of_half = upper * PAIRS
    across = lax.rem(me + PAIRS, N_SEQ)
    sbuf, rbuf = (sbuf_one, sbuf_two), (rbuf_one, rbuf_two)
    ybuf, back = (ybuf_one, ybuf_two), (back_one, back_two)

    early = [
        pltpu.make_async_copy(src, dst, load_sem.at[i])
        for i, (src, dst) in enumerate(
            (
                (old_hbm, held.at[0]),
                (new_hbm, held.at[1]),
                (one_hbm.at[0], routes.at[0]),
                (two_hbm.at[0], routes.at[1]),
                (bias_hbm, table),
            )
        )
    ]
    late = [
        pltpu.make_async_copy(src, dst, load_sem.at[i + 5])
        for i, (src, dst) in enumerate(
            (
                (router_hbm, router),
                (tok_hbm, tok),
                (proj_hbm, proj),
                (gate_hbm.at[0], gate_w),
                (up_hbm.at[0], up_w),
                (down_hbm.at[0], down_w),
            )
        )
    ]
    for copy in early:
        copy.start()

    for batch in range(2):
        low = STRIDE[batch] - 16
        back[batch][:, low:, :] = jnp.zeros((N_EXP, 16, D), BF16)

    @pl.when(upper == 0)
    def _():
        for batch in range(2):
            kb[batch, 0:WIN] = jnp.zeros((WIN, TOK, LANES), BF16)
            vb[batch, 0:WIN] = jnp.zeros((WIN, TOK, LANES), BF16)
            segs[batch, 0:PAIRS] = jnp.full((PAIRS, 1, TOK), -1, I32)
            sink_in[batch] = jnp.zeros((2, 8, LANES), F32)

    barrier = pltpu.get_barrier_semaphore()
    for step in range(1, PAIRS):
        pl.semaphore_signal(
            barrier,
            inc=1,
            device_id={"seq": first_of_half + lax.rem(pair + step, PAIRS)},
            device_id_type=MESH,
        )
    pl.semaphore_signal(barrier, inc=1, device_id={"seq": across}, device_id_type=MESH)
    for step in range(1, N_EXP):
        pl.semaphore_signal(
            barrier,
            inc=1,
            device_id={"exp": lax.rem(my_exp + step, N_EXP)},
            device_id_type=MESH,
        )
    pl.semaphore_wait(barrier, PAIRS + N_EXP - 1)

    def lanes_of(which):
        return pl.ds(pl.multiple_of(which * LANES, LANES), LANES)

    def qkv_parts(batch, target):
        lanes = lanes_of(target)
        return (
            (k_hbm.at[batch, 0, :, lanes], kb.at[batch, pair + WIN]),
            (v_hbm.at[batch, 0, :, lanes], vb.at[batch, pair + WIN]),
            (q_hbm.at[batch, 0, :, lanes], qb.at[batch, pair]),
        )

    def qkv_copies(batch):
        copies = []
        for step in range(1, PAIRS):
            target = lax.rem(pair + step, PAIRS)
            for kind, (src, dst) in enumerate(qkv_parts(batch, target)):
                copies.append(
                    remote(
                        src,
                        dst,
                        qkv_send.at[batch, kind, step],
                        qkv_recv.at[batch, kind, step],
                        seq=first_of_half + target,
                    )
                )
        for kind, (src, dst) in enumerate(qkv_parts(batch, pair)):
            copies.append(pltpu.make_async_copy(src, dst, qkv_own.at[batch, kind]))
        return copies

    qkv = [qkv_copies(batch) for batch in range(2)]
    seg_copies = [
        remote(
            seg_hbm,
            segs.at[:, PAIRS + pair],
            seg_send.at[step],
            seg_recv.at[step],
            seq=first_of_half + lax.rem(pair + step, PAIRS),
        )
        for step in range(1, PAIRS)
    ]
    seg_copies.append(pltpu.make_async_copy(seg_hbm, segs.at[:, PAIRS + pair], seg_own))
    seg_hop = remote(
        segs.at[:, PAIRS : 2 * PAIRS],
        segs.at[:, 0:PAIRS],
        hop_send.at[4],
        hop_recv.at[4],
        seq=across,
    )

    def halo_hop(batch, kind):
        block = (kb, vb)[kind]
        return remote(
            block.at[batch, PAIRS : PAIRS + WIN],
            block.at[batch, 0:WIN],
            hop_send.at[2 * batch + kind],
            hop_recv.at[2 * batch + kind],
            seq=across,
        )

    def sink_hop(batch):
        return remote(
            sink_out.at[batch],
            sink_in.at[batch],
            sink_send.at[batch],
            sink_recv.at[batch],
            seq=across,
        )

    for copy in seg_copies:
        copy.start()
    for copy in qkv[1]:
        copy.start()
    for copy in late:
        copy.start()
    for copy in early:
        copy.wait()

    qi = iota((TOK, TOK), 0)
    kj = iota((TOK, TOK), 1)
    for head in range(2):
        head_row = table[pl.ds(2 * pair + head, 1), :]
        values = [head_row[:, bucket : bucket + 1] for bucket in range(10)]
        rows = slice(head * TOK, (head + 1) * TOK)
        merged = jnp.where(kj <= qi, qi - kj, qi - kj + WIN * TOK)
        bias[0, rows, :] = bias_of_distance(merged, values)
        for block in range(1, WIN):
            bias[block, rows, :] = bias_of_distance(qi - kj + (WIN - block) * TOK, values)
    sink_bias = jnp.where(
        iota((2 * TOK, 1), 0) < TOK,
        table[pl.ds(2 * pair, 1), :][:, SINK_BUCKET : SINK_BUCKET + 1],
        table[pl.ds(2 * pair + 1, 1), :][:, SINK_BUCKET : SINK_BUCKET + 1],
    )

    lane = iota((LANES, LANES), 1)
    row = iota((LANES, LANES), 0)
    tabs[...] = jnp.full((2, LANES), -1, I32)
    tabs[0:1, 0:N_EXP] = held[0]
    tabs[1:2, 0:N_EXP] = held[1]
    steps_y = lax.rem(row // EXP_Z - me_y + 2 * EXP_Y * EXP_Y, EXP_Y)
    steps_z = lax.rem(lax.rem(row, EXP_Z) - me_z + EXP_Z, EXP_Z)
    groups = steps_z + (steps_z // 2) * (1 - 2 * lax.rem(steps_z, 2))
    slot_of_row = (groups * EXP_Y + steps_y).astype(F32)
    holds = turned(tabs[0:1, :]) == lane
    slot_of_expert = jnp.sum(jnp.where(holds, slot_of_row, 0.0), axis=0, keepdims=True)
    new_row = tabs[1:2, :]
    new_col = turned(new_row)
    served = new_col == lane
    serving = jnp.where(served, 1.0, 0.0).astype(BF16)
    slot_two = jnp.sum(jnp.where(served, slot_of_expert, 0.0), axis=1, keepdims=True)
    again = jnp.where((new_col == new_row) & (lane < row), 1.0, 0.0)
    again = jnp.sum(again, axis=1, keepdims=True)
    base_two = jnp.transpose(
        jnp.broadcast_to(slot_two * STRIDE[1] + again * CAP, (LANES, LANES))
    )[0:1, :]
    bases = (slot_of_expert * STRIDE[0], base_two)
    lower = jnp.where(row > lane, 1.0, 0.0).astype(BF16)
    place_cols, place_rows, differences = [], [], []
    for batch in range(2):
        member = [
            jnp.where(turned(routes[batch, c : c + 1, :]) == lane, 1.0, 0.0) for c in range(2)
        ]
        counts = [dot(lower, m.astype(BF16)) for m in member]
        counts[1] = counts[1] + jnp.sum(member[0], axis=0, keepdims=True)
        cols = [
            jnp.sum(m * (c + bases[batch]), axis=1, keepdims=True)
            for m, c in zip(member, counts)
        ]
        place_cols.append(cols)
        place_rows.append(
            [jnp.transpose(jnp.broadcast_to(col, (TOK, TOK)))[0:1, :] for col in cols]
        )
        difference = member[0] - member[1]
        if batch == 1:
            difference = dot(difference.astype(BF16), serving)
        differences.append(difference)
    for c in range(2):
        place_out[c : c + 1, :] = place_rows[1][c]
    place_in[0] = place_out[...]

    def plane(step):
        return me_y * EXP_Z + lax.rem(me_z + step, EXP_Z)

    place_copies = [
        remote(
            place_out,
            place_in.at[group],
            place_send.at[group],
            place_recv.at[group],
            exp=plane(step),
        )
        for group, step in ((1, 1), (2, 3), (3, 2))
    ]
    for copy in place_copies:
        copy.start()
    gate_copies = [
        remote(
            gate_out,
            gate_in.at[group],
            gate_send.at[group],
            gate_recv.at[group],
            exp=plane(step),
        )
        for group, step in ((1, 1), (2, 3), (3, 2))
    ]

    def part_copy(group, half):
        rows = slice(half * (TOK // 2), (half + 1) * (TOK // 2))
        return remote(
            part_out.at[group, rows],
            part_in.at[group, rows],
            part_send.at[group, half],
            part_recv.at[group, half],
            exp=plane((3, 1)[group - 1]),
        )

    def far_copy(half):
        rows = slice(half * (TOK // 2), (half + 1) * (TOK // 2))
        return remote(
            part_out.at[3, rows],
            red_in.at[half],
            red_send.at[half],
            red_recv.at[half],
            exp=plane((3, 1)[half]),
        )

    def token_copy(group, half):
        rows = slice(half * (TOK // 2), (half + 1) * (TOK // 2))
        origin = 1 + half if group == 3 else 0
        step = (1, 3)[half] if group == 3 else (1, 3)[group - 1]
        return remote(
            tok_in.at[origin, rows],
            tok_in.at[group, rows],
            tok_send.at[group, half],
            tok_recv.at[group, half],
            exp=plane(step),
        )

    def relay():
        for half in range(2):
            token_copy(1 + half, half).wait_recv()
            token_copy(3, half).start()

    lane_head = iota((2 * TOK, LANES), 1) // HALF
    row_head = iota((2 * TOK, LANES), 0) // TOK
    own_half = lane_head == row_head
    causal = lax.rem(iota((2 * TOK, TOK), 0), TOK) >= iota((2 * TOK, TOK), 1)

    def twice(value):
        return jnp.concatenate([value, value], axis=0)

    def context_copy(batch, block):
        return remote(
            ctx_out.at[batch, block],
            ctx_in.at[batch, :, lanes_of(pair)],
            ctx_send.at[batch, block],
            ctx_recv.at[batch, pair],
            seq=first_of_half + block,
        )

    def context_own(batch):
        return pltpu.make_async_copy(
            ctx_out.at[batch, pair], ctx_in.at[batch, :, lanes_of(pair)], ctx_own.at[batch]
        )

    def attention(batch, opening):
        if opening:
            for copy in seg_copies:
                copy.wait()

            @pl.when(upper == 0)
            def _():
                seg_hop.start()

        for copy in qkv[batch]:
            copy.wait()

        @pl.when(upper == 0)
        def _():
            for kind in range(2):
                halo_hop(batch, kind).start()

        if opening:
            for copy in qkv[0]:
                copy.start()

            @pl.when(upper == 1)
            def _():
                seg_hop.wait_recv()

        def columns(block, before):
            line = segs[batch, block]
            segcol[block] = turned(line)
            document = iota((8, TOK), 0)
            return before + jnp.where((line < document) & (line >= 0), 1, 0)

        ahead = lax.fori_loop(0, 2 * PAIRS, columns, jnp.zeros((8, TOK), I32))
        starts = jnp.sum(ahead, axis=1, keepdims=True)

        def sinks(block, sums):
            k_sum, v_sum = sums
            spot = (upper * PAIRS + block) * TOK + iota((8, TOK), 1)
            pick = jnp.where(spot == starts, 1.0, 0.0).astype(BF16)
            return (
                k_sum + dot(pick, kb[batch, block + WIN]),
                v_sum + dot(pick, vb[batch, block + WIN]),
            )

        zero = jnp.zeros((8, LANES), F32)
        k_sink, v_sink = lax.fori_loop(0, PAIRS, sinks, (zero, zero))
        sink_out[batch, 0] = k_sink
        sink_out[batch, 1] = v_sink

        @pl.when(upper == 0)
        def _():
            sink_hop(batch).start()

        @pl.when(upper == 1)
        def _():
            sink_hop(batch).wait_recv()

        sink_rows[0] = k_sink + sink_in[batch, 0]
        sink_rows[1] = v_sink + sink_in[batch, 1]

        def attend(block):
            query = twice(qb[batch, block].astype(F32) * 0.125)
            query = jnp.where(own_half, query, 0.0)
            query_rows = query.astype(BF16)
            mine = segcol[block + PAIRS]
            pieces = []
            for near in range(WIN + 1):
                raw = dot_t(query_rows, kb[batch, block + near])
                same = twice(mine == segs[batch, block + near + WIN])
                pieces.append((raw, same))
            merged = jnp.where(causal, pieces[WIN][0], pieces[0][0])
            merged_same = jnp.where(
                causal, pieces[WIN][1].astype(I32), pieces[0][1].astype(I32)
            )
            scores = [jnp.where(merged_same > 0, merged + bias[0], MASKED)]
            for near in range(1, WIN):
                raw, same = pieces[near]
                scores.append(jnp.where(same, raw + bias[near], MASKED))
            chosen_doc = iota((8, LANES), 0) == segs[batch, block + PAIRS][:, 0:1]
            k_row = jnp.sum(jnp.where(chosen_doc, sink_rows[0], 0.0), axis=0, keepdims=True)
            v_row = jnp.sum(jnp.where(chosen_doc, sink_rows[1], 0.0), axis=0, keepdims=True)
            sink_seen = twice(mine[:, 0:1] == segcol[block + WIN][:, 0:1])
            sink = jnp.sum(query * k_row, axis=1, keepdims=True) + sink_bias
            sink = jnp.where(sink_seen, sink, MASKED)
            peak = jnp.maximum(
                jnp.maximum(scores[0], scores[1]), jnp.maximum(scores[2], scores[3])
            )
            peak = jnp.maximum(jnp.max(peak, axis=1, keepdims=True), sink)
            weights = [jnp.exp(score - peak) for score in scores]
            sink_weight = jnp.exp(sink - peak)
            total = (weights[0] + weights[1]) + (weights[2] + weights[3])
            total = jnp.sum(total, axis=1, keepdims=True) + sink_weight
            mixed = sink_weight * v_row
            mixed = mixed + dot(jnp.where(causal, 0.0, weights[0]).astype(BF16), vb[batch, block])
            mixed = mixed + dot(
                jnp.where(causal, weights[0], 0.0).astype(BF16), vb[batch, block + WIN]
            )
            for near in range(1, WIN):
                mixed = mixed + dot(weights[near].astype(BF16), vb[batch, block + near])
            mixed = mixed / total
            ctx_out[batch, block] = jnp.where(
                lane_head[:TOK] == 0, mixed[:TOK], mixed[TOK:]
            ).astype(BF16)

            @pl.when(block == pair)
            def _():
                context_own(batch).start()

            @pl.when(block != pair)
            def _():
                context_copy(batch, block).start()

        def attend_late(turn, carry):
            attend(WIN + lax.rem(pair + turn, WIN))
            return carry

        def attend_early(turn, carry):
            attend(lax.rem(pair + turn, WIN))
            return carry

        lax.fori_loop(0, WIN, attend_late, 0)
        if not opening:
            relay()

        @pl.when(upper == 1)
        def _():
            for kind in range(2):
                halo_hop(batch, kind).wait_recv()

        lax.fori_loop(0, WIN, attend_early, 0)

    def target_of(group, dy, sign):
        y = lax.rem(me_y + EXP_Y + sign * dy, EXP_Y)
        z = lax.rem(me_z + EXP_Z + sign * plane_step(group), EXP_Z)
        return y * EXP_Z + z

    def beside(dy):
        return lax.rem(me_y + dy, EXP_Y) * EXP_Z + me_z

    def dispatch(batch, group, dy):
        slot = group * EXP_Y + dy
        rows = slice(0, SENT[batch])
        return remote(
            sbuf[batch].at[slot, rows],
            rbuf[batch].at[slot, rows],
            go_send.at[batch, slot],
            go_recv.at[batch, slot],
            exp=beside(dy) if batch == 1 else target_of(group, dy, 1),
        )

    def answer(batch, group, dy):
        slot = group * EXP_Y + dy
        rows = slice(0, SENT[batch])
        return remote(
            ybuf[batch].at[slot, rows],
            back[batch].at[slot, rows],
            back_send.at[batch, slot],
            back_recv.at[batch, slot],
            exp=beside(EXP_Y - dy) if batch == 1 else target_of(group, dy, -1),
        )

    gates = [None, None]

    def pick(batch, group, places, source):
        stride = STRIDE[batch]
        spot = (iota((EXP_Y * stride, TOK), 0) + group * EXP_Y * stride).astype(F32)
        hit = (spot == places[0]) | (spot == places[1])
        plan = jnp.where(hit, 1.0, 0.0).astype(BF16)
        for part in range(2):
            cols = slice(part * 512, (part + 1) * 512)
            sbuf[batch][group * EXP_Y : (group + 1) * EXP_Y, :, cols] = (
                dot(plan, source[:, cols]).astype(BF16).reshape(EXP_Y, stride, 512)
            )

    def spread(group):
        if group > 0:
            place_copies[group - 1].wait_recv()
            for half in range(2):
                if (group, half) not in ((1, 0), (2, 1)):
                    token_copy(group, half).wait_recv()
        places = [place_in[group, c : c + 1, :] for c in range(2)]
        pick(1, group, places, tok_in.at[group])
        for dy in range(1, EXP_Y):
            dispatch(1, group, dy).start()
        rbuf[1][group * EXP_Y] = sbuf[1][group * EXP_Y]

    def front(batch, opening):
        for step in range(1, PAIRS):
            source = lax.rem(pair + step, PAIRS)
            remote(
                ctx_out.at[batch, source],
                ctx_in.at[batch, :, lanes_of(source)],
                ctx_send.at[batch, source],
                ctx_recv.at[batch, source],
                seq=first_of_half + source,
            ).wait_recv()
        context_own(batch).wait()
        if opening:
            for copy in late[:3]:
                copy.wait()
        context = ctx_in[batch]
        for part in range(2):
            cols = slice(part * 512, (part + 1) * 512)
            hidden[batch, :, cols] = tok[batch, 0, :, cols].astype(F32) + dot(
                context, proj[:, cols]
            )
        value = hidden[batch]
        scale = lax.rsqrt(jnp.mean(value * value, axis=1, keepdims=True) + EPSILON)
        rows_value = (value * scale).astype(BF16)
        if batch == 1:
            tok_in[0] = rows_value
            for group, half in ((1, 0), (2, 1), (1, 1), (2, 0)):
                token_copy(group, half).start()
            spread(0)
            source = tok_in[0]
        else:
            normed[...] = rows_value
            for group in (3, 1, 2, 0):
                pick(batch, group, place_rows[0], normed)
                for dy in range(EXP_Y):
                    if group + dy > 0:
                        dispatch(batch, group, dy).start()
            rbuf[batch][0] = sbuf[batch][0]
            source = normed[...]
        logits = dot_t(source, router[...])
        picked = jnp.sum(differences[batch][:, :N_EXP] * logits, axis=1, keepdims=True)
        first = jax.nn.sigmoid(picked)
        gates[batch] = (first, 1.0 - first)
        if batch == 1:
            for c in range(2):
                gate_out[c : c + 1, :] = jnp.transpose(
                    jnp.broadcast_to(gates[batch][c], (TOK, TOK))
                )[0:1, :]
            gate_in[0] = gate_out[...]
            for copy in gate_copies:
                copy.start()

    def serve_all(batch):
        stride = STRIDE[batch]
        count = EXP_Y * stride

        def serve(group, carry):
            for dy in range(EXP_Y):
                if dy == 0 and batch == 1:
                    continue
                if dy == 0:

                    @pl.when(group > 0)
                    def _():
                        dispatch(batch, group, dy).wait_recv()

                else:
                    dispatch(batch, group, dy).wait_recv()
            inputs = rbuf[batch][pl.ds(group * EXP_Y, EXP_Y)].reshape(count, D)
            for low, high in ((0, 512), (512, 1024), (1024, FFW)):
                gate = dot(inputs, gate_w[:, low:high])
                up = dot(inputs, up_w[:, low:high])
                inner = 0.7978845608028654 * (gate + 0.044715 * (gate * gate * gate))
                active[0:count, low:high] = (0.5 * gate * (1.0 + jnp.tanh(inner)) * up).astype(
                    BF16
                )
            for part in range(2):
                cols = slice(part * 512, (part + 1) * 512)
                ybuf[batch][pl.ds(group * EXP_Y, EXP_Y), :, cols] = (
                    dot(active[0:count], down_w[:, cols])
                    .astype(BF16)
                    .reshape(EXP_Y, stride, 512)
                )
            for dy in range(EXP_Y):
                if dy == 0 and batch == 1:
                    back[1][group * EXP_Y] = ybuf[1][group * EXP_Y]
                elif dy == 0:

                    @pl.when(group > 0)
                    def _():
                        answer(batch, group, dy).start()

                else:
                    answer(batch, group, dy).start()
            return carry

        lax.fori_loop(0, EXP_Z, serve, 0)
        if batch == 0:
            back[batch][0] = ybuf[batch][0]

    def blend(batch, group, places, weights):
        stride = STRIDE[batch]
        spot = (iota((TOK, EXP_Y * stride), 1) + group * EXP_Y * stride).astype(F32)
        mix = jnp.where(spot == places[0], weights[0], 0.0) + jnp.where(
            spot == places[1], weights[1], 0.0
        )
        coarse = mix.astype(BF16)
        fine = (mix - coarse.astype(F32)).astype(BF16)
        rows = back[batch][group * EXP_Y : (group + 1) * EXP_Y].reshape(EXP_Y * stride, D)
        both = dot(jnp.concatenate([coarse, fine], axis=0), rows)
        return both[:TOK] + both[TOK:]

    def plane_sum(group):
        for dy in range(1, EXP_Y):
            answer(1, group, dy).wait_recv()
        if group == 0:
            return blend(1, 0, place_cols[1], gates[1])
        gate_copies[group - 1].wait_recv()
        places = [turned(place_in[group, c : c + 1, :])[:, 0:1] for c in range(2)]
        weights = [turned(gate_in[group, c : c + 1, :])[:, 0:1] for c in range(2)]
        return blend(1, group, places, weights)

    half_rows = (slice(0, TOK // 2), slice(TOK // 2, TOK))

    def plane_sums():
        part_out[3] = plane_sum(3).astype(BF16)
        for half in range(2):
            far_copy(half).start()
        for group in (1, 2):
            total = plane_sum(group)
            near, far = half_rows[group - 1], half_rows[2 - group]
            part_out[group, far] = total[far].astype(BF16)
            part_copy(group, 2 - group).start()
            hidden_part[group - 1] = total[near]
        hidden[1] = hidden[1] + plane_sum(0)

    def pass_on():
        for group in (1, 2):
            near = half_rows[group - 1]
            far_copy(group - 1).wait_recv()
            total = hidden_part[group - 1] + red_in[group - 1].astype(F32)
            part_out[group, near] = total.astype(BF16)
            part_copy(group, group - 1).start()

    def finish_one():
        result = hidden[0]
        for group in range(EXP_Z):
            for dy in range(EXP_Y):
                if group + dy > 0:
                    answer(0, group, dy).wait_recv()
            result = result + blend(0, group, place_cols[0], gates[0])
        out_ref[0, 0] = result.astype(BF16)

    def finish_two():
        for group in (1, 2):
            for half in range(2):
                part_copy(group, half).wait_recv()
        result = hidden[1] + part_in[1].astype(F32) + part_in[2].astype(F32)
        out_ref[1, 0] = result.astype(BF16)

    attention(1, True)
    front(1, True)
    attention(0, False)
    spread(1)
    spread(2)
    front(0, False)
    spread(3)
    for copy in late[3:]:
        copy.wait()
    serve_all(1)
    serve_all(0)
    plane_sums()
    pass_on()
    finish_one()
    finish_two()

    for batch in range(2):
        for group in range(EXP_Z):
            for dy in range(EXP_Y):
                if dy > 0 or (batch == 0 and group > 0):
                    dispatch(batch, group, dy).wait_send()
                    answer(batch, group, dy).wait_send()
        for step in range(1, PAIRS):
            context_copy(batch, lax.rem(pair + step, PAIRS)).wait_send()

    for group in range(1, EXP_Z):
        place_copies[group - 1].wait_send()
        gate_copies[group - 1].wait_send()
        for half in range(2):
            token_copy(group, half).wait_send()
            if group < 3:
                part_copy(group, half).wait_send()
    for half in range(2):
        far_copy(half).wait_send()

    @pl.when(upper == 0)
    def _():
        seg_hop.wait_send()
        for batch in range(2):
            sink_hop(batch).wait_send()
            for kind in range(2):
                halo_hop(batch, kind).wait_send()


def local(
    tokens,
    queries,
    key_rows,
    value_rows,
    segments,
    bias_table,
    out_proj,
    router,
    gate_weight,
    up_weight,
    down_weight,
    old_table,
    new_table,
    routes_one,
    routes_two,
):
    any_spec = pl.BlockSpec(memory_space=pl.ANY)
    vmem = pltpu.VMEM
    dma = pltpu.SemaphoreType.DMA
    buffers = [vmem((N_EXP, stride, D), BF16) for stride in STRIDE]
    return pl.pallas_call(
        layer_kernel,
        out_shape=jax.ShapeDtypeStruct((2, 1, TOK, D), BF16),
        in_specs=[any_spec] * 15,
        out_specs=pl.BlockSpec(memory_space=pltpu.VMEM),
        scratch_shapes=[
            vmem((N_EXP, NBUCK), F32),
            vmem((2, 2, TOK), I32),
            vmem((2, 1, N_EXP), I32),
            vmem((2, LANES), I32),
            vmem((N_EXP, D), BF16),
            vmem((2, 1, TOK, D), BF16),
            vmem((D, D), BF16),
            vmem((D, FFW), BF16),
            vmem((D, FFW), BF16),
            vmem((FFW, D), BF16),
            vmem((2, N_SEQ, 1, TOK), I32),
            vmem((2, PAIRS, TOK, LANES), BF16),
            vmem((2, PAIRS + WIN, TOK, LANES), BF16),
            vmem((2, PAIRS + WIN, TOK, LANES), BF16),
            vmem((N_SEQ, TOK, TOK), I32),
            vmem((WIN, 2 * TOK, TOK), F32),
            vmem((2, 2, 8, LANES), F32),
            vmem((2, 2, 8, LANES), F32),
            vmem((2, 8, LANES), F32),
            vmem((2, PAIRS, TOK, LANES), BF16),
            vmem((2, TOK, D), BF16),
            vmem((2, TOK, D), F32),
            vmem((TOK, D), BF16),
            *buffers,
            *buffers,
            *buffers,
            *buffers,
            vmem((EXP_Y * STRIDE[1], FFW), BF16),
            dma((11,)),
            dma((2, 3, PAIRS)),
            dma((2, 3, PAIRS)),
            dma((2, 3)),
            dma((PAIRS,)),
            dma((PAIRS,)),
            dma(()),
            dma((5,)),
            dma((5,)),
            dma((2,)),
            dma((2,)),
            dma((2, PAIRS)),
            dma((2, PAIRS)),
            dma((2,)),
            dma((2, N_EXP)),
            dma((2, N_EXP)),
            dma((2, N_EXP)),
            dma((2, N_EXP)),
            vmem((EXP_Z, TOK, D), BF16),
            vmem((EXP_Z, 2, TOK), F32),
            vmem((2, TOK), F32),
            dma((EXP_Z, 2)),
            dma((EXP_Z, 2)),
            dma((EXP_Z,)),
            dma((EXP_Z,)),
            vmem((EXP_Z, 2, TOK), F32),
            vmem((2, TOK), F32),
            dma((EXP_Z,)),
            dma((EXP_Z,)),
            vmem((EXP_Z, TOK, D), BF16),
            vmem((EXP_Z, TOK, D), BF16),
            vmem((2, TOK // 2, D), BF16),
            dma((EXP_Z, 2)),
            dma((EXP_Z, 2)),
            dma((2,)),
            dma((2,)),
            vmem((2, TOK // 2, D), F32),
        ],
        compiler_params=pltpu.CompilerParams(
            collective_id=0, has_side_effects=True, vmem_limit_bytes=56 << 20
        ),
        name="layer",
    )(
        bias_table,
        segments,
        queries,
        key_rows,
        value_rows,
        tokens,
        out_proj,
        router.T,
        jnp.swapaxes(routes_one, 1, 2),
        jnp.swapaxes(routes_two, 1, 2),
        old_table[None],
        new_table[None],
        gate_weight,
        up_weight,
        down_weight,
    )


def solution(mesh):
    placed = (
        P(None, "exp", "seq", None),
        P(None, "exp", "seq", None),
        P(None, "exp", "seq", None),
        P(None, "exp", "seq", None),
        P(None, "exp", "seq"),
        P(),
        P(),
        P(),
        P("exp", None, None),
        P("exp", None, None),
        P("exp", None, None),
        P(),
        P(),
        P("exp", "seq", None),
        P("exp", "seq", None),
    )
    return jax.shard_map(
        local, mesh=mesh, in_specs=placed, out_specs=P(None, "exp", "seq", None), check_vma=False
    )
```

```python
import jax
import jax.numpy as jnp
from jax import lax
from jax.experimental import pallas as pl
from jax.experimental.pallas import tpu as pltpu
from jax.sharding import PartitionSpec as P

MESH = pl.DeviceIdType.MESH
BF16 = jnp.bfloat16
F32 = jnp.float32
I32 = jnp.int32

N_SEQ = 16
N_EXP = 16
EXP_Y = 4
EXP_Z = 4
TOK = 128
D = 1024
FFW = 1408
NBUCK = 32
WIN = 4
PAIRS = 8
LANES = 128
HALF = 64
CAP = 20
STRIDE = (32, 48)
SENT = (24, 40)
SINK_BUCKET = 31

EPSILON = 1e-06
MASKED = -1e30


def iota(shape, dim):
    return lax.broadcasted_iota(I32, shape, dim)


def dot(a, b):
    return jnp.dot(a, b, preferred_element_type=F32)


def dot_t(a, b):
    return lax.dot_general(a, b, (((1,), (1,)), ((), ())), preferred_element_type=F32)


def turned(row):
    return jnp.transpose(jnp.broadcast_to(row, (LANES, LANES)))


def remote(src, dst, send, recv, **device):
    return pltpu.make_async_remote_copy(
        src_ref=src,
        dst_ref=dst,
        send_sem=send,
        recv_sem=recv,
        device_id=device,
        device_id_type=MESH,
    )


def bias_of_distance(distance, values):
    result = jnp.broadcast_to(values[0], distance.shape)
    for bucket in range(1, 10):
        result = jnp.where(distance >= (1 << (bucket - 1)), values[bucket], result)
    return result


def plane_step(group):
    return group + (group // 2) * (1 - 2 * lax.rem(group, 2))


def layer_kernel(
    bias_hbm,
    seg_hbm,
    q_hbm,
    k_hbm,
    v_hbm,
    tok_hbm,
    proj_hbm,
    router_hbm,
    one_hbm,
    two_hbm,
    old_hbm,
    new_hbm,
    gate_hbm,
    up_hbm,
    down_hbm,
    out_ref,
    table,
    routes,
    held,
    tabs,
    router,
    tok,
    proj,
    gate_w,
    up_w,
    down_w,
    segs,
    qb,
    kb,
    vb,
    segcol,
    bias,
    sink_out,
    sink_in,
    sink_rows,
    ctx_out,
    ctx_in,
    hidden,
    normed,
    sbuf_one,
    sbuf_two,
    rbuf_one,
    rbuf_two,
    ybuf_one,
    ybuf_two,
    back_one,
    back_two,
    active,
    load_sem,
    qkv_send,
    qkv_recv,
    qkv_own,
    seg_send,
    seg_recv,
    seg_own,
    hop_send,
    hop_recv,
    sink_send,
    sink_recv,
    ctx_send,
    ctx_recv,
    ctx_own,
    go_send,
    go_recv,
    back_send,
    back_recv,
    tok_in,
    place_in,
    place_out,
    tok_send,
    tok_recv,
    place_send,
    place_recv,
    gate_in,
    gate_out,
    gate_send,
    gate_recv,
    part_out,
    part_in,
    red_in,
    part_send,
    part_recv,
    red_send,
    red_recv,
    hidden_part,
):
    me = lax.axis_index("seq")
    my_exp = lax.axis_index("exp")
    upper, pair = me // PAIRS, lax.rem(me, PAIRS)
    me_y, me_z = my_exp // EXP_Z, lax.rem(my_exp, EXP_Z)
    first_of_half = upper * PAIRS
    across = lax.rem(me + PAIRS, N_SEQ)
    sbuf, rbuf = (sbuf_one, sbuf_two), (rbuf_one, rbuf_two)
    ybuf, back = (ybuf_one, ybuf_two), (back_one, back_two)

    early = [
        pltpu.make_async_copy(src, dst, load_sem.at[i])
        for i, (src, dst) in enumerate(
            (
                (old_hbm, held.at[0]),
                (new_hbm, held.at[1]),
                (one_hbm.at[0], routes.at[0]),
                (two_hbm.at[0], routes.at[1]),
                (bias_hbm, table),
            )
        )
    ]
    late = [
        pltpu.make_async_copy(src, dst, load_sem.at[i + 5])
        for i, (src, dst) in enumerate(
            (
                (router_hbm, router),
                (tok_hbm, tok),
                (proj_hbm, proj),
                (gate_hbm.at[0], gate_w),
                (up_hbm.at[0], up_w),
                (down_hbm.at[0], down_w),
            )
        )
    ]
    for copy in early:
        copy.start()

    for batch in range(2):
        low = STRIDE[batch] - 16
        back[batch][:, low:, :] = jnp.zeros((N_EXP, 16, D), BF16)

    @pl.when(upper == 0)
    def _():
        for batch in range(2):
            kb[batch, 0:WIN] = jnp.zeros((WIN, TOK, LANES), BF16)
            vb[batch, 0:WIN] = jnp.zeros((WIN, TOK, LANES), BF16)
            segs[batch, 0:PAIRS] = jnp.full((PAIRS, 1, TOK), -1, I32)
            sink_in[batch] = jnp.zeros((2, 8, LANES), F32)

    barrier = pltpu.get_barrier_semaphore()
    for step in range(1, PAIRS):
        pl.semaphore_signal(
            barrier,
            inc=1,
            device_id={"seq": first_of_half + lax.rem(pair + step, PAIRS)},
            device_id_type=MESH,
        )
    pl.semaphore_signal(barrier, inc=1, device_id={"seq": across}, device_id_type=MESH)
    for step in range(1, N_EXP):
        pl.semaphore_signal(
            barrier,
            inc=1,
            device_id={"exp": lax.rem(my_exp + step, N_EXP)},
            device_id_type=MESH,
        )
    pl.semaphore_wait(barrier, PAIRS + N_EXP - 1)

    def lanes_of(which):
        return pl.ds(pl.multiple_of(which * LANES, LANES), LANES)

    def qkv_parts(batch, target):
        lanes = lanes_of(target)
        return (
            (k_hbm.at[batch, 0, :, lanes], kb.at[batch, pair + WIN]),
            (v_hbm.at[batch, 0, :, lanes], vb.at[batch, pair + WIN]),
            (q_hbm.at[batch, 0, :, lanes], qb.at[batch, pair]),
        )

    def qkv_copies(batch):
        copies = []
        for step in range(1, PAIRS):
            target = lax.rem(pair + step, PAIRS)
            for kind, (src, dst) in enumerate(qkv_parts(batch, target)):
                copies.append(
                    remote(
                        src,
                        dst,
                        qkv_send.at[batch, kind, step],
                        qkv_recv.at[batch, kind, step],
                        seq=first_of_half + target,
                    )
                )
        for kind, (src, dst) in enumerate(qkv_parts(batch, pair)):
            copies.append(pltpu.make_async_copy(src, dst, qkv_own.at[batch, kind]))
        return copies

    qkv = [qkv_copies(batch) for batch in range(2)]
    seg_copies = [
        remote(
            seg_hbm,
            segs.at[:, PAIRS + pair],
            seg_send.at[step],
            seg_recv.at[step],
            seq=first_of_half + lax.rem(pair + step, PAIRS),
        )
        for step in range(1, PAIRS)
    ]
    seg_copies.append(pltpu.make_async_copy(seg_hbm, segs.at[:, PAIRS + pair], seg_own))
    seg_hop = remote(
        segs.at[:, PAIRS : 2 * PAIRS],
        segs.at[:, 0:PAIRS],
        hop_send.at[4],
        hop_recv.at[4],
        seq=across,
    )

    def halo_hop(batch, kind):
        block = (kb, vb)[kind]
        return remote(
            block.at[batch, PAIRS : PAIRS + WIN],
            block.at[batch, 0:WIN],
            hop_send.at[2 * batch + kind],
            hop_recv.at[2 * batch + kind],
            seq=across,
        )

    def sink_hop(batch):
        return remote(
            sink_out.at[batch],
            sink_in.at[batch],
            sink_send.at[batch],
            sink_recv.at[batch],
            seq=across,
        )

    for copy in seg_copies:
        copy.start()
    for copy in qkv[1]:
        copy.start()
    for copy in late:
        copy.start()
    for copy in early:
        copy.wait()

    qi = iota((TOK, TOK), 0)
    kj = iota((TOK, TOK), 1)
    for head in range(2):
        head_row = table[pl.ds(2 * pair + head, 1), :]
        values = [head_row[:, bucket : bucket + 1] for bucket in range(10)]
        rows = slice(head * TOK, (head + 1) * TOK)
        merged = jnp.where(kj <= qi, qi - kj, qi - kj + WIN * TOK)
        bias[0, rows, :] = bias_of_distance(merged, values)
        for block in range(1, WIN):
            bias[block, rows, :] = bias_of_distance(qi - kj + (WIN - block) * TOK, values)
    sink_bias = jnp.where(
        iota((2 * TOK, 1), 0) < TOK,
        table[pl.ds(2 * pair, 1), :][:, SINK_BUCKET : SINK_BUCKET + 1],
        table[pl.ds(2 * pair + 1, 1), :][:, SINK_BUCKET : SINK_BUCKET + 1],
    )

    lane = iota((LANES, LANES), 1)
    row = iota((LANES, LANES), 0)
    tabs[...] = jnp.full((2, LANES), -1, I32)
    tabs[0:1, 0:N_EXP] = held[0]
    tabs[1:2, 0:N_EXP] = held[1]
    steps_y = lax.rem(row // EXP_Z - me_y + 2 * EXP_Y * EXP_Y, EXP_Y)
    steps_z = lax.rem(lax.rem(row, EXP_Z) - me_z + EXP_Z, EXP_Z)
    groups = steps_z + (steps_z // 2) * (1 - 2 * lax.rem(steps_z, 2))
    slot_of_row = (groups * EXP_Y + steps_y).astype(F32)
    holds = turned(tabs[0:1, :]) == lane
    slot_of_expert = jnp.sum(jnp.where(holds, slot_of_row, 0.0), axis=0, keepdims=True)
    new_row = tabs[1:2, :]
    new_col = turned(new_row)
    served = new_col == lane
    serving = jnp.where(served, 1.0, 0.0).astype(BF16)
    slot_two = jnp.sum(jnp.where(served, slot_of_expert, 0.0), axis=1, keepdims=True)
    again = jnp.where((new_col == new_row) & (lane < row), 1.0, 0.0)
    again = jnp.sum(again, axis=1, keepdims=True)
    base_two = jnp.transpose(
        jnp.broadcast_to(slot_two * STRIDE[1] + again * CAP, (LANES, LANES))
    )[0:1, :]
    bases = (slot_of_expert * STRIDE[0], base_two)
    lower = jnp.where(row > lane, 1.0, 0.0).astype(BF16)
    place_cols, place_rows, differences = [], [], []
    for batch in range(2):
        member = [
            jnp.where(turned(routes[batch, c : c + 1, :]) == lane, 1.0, 0.0) for c in range(2)
        ]
        counts = [dot(lower, m.astype(BF16)) for m in member]
        counts[1] = counts[1] + jnp.sum(member[0], axis=0, keepdims=True)
        cols = [
            jnp.sum(m * (c + bases[batch]), axis=1, keepdims=True)
            for m, c in zip(member, counts)
        ]
        place_cols.append(cols)
        place_rows.append(
            [jnp.transpose(jnp.broadcast_to(col, (TOK, TOK)))[0:1, :] for col in cols]
        )
        difference = member[0] - member[1]
        if batch == 1:
            difference = dot(difference.astype(BF16), serving)
        differences.append(difference)
    for c in range(2):
        place_out[c : c + 1, :] = place_rows[1][c]
    place_in[0] = place_out[...]

    def plane(step):
        return me_y * EXP_Z + lax.rem(me_z + step, EXP_Z)

    place_copies = [
        remote(
            place_out,
            place_in.at[group],
            place_send.at[group],
            place_recv.at[group],
            exp=plane(step),
        )
        for group, step in ((1, 1), (2, 3), (3, 2))
    ]
    for copy in place_copies:
        copy.start()
    gate_copies = [
        remote(
            gate_out,
            gate_in.at[group],
            gate_send.at[group],
            gate_recv.at[group],
            exp=plane(step),
        )
        for group, step in ((1, 1), (2, 3), (3, 2))
    ]

    def part_copy(group, half):
        rows = slice(half * (TOK // 2), (half + 1) * (TOK // 2))
        return remote(
            part_out.at[group, rows],
            part_in.at[group, rows],
            part_send.at[group, half],
            part_recv.at[group, half],
            exp=plane((3, 1)[group - 1]),
        )

    def far_copy(half):
        rows = slice(half * (TOK // 2), (half + 1) * (TOK // 2))
        return remote(
            part_out.at[3, rows],
            red_in.at[half],
            red_send.at[half],
            red_recv.at[half],
            exp=plane((3, 1)[half]),
        )

    def token_copy(group, half):
        rows = slice(half * (TOK // 2), (half + 1) * (TOK // 2))
        origin = 1 + half if group == 3 else 0
        step = (1, 3)[half] if group == 3 else (1, 3)[group - 1]
        return remote(
            tok_in.at[origin, rows],
            tok_in.at[group, rows],
            tok_send.at[group, half],
            tok_recv.at[group, half],
            exp=plane(step),
        )

    def relay():
        for half in range(2):
            token_copy(1 + half, half).wait_recv()
            token_copy(3, half).start()

    lane_head = iota((2 * TOK, LANES), 1) // HALF
    row_head = iota((2 * TOK, LANES), 0) // TOK
    own_half = lane_head == row_head
    causal = lax.rem(iota((2 * TOK, TOK), 0), TOK) >= iota((2 * TOK, TOK), 1)

    def twice(value):
        return jnp.concatenate([value, value], axis=0)

    def context_copy(batch, block):
        return remote(
            ctx_out.at[batch, block],
            ctx_in.at[batch, :, lanes_of(pair)],
            ctx_send.at[batch, block],
            ctx_recv.at[batch, pair],
            seq=first_of_half + block,
        )

    def context_own(batch):
        return pltpu.make_async_copy(
            ctx_out.at[batch, pair], ctx_in.at[batch, :, lanes_of(pair)], ctx_own.at[batch]
        )

    def prepare(batch, opening):
        if opening:
            for copy in seg_copies:
                copy.wait()

            @pl.when(upper == 0)
            def _():
                seg_hop.start()

        for copy in qkv[batch]:
            copy.wait()

        @pl.when(upper == 0)
        def _():
            for kind in range(2):
                halo_hop(batch, kind).start()

        if opening:
            for copy in qkv[0]:
                copy.start()

            @pl.when(upper == 1)
            def _():
                seg_hop.wait_recv()

        def columns(block, before):
            line = segs[batch, block]
            segcol[block] = turned(line)
            document = iota((8, TOK), 0)
            return before + jnp.where((line < document) & (line >= 0), 1, 0)

        ahead = lax.fori_loop(0, 2 * PAIRS, columns, jnp.zeros((8, TOK), I32))
        starts = jnp.sum(ahead, axis=1, keepdims=True)

        def sinks(block, sums):
            k_sum, v_sum = sums
            spot = (upper * PAIRS + block) * TOK + iota((8, TOK), 1)
            pick = jnp.where(spot == starts, 1.0, 0.0).astype(BF16)
            return (
                k_sum + dot(pick, kb[batch, block + WIN]),
                v_sum + dot(pick, vb[batch, block + WIN]),
            )

        zero = jnp.zeros((8, LANES), F32)
        k_sink, v_sink = lax.fori_loop(0, PAIRS, sinks, (zero, zero))
        sink_out[batch, 0] = k_sink
        sink_out[batch, 1] = v_sink

        @pl.when(upper == 0)
        def _():
            sink_hop(batch).start()

    def attention(batch, opening):
        @pl.when(upper == 1)
        def _():
            sink_hop(batch).wait_recv()

        sink_rows[0] = sink_out[batch, 0] + sink_in[batch, 0]
        sink_rows[1] = sink_out[batch, 1] + sink_in[batch, 1]

        def attend(block):
            query = twice(qb[batch, block].astype(F32) * 0.125)
            query = jnp.where(own_half, query, 0.0)
            query_rows = query.astype(BF16)
            mine = segcol[block + PAIRS]
            pieces = []
            for near in range(WIN + 1):
                raw = dot_t(query_rows, kb[batch, block + near])
                same = twice(mine == segs[batch, block + near + WIN])
                pieces.append((raw, same))
            merged = jnp.where(causal, pieces[WIN][0], pieces[0][0])
            merged_same = jnp.where(
                causal, pieces[WIN][1].astype(I32), pieces[0][1].astype(I32)
            )
            scores = [jnp.where(merged_same > 0, merged + bias[0], MASKED)]
            for near in range(1, WIN):
                raw, same = pieces[near]
                scores.append(jnp.where(same, raw + bias[near], MASKED))
            chosen_doc = iota((8, LANES), 0) == segs[batch, block + PAIRS][:, 0:1]
            k_row = jnp.sum(jnp.where(chosen_doc, sink_rows[0], 0.0), axis=0, keepdims=True)
            v_row = jnp.sum(jnp.where(chosen_doc, sink_rows[1], 0.0), axis=0, keepdims=True)
            sink_seen = twice(mine[:, 0:1] == segcol[block + WIN][:, 0:1])
            sink = jnp.sum(query * k_row, axis=1, keepdims=True) + sink_bias
            sink = jnp.where(sink_seen, sink, MASKED)
            peak = jnp.maximum(
                jnp.maximum(scores[0], scores[1]), jnp.maximum(scores[2], scores[3])
            )
            peak = jnp.maximum(jnp.max(peak, axis=1, keepdims=True), sink)
            weights = [jnp.exp(score - peak) for score in scores]
            sink_weight = jnp.exp(sink - peak)
            total = (weights[0] + weights[1]) + (weights[2] + weights[3])
            total = jnp.sum(total, axis=1, keepdims=True) + sink_weight
            mixed = sink_weight * v_row
            mixed = mixed + dot(jnp.where(causal, 0.0, weights[0]).astype(BF16), vb[batch, block])
            mixed = mixed + dot(
                jnp.where(causal, weights[0], 0.0).astype(BF16), vb[batch, block + WIN]
            )
            for near in range(1, WIN):
                mixed = mixed + dot(weights[near].astype(BF16), vb[batch, block + near])
            mixed = mixed / total
            ctx_out[batch, block] = jnp.where(
                lane_head[:TOK] == 0, mixed[:TOK], mixed[TOK:]
            ).astype(BF16)

            @pl.when(block == pair)
            def _():
                context_own(batch).start()

            @pl.when(block != pair)
            def _():
                context_copy(batch, block).start()

        def attend_late(turn, carry):
            attend(WIN + lax.rem(pair + turn, WIN))
            return carry

        def attend_early(turn, carry):
            attend(lax.rem(pair + turn, WIN))
            return carry

        lax.fori_loop(0, WIN, attend_late, 0)
        if not opening:
            relay()

        @pl.when(upper == 1)
        def _():
            for kind in range(2):
                halo_hop(batch, kind).wait_recv()

        lax.fori_loop(0, WIN, attend_early, 0)

    def target_of(group, dy, sign):
        y = lax.rem(me_y + EXP_Y + sign * dy, EXP_Y)
        z = lax.rem(me_z + EXP_Z + sign * plane_step(group), EXP_Z)
        return y * EXP_Z + z

    def beside(dy):
        return lax.rem(me_y + dy, EXP_Y) * EXP_Z + me_z

    def dispatch(batch, group, dy):
        slot = group * EXP_Y + dy
        rows = slice(0, SENT[batch])
        return remote(
            sbuf[batch].at[slot, rows],
            rbuf[batch].at[slot, rows],
            go_send.at[batch, slot],
            go_recv.at[batch, slot],
            exp=beside(dy) if batch == 1 else target_of(group, dy, 1),
        )

    def answer(batch, group, dy):
        slot = group * EXP_Y + dy
        rows = slice(0, SENT[batch])
        return remote(
            ybuf[batch].at[slot, rows],
            back[batch].at[slot, rows],
            back_send.at[batch, slot],
            back_recv.at[batch, slot],
            exp=beside(EXP_Y - dy) if batch == 1 else target_of(group, dy, -1),
        )

    gates = [None, None]

    def pick(batch, group, places, source):
        stride = STRIDE[batch]
        spot = (iota((EXP_Y * stride, TOK), 0) + group * EXP_Y * stride).astype(F32)
        hit = (spot == places[0]) | (spot == places[1])
        plan = jnp.where(hit, 1.0, 0.0).astype(BF16)
        for part in range(2):
            cols = slice(part * 512, (part + 1) * 512)
            sbuf[batch][group * EXP_Y : (group + 1) * EXP_Y, :, cols] = (
                dot(plan, source[:, cols]).astype(BF16).reshape(EXP_Y, stride, 512)
            )

    def spread(group):
        if group > 0:
            place_copies[group - 1].wait_recv()
            for half in range(2):
                if (group, half) not in ((1, 0), (2, 1)):
                    token_copy(group, half).wait_recv()
        places = [place_in[group, c : c + 1, :] for c in range(2)]
        pick(1, group, places, tok_in.at[group])
        for dy in range(1, EXP_Y):
            dispatch(1, group, dy).start()
        rbuf[1][group * EXP_Y] = sbuf[1][group * EXP_Y]

    def front(batch, opening):
        for step in range(1, PAIRS):
            source = lax.rem(pair + step, PAIRS)
            remote(
                ctx_out.at[batch, source],
                ctx_in.at[batch, :, lanes_of(source)],
                ctx_send.at[batch, source],
                ctx_recv.at[batch, source],
                seq=first_of_half + source,
            ).wait_recv()
        context_own(batch).wait()
        if opening:
            for copy in late[:3]:
                copy.wait()
        context = ctx_in[batch]
        for part in range(2):
            cols = slice(part * 512, (part + 1) * 512)
            hidden[batch, :, cols] = tok[batch, 0, :, cols].astype(F32) + dot(
                context, proj[:, cols]
            )
        value = hidden[batch]
        scale = lax.rsqrt(jnp.mean(value * value, axis=1, keepdims=True) + EPSILON)
        rows_value = (value * scale).astype(BF16)
        if batch == 1:
            tok_in[0] = rows_value
            for group, half in ((1, 0), (2, 1), (1, 1), (2, 0)):
                token_copy(group, half).start()
            spread(0)
            source = tok_in[0]
        else:
            normed[...] = rows_value
            for group in (3, 1, 2, 0):
                pick(batch, group, place_rows[0], normed)
                for dy in range(EXP_Y):
                    if group + dy > 0:
                        dispatch(batch, group, dy).start()
            rbuf[batch][0] = sbuf[batch][0]
            source = normed[...]
        logits = dot_t(source, router[...])
        picked = jnp.sum(differences[batch][:, :N_EXP] * logits, axis=1, keepdims=True)
        first = jax.nn.sigmoid(picked)
        gates[batch] = (first, 1.0 - first)
        if batch == 1:
            for c in range(2):
                gate_out[c : c + 1, :] = jnp.transpose(
                    jnp.broadcast_to(gates[batch][c], (TOK, TOK))
                )[0:1, :]
            gate_in[0] = gate_out[...]
            for copy in gate_copies:
                copy.start()

    def serve_all(batch, low, high):
        stride = STRIDE[batch]
        count = EXP_Y * stride

        def serve(turn, carry):
            group = lax.rem(turn + 1, EXP_Z)
            for dy in range(EXP_Y):
                if dy == 0 and batch == 1:
                    continue
                if dy == 0:

                    @pl.when(group > 0)
                    def _():
                        dispatch(batch, group, dy).wait_recv()

                else:
                    dispatch(batch, group, dy).wait_recv()
            inputs = rbuf[batch][pl.ds(group * EXP_Y, EXP_Y)].reshape(count, D)
            for low, high in ((0, 512), (512, 1024), (1024, FFW)):
                gate = dot(inputs, gate_w[:, low:high])
                up = dot(inputs, up_w[:, low:high])
                inner = 0.7978845608028654 * (gate + 0.044715 * (gate * gate * gate))
                active[0:count, low:high] = (0.5 * gate * (1.0 + jnp.tanh(inner)) * up).astype(
                    BF16
                )
            for part in range(2):
                cols = slice(part * 512, (part + 1) * 512)
                ybuf[batch][pl.ds(group * EXP_Y, EXP_Y), :, cols] = (
                    dot(active[0:count], down_w[:, cols])
                    .astype(BF16)
                    .reshape(EXP_Y, stride, 512)
                )
            for dy in range(EXP_Y):
                if dy == 0 and batch == 1:
                    back[1][group * EXP_Y] = ybuf[1][group * EXP_Y]
                elif dy == 0:

                    @pl.when(group > 0)
                    def _():
                        answer(batch, group, dy).start()

                else:
                    answer(batch, group, dy).start()
            return carry

        lax.fori_loop(low, high, serve, 0)
        if batch == 0 and high == EXP_Z:
            back[batch][0] = ybuf[batch][0]

    def blend(batch, group, places, weights):
        stride = STRIDE[batch]
        spot = (iota((TOK, EXP_Y * stride), 1) + group * EXP_Y * stride).astype(F32)
        mix = jnp.where(spot == places[0], weights[0], 0.0) + jnp.where(
            spot == places[1], weights[1], 0.0
        )
        coarse = mix.astype(BF16)
        fine = (mix - coarse.astype(F32)).astype(BF16)
        rows = back[batch][group * EXP_Y : (group + 1) * EXP_Y].reshape(EXP_Y * stride, D)
        both = dot(jnp.concatenate([coarse, fine], axis=0), rows)
        return both[:TOK] + both[TOK:]

    def plane_sum(group):
        for dy in range(1, EXP_Y):
            answer(1, group, dy).wait_recv()
        if group == 0:
            return blend(1, 0, place_cols[1], gates[1])
        gate_copies[group - 1].wait_recv()
        places = [turned(place_in[group, c : c + 1, :])[:, 0:1] for c in range(2)]
        weights = [turned(gate_in[group, c : c + 1, :])[:, 0:1] for c in range(2)]
        return blend(1, group, places, weights)

    half_rows = (slice(0, TOK // 2), slice(TOK // 2, TOK))

    def plane_sums():
        part_out[3] = plane_sum(3).astype(BF16)
        for half in range(2):
            far_copy(half).start()
        for group in (1, 2):
            total = plane_sum(group)
            near, far = half_rows[group - 1], half_rows[2 - group]
            part_out[group, far] = total[far].astype(BF16)
            part_copy(group, 2 - group).start()
            hidden_part[group - 1] = total[near]

    def pass_on():
        for group in (1, 2):
            near = half_rows[group - 1]
            far_copy(group - 1).wait_recv()
            total = hidden_part[group - 1] + red_in[group - 1].astype(F32)
            part_out[group, near] = total.astype(BF16)
            part_copy(group, group - 1).start()

    def finish_one():
        result = hidden[0]
        for group in range(EXP_Z):
            for dy in range(EXP_Y):
                if group + dy > 0:
                    answer(0, group, dy).wait_recv()
            result = result + blend(0, group, place_cols[0], gates[0])
        out_ref[0, 0] = result.astype(BF16)

    def finish_two():
        result = hidden[1] + plane_sum(0)
        for group in (1, 2):
            for half in range(2):
                part_copy(group, half).wait_recv()
        result = result + part_in[1].astype(F32) + part_in[2].astype(F32)
        out_ref[1, 0] = result.astype(BF16)

    prepare(1, True)
    attention(1, True)
    prepare(0, False)
    front(1, True)
    attention(0, False)
    spread(1)
    spread(2)
    front(0, False)
    spread(3)
    for copy in late[3:]:
        copy.wait()
    serve_all(1, 0, EXP_Z)
    plane_sums()
    serve_all(0, 0, 2)
    pass_on()
    serve_all(0, 2, EXP_Z)
    finish_one()
    finish_two()

    for batch in range(2):
        for group in range(EXP_Z):
            for dy in range(EXP_Y):
                if dy > 0 or (batch == 0 and group > 0):
                    dispatch(batch, group, dy).wait_send()
                    answer(batch, group, dy).wait_send()
        for step in range(1, PAIRS):
            context_copy(batch, lax.rem(pair + step, PAIRS)).wait_send()

    for group in range(1, EXP_Z):
        place_copies[group - 1].wait_send()
        gate_copies[group - 1].wait_send()
        for half in range(2):
            token_copy(group, half).wait_send()
            if group < 3:
                part_copy(group, half).wait_send()
    for half in range(2):
        far_copy(half).wait_send()

    @pl.when(upper == 0)
    def _():
        seg_hop.wait_send()
        for batch in range(2):
            sink_hop(batch).wait_send()
            for kind in range(2):
                halo_hop(batch, kind).wait_send()


def local(
    tokens,
    queries,
    key_rows,
    value_rows,
    segments,
    bias_table,
    out_proj,
    router,
    gate_weight,
    up_weight,
    down_weight,
    old_table,
    new_table,
    routes_one,
    routes_two,
):
    any_spec = pl.BlockSpec(memory_space=pl.ANY)
    vmem = pltpu.VMEM
    dma = pltpu.SemaphoreType.DMA
    buffers = [vmem((N_EXP, stride, D), BF16) for stride in STRIDE]
    return pl.pallas_call(
        layer_kernel,
        out_shape=jax.ShapeDtypeStruct((2, 1, TOK, D), BF16),
        in_specs=[any_spec] * 15,
        out_specs=pl.BlockSpec(memory_space=pltpu.VMEM),
        scratch_shapes=[
            vmem((N_EXP, NBUCK), F32),
            vmem((2, 2, TOK), I32),
            vmem((2, 1, N_EXP), I32),
            vmem((2, LANES), I32),
            vmem((N_EXP, D), BF16),
            vmem((2, 1, TOK, D), BF16),
            vmem((D, D), BF16),
            vmem((D, FFW), BF16),
            vmem((D, FFW), BF16),
            vmem((FFW, D), BF16),
            vmem((2, N_SEQ, 1, TOK), I32),
            vmem((2, PAIRS, TOK, LANES), BF16),
            vmem((2, PAIRS + WIN, TOK, LANES), BF16),
            vmem((2, PAIRS + WIN, TOK, LANES), BF16),
            vmem((N_SEQ, TOK, TOK), I32),
            vmem((WIN, 2 * TOK, TOK), F32),
            vmem((2, 2, 8, LANES), F32),
            vmem((2, 2, 8, LANES), F32),
            vmem((2, 8, LANES), F32),
            vmem((2, PAIRS, TOK, LANES), BF16),
            vmem((2, TOK, D), BF16),
            vmem((2, TOK, D), F32),
            vmem((TOK, D), BF16),
            *buffers,
            *buffers,
            *buffers,
            *buffers,
            vmem((EXP_Y * STRIDE[1], FFW), BF16),
            dma((11,)),
            dma((2, 3, PAIRS)),
            dma((2, 3, PAIRS)),
            dma((2, 3)),
            dma((PAIRS,)),
            dma((PAIRS,)),
            dma(()),
            dma((5,)),
            dma((5,)),
            dma((2,)),
            dma((2,)),
            dma((2, PAIRS)),
            dma((2, PAIRS)),
            dma((2,)),
            dma((2, N_EXP)),
            dma((2, N_EXP)),
            dma((2, N_EXP)),
            dma((2, N_EXP)),
            vmem((EXP_Z, TOK, D), BF16),
            vmem((EXP_Z, 2, TOK), F32),
            vmem((2, TOK), F32),
            dma((EXP_Z, 2)),
            dma((EXP_Z, 2)),
            dma((EXP_Z,)),
            dma((EXP_Z,)),
            vmem((EXP_Z, 2, TOK), F32),
            vmem((2, TOK), F32),
            dma((EXP_Z,)),
            dma((EXP_Z,)),
            vmem((EXP_Z, TOK, D), BF16),
            vmem((EXP_Z, TOK, D), BF16),
            vmem((2, TOK // 2, D), BF16),
            dma((EXP_Z, 2)),
            dma((EXP_Z, 2)),
            dma((2,)),
            dma((2,)),
            vmem((2, TOK // 2, D), F32),
        ],
        compiler_params=pltpu.CompilerParams(
            collective_id=0, has_side_effects=True, vmem_limit_bytes=56 << 20
        ),
        name="layer",
    )(
        bias_table,
        segments,
        queries,
        key_rows,
        value_rows,
        tokens,
        out_proj,
        router.T,
        jnp.swapaxes(routes_one, 1, 2),
        jnp.swapaxes(routes_two, 1, 2),
        old_table[None],
        new_table[None],
        gate_weight,
        up_weight,
        down_weight,
    )


def solution(mesh):
    placed = (
        P(None, "exp", "seq", None),
        P(None, "exp", "seq", None),
        P(None, "exp", "seq", None),
        P(None, "exp", "seq", None),
        P(None, "exp", "seq"),
        P(),
        P(),
        P(),
        P("exp", None, None),
        P("exp", None, None),
        P("exp", None, None),
        P(),
        P(),
        P("exp", "seq", None),
        P("exp", "seq", None),
    )
    return jax.shard_map(
        local, mesh=mesh, in_specs=placed, out_specs=P(None, "exp", "seq", None), check_vma=False
    )
```

```python
import jax
import jax.numpy as jnp
from jax import lax
from jax.experimental import pallas as pl
from jax.experimental.pallas import tpu as pltpu
from jax.sharding import PartitionSpec as P

MESH = pl.DeviceIdType.MESH
BF16 = jnp.bfloat16
F32 = jnp.float32
I32 = jnp.int32

N_SEQ = 16
N_EXP = 16
EXP_Y = 4
EXP_Z = 4
TOK = 128
D = 1024
FFW = 1408
NBUCK = 32
WIN = 4
PAIRS = 8
LANES = 128
HALF = 64
CAP = 20
STRIDE = (32, 48)
SENT = (24, 40)
SINK_BUCKET = 31

EPSILON = 1e-06
MASKED = -1e30


def iota(shape, dim):
    return lax.broadcasted_iota(I32, shape, dim)


def dot(a, b):
    return jnp.dot(a, b, preferred_element_type=F32)


def dot_t(a, b):
    return lax.dot_general(a, b, (((1,), (1,)), ((), ())), preferred_element_type=F32)


def turned(row):
    return jnp.transpose(jnp.broadcast_to(row, (LANES, LANES)))


def remote(src, dst, send, recv, **device):
    return pltpu.make_async_remote_copy(
        src_ref=src,
        dst_ref=dst,
        send_sem=send,
        recv_sem=recv,
        device_id=device,
        device_id_type=MESH,
    )


def bias_of_distance(distance, values):
    result = jnp.broadcast_to(values[0], distance.shape)
    for bucket in range(1, 10):
        result = jnp.where(distance >= (1 << (bucket - 1)), values[bucket], result)
    return result


def plane_step(group):
    return group + (group // 2) * (1 - 2 * lax.rem(group, 2))


def layer_kernel(
    bias_hbm,
    seg_hbm,
    q_hbm,
    k_hbm,
    v_hbm,
    tok_hbm,
    proj_hbm,
    router_hbm,
    one_hbm,
    two_hbm,
    old_hbm,
    new_hbm,
    gate_hbm,
    up_hbm,
    down_hbm,
    out_ref,
    table,
    routes,
    held,
    tabs,
    router,
    tok,
    proj,
    gate_w,
    up_w,
    down_w,
    segs,
    qb,
    kb,
    vb,
    segcol,
    bias,
    sink_out,
    sink_in,
    sink_rows,
    ctx_out,
    ctx_in,
    hidden,
    normed,
    sbuf_one,
    sbuf_two,
    rbuf_one,
    rbuf_two,
    ybuf_one,
    ybuf_two,
    back_one,
    back_two,
    active,
    load_sem,
    qkv_send,
    qkv_recv,
    qkv_own,
    seg_send,
    seg_recv,
    seg_own,
    hop_send,
    hop_recv,
    sink_send,
    sink_recv,
    ctx_send,
    ctx_recv,
    ctx_own,
    go_send,
    go_recv,
    back_send,
    back_recv,
    tok_in,
    place_in,
    place_out,
    tok_send,
    tok_recv,
    place_send,
    place_recv,
    gate_in,
    gate_out,
    gate_send,
    gate_recv,
    part_out,
    part_in,
    red_in,
    part_send,
    part_recv,
    red_send,
    red_recv,
    hidden_part,
):
    me = lax.axis_index("seq")
    my_exp = lax.axis_index("exp")
    upper, pair = me // PAIRS, lax.rem(me, PAIRS)
    me_y, me_z = my_exp // EXP_Z, lax.rem(my_exp, EXP_Z)
    first_of_half = upper * PAIRS
    across = lax.rem(me + PAIRS, N_SEQ)
    sbuf, rbuf = (sbuf_one, sbuf_two), (rbuf_one, rbuf_two)
    ybuf, back = (ybuf_one, ybuf_two), (back_one, back_two)

    early = [
        pltpu.make_async_copy(src, dst, load_sem.at[i])
        for i, (src, dst) in enumerate(
            (
                (old_hbm, held.at[0]),
                (new_hbm, held.at[1]),
                (one_hbm.at[0], routes.at[0]),
                (two_hbm.at[0], routes.at[1]),
                (bias_hbm, table),
            )
        )
    ]
    late = [
        pltpu.make_async_copy(src, dst, load_sem.at[i + 5])
        for i, (src, dst) in enumerate(
            (
                (router_hbm, router),
                (tok_hbm, tok),
                (proj_hbm, proj),
                (gate_hbm.at[0], gate_w),
                (up_hbm.at[0], up_w),
                (down_hbm.at[0], down_w),
            )
        )
    ]
    for copy in early:
        copy.start()

    for batch in range(2):
        low = STRIDE[batch] - 16
        back[batch][:, low:, :] = jnp.zeros((N_EXP, 16, D), BF16)

    @pl.when(upper == 0)
    def _():
        for batch in range(2):
            kb[batch, 0:WIN] = jnp.zeros((WIN, TOK, LANES), BF16)
            vb[batch, 0:WIN] = jnp.zeros((WIN, TOK, LANES), BF16)
            segs[batch, 0:PAIRS] = jnp.full((PAIRS, 1, TOK), -1, I32)
            sink_in[batch] = jnp.zeros((2, 8, LANES), F32)

    barrier = pltpu.get_barrier_semaphore()
    for step in range(1, PAIRS):
        pl.semaphore_signal(
            barrier,
            inc=1,
            device_id={"seq": first_of_half + lax.rem(pair + step, PAIRS)},
            device_id_type=MESH,
        )
    pl.semaphore_signal(barrier, inc=1, device_id={"seq": across}, device_id_type=MESH)
    for step in range(1, N_EXP):
        pl.semaphore_signal(
            barrier,
            inc=1,
            device_id={"exp": lax.rem(my_exp + step, N_EXP)},
            device_id_type=MESH,
        )
    pl.semaphore_wait(barrier, PAIRS + N_EXP - 1)

    def lanes_of(which):
        return pl.ds(pl.multiple_of(which * LANES, LANES), LANES)

    def qkv_parts(batch, target):
        lanes = lanes_of(target)
        return (
            (k_hbm.at[batch, 0, :, lanes], kb.at[batch, pair + WIN]),
            (v_hbm.at[batch, 0, :, lanes], vb.at[batch, pair + WIN]),
            (q_hbm.at[batch, 0, :, lanes], qb.at[batch, pair]),
        )

    def qkv_copies(batch):
        copies = []
        for step in range(1, PAIRS):
            target = lax.rem(pair + step, PAIRS)
            for kind, (src, dst) in enumerate(qkv_parts(batch, target)):
                copies.append(
                    remote(
                        src,
                        dst,
                        qkv_send.at[batch, kind, step],
                        qkv_recv.at[batch, kind, step],
                        seq=first_of_half + target,
                    )
                )
        for kind, (src, dst) in enumerate(qkv_parts(batch, pair)):
            copies.append(pltpu.make_async_copy(src, dst, qkv_own.at[batch, kind]))
        return copies

    qkv = [qkv_copies(batch) for batch in range(2)]
    seg_copies = [
        remote(
            seg_hbm,
            segs.at[:, PAIRS + pair],
            seg_send.at[step],
            seg_recv.at[step],
            seq=first_of_half + lax.rem(pair + step, PAIRS),
        )
        for step in range(1, PAIRS)
    ]
    seg_copies.append(pltpu.make_async_copy(seg_hbm, segs.at[:, PAIRS + pair], seg_own))
    seg_hop = remote(
        segs.at[:, PAIRS : 2 * PAIRS],
        segs.at[:, 0:PAIRS],
        hop_send.at[4],
        hop_recv.at[4],
        seq=across,
    )

    def halo_hop(batch, kind):
        block = (kb, vb)[kind]
        return remote(
            block.at[batch, PAIRS : PAIRS + WIN],
            block.at[batch, 0:WIN],
            hop_send.at[2 * batch + kind],
            hop_recv.at[2 * batch + kind],
            seq=across,
        )

    def sink_hop(batch):
        return remote(
            sink_out.at[batch],
            sink_in.at[batch],
            sink_send.at[batch],
            sink_recv.at[batch],
            seq=across,
        )

    for copy in seg_copies:
        copy.start()
    for copy in qkv[1]:
        copy.start()
    for copy in late:
        copy.start()
    for copy in early:
        copy.wait()

    qi = iota((TOK, TOK), 0)
    kj = iota((TOK, TOK), 1)
    for head in range(2):
        head_row = table[pl.ds(2 * pair + head, 1), :]
        values = [head_row[:, bucket : bucket + 1] for bucket in range(10)]
        rows = slice(head * TOK, (head + 1) * TOK)
        merged = jnp.where(kj <= qi, qi - kj, qi - kj + WIN * TOK)
        bias[0, rows, :] = bias_of_distance(merged, values)
        for block in range(1, WIN):
            bias[block, rows, :] = bias_of_distance(qi - kj + (WIN - block) * TOK, values)
    sink_bias = jnp.where(
        iota((2 * TOK, 1), 0) < TOK,
        table[pl.ds(2 * pair, 1), :][:, SINK_BUCKET : SINK_BUCKET + 1],
        table[pl.ds(2 * pair + 1, 1), :][:, SINK_BUCKET : SINK_BUCKET + 1],
    )

    lane = iota((LANES, LANES), 1)
    row = iota((LANES, LANES), 0)
    tabs[...] = jnp.full((2, LANES), -1, I32)
    tabs[0:1, 0:N_EXP] = held[0]
    tabs[1:2, 0:N_EXP] = held[1]
    steps_y = lax.rem(row // EXP_Z - me_y + 2 * EXP_Y * EXP_Y, EXP_Y)
    steps_z = lax.rem(lax.rem(row, EXP_Z) - me_z + EXP_Z, EXP_Z)
    groups = steps_z + (steps_z // 2) * (1 - 2 * lax.rem(steps_z, 2))
    slot_of_row = (groups * EXP_Y + steps_y).astype(F32)
    holds = turned(tabs[0:1, :]) == lane
    slot_of_expert = jnp.sum(jnp.where(holds, slot_of_row, 0.0), axis=0, keepdims=True)
    new_row = tabs[1:2, :]
    new_col = turned(new_row)
    served = new_col == lane
    serving = jnp.where(served, 1.0, 0.0).astype(BF16)
    slot_two = jnp.sum(jnp.where(served, slot_of_expert, 0.0), axis=1, keepdims=True)
    again = jnp.where((new_col == new_row) & (lane < row), 1.0, 0.0)
    again = jnp.sum(again, axis=1, keepdims=True)
    base_two = jnp.transpose(
        jnp.broadcast_to(slot_two * STRIDE[1] + again * CAP, (LANES, LANES))
    )[0:1, :]
    bases = (slot_of_expert * STRIDE[0], base_two)
    lower = jnp.where(row > lane, 1.0, 0.0).astype(BF16)
    place_cols, place_rows, differences = [], [], []
    for batch in range(2):
        member = [
            jnp.where(turned(routes[batch, c : c + 1, :]) == lane, 1.0, 0.0) for c in range(2)
        ]
        counts = [dot(lower, m.astype(BF16)) for m in member]
        counts[1] = counts[1] + jnp.sum(member[0], axis=0, keepdims=True)
        cols = [
            jnp.sum(m * (c + bases[batch]), axis=1, keepdims=True)
            for m, c in zip(member, counts)
        ]
        place_cols.append(cols)
        place_rows.append(
            [jnp.transpose(jnp.broadcast_to(col, (TOK, TOK)))[0:1, :] for col in cols]
        )
        difference = member[0] - member[1]
        if batch == 1:
            difference = dot(difference.astype(BF16), serving)
        differences.append(difference)
    for c in range(2):
        place_out[c : c + 1, :] = place_rows[1][c]
    place_in[0] = place_out[...]

    def plane(step):
        return me_y * EXP_Z + lax.rem(me_z + step, EXP_Z)

    place_copies = [
        remote(
            place_out,
            place_in.at[group],
            place_send.at[group],
            place_recv.at[group],
            exp=plane(step),
        )
        for group, step in ((1, 1), (2, 3), (3, 2))
    ]
    for copy in place_copies:
        copy.start()
    gate_copies = [
        remote(
            gate_out,
            gate_in.at[group],
            gate_send.at[group],
            gate_recv.at[group],
            exp=plane(step),
        )
        for group, step in ((1, 1), (2, 3), (3, 2))
    ]

    def part_copy(group, half):
        rows = slice(half * (TOK // 2), (half + 1) * (TOK // 2))
        return remote(
            part_out.at[group, rows],
            part_in.at[group, rows],
            part_send.at[group, half],
            part_recv.at[group, half],
            exp=plane((3, 1)[group - 1]),
        )

    def far_copy(half):
        rows = slice(half * (TOK // 2), (half + 1) * (TOK // 2))
        return remote(
            part_out.at[3, rows],
            red_in.at[half],
            red_send.at[half],
            red_recv.at[half],
            exp=plane((3, 1)[half]),
        )

    def token_copy(group, half):
        rows = slice(half * (TOK // 2), (half + 1) * (TOK // 2))
        origin = 1 + half if group == 3 else 0
        step = (1, 3)[half] if group == 3 else (1, 3)[group - 1]
        return remote(
            tok_in.at[origin, rows],
            tok_in.at[group, rows],
            tok_send.at[group, half],
            tok_recv.at[group, half],
            exp=plane(step),
        )

    def relay():
        for half in range(2):
            token_copy(1 + half, half).wait_recv()
            token_copy(3, half).start()

    lane_head = iota((2 * TOK, LANES), 1) // HALF
    row_head = iota((2 * TOK, LANES), 0) // TOK
    own_half = lane_head == row_head
    causal = lax.rem(iota((2 * TOK, TOK), 0), TOK) >= iota((2 * TOK, TOK), 1)

    def twice(value):
        return jnp.concatenate([value, value], axis=0)

    def context_copy(batch, block):
        return remote(
            ctx_out.at[batch, block],
            ctx_in.at[batch, :, lanes_of(pair)],
            ctx_send.at[batch, block],
            ctx_recv.at[batch, pair],
            seq=first_of_half + block,
        )

    def context_own(batch):
        return pltpu.make_async_copy(
            ctx_out.at[batch, pair], ctx_in.at[batch, :, lanes_of(pair)], ctx_own.at[batch]
        )

    def columns(batch):
        def column(block, before):
            line = segs[batch, block]
            segcol[batch, block] = turned(line)
            document = iota((8, TOK), 0)
            return before + jnp.where((line < document) & (line >= 0), 1, 0)

        ahead = lax.fori_loop(
            0, 2 * PAIRS, column, jnp.zeros((8, TOK), I32), unroll=4
        )
        return jnp.sum(ahead, axis=1, keepdims=True)

    for copy in seg_copies:
        copy.wait()

    @pl.when(upper == 0)
    def _():
        seg_hop.start()

    @pl.when(upper == 1)
    def _():
        seg_hop.wait_recv()

    starts = [columns(batch) for batch in range(2)]

    def prepare(batch, opening):
        for copy in qkv[batch]:
            copy.wait()

        @pl.when(upper == 0)
        def _():
            for kind in range(2):
                halo_hop(batch, kind).start()

        if opening:
            for copy in qkv[0]:
                copy.start()

        def sinks(block, sums):
            k_sum, v_sum = sums
            spot = (upper * PAIRS + block) * TOK + iota((8, TOK), 1)
            pick = jnp.where(spot == starts[batch], 1.0, 0.0).astype(BF16)
            return (
                k_sum + dot(pick, kb[batch, block + WIN]),
                v_sum + dot(pick, vb[batch, block + WIN]),
            )

        zero = jnp.zeros((8, LANES), F32)
        k_sink, v_sink = lax.fori_loop(0, PAIRS, sinks, (zero, zero), unroll=True)
        sink_out[batch, 0] = k_sink
        sink_out[batch, 1] = v_sink

        @pl.when(upper == 0)
        def _():
            sink_hop(batch).start()

    def attention(batch, opening):
        @pl.when(upper == 1)
        def _():
            sink_hop(batch).wait_recv()

        sink_rows[0] = sink_out[batch, 0] + sink_in[batch, 0]
        sink_rows[1] = sink_out[batch, 1] + sink_in[batch, 1]

        def attend(block):
            query = twice(qb[batch, block].astype(F32) * 0.125)
            query = jnp.where(own_half, query, 0.0)
            query_rows = query.astype(BF16)
            mine = segcol[batch, block + PAIRS]
            pieces = []
            for near in range(WIN + 1):
                raw = dot_t(query_rows, kb[batch, block + near])
                same = twice(mine == segs[batch, block + near + WIN])
                pieces.append((raw, same))
            merged = jnp.where(causal, pieces[WIN][0], pieces[0][0])
            merged_same = jnp.where(
                causal, pieces[WIN][1].astype(I32), pieces[0][1].astype(I32)
            )
            scores = [jnp.where(merged_same > 0, merged + bias[0], MASKED)]
            for near in range(1, WIN):
                raw, same = pieces[near]
                scores.append(jnp.where(same, raw + bias[near], MASKED))
            chosen_doc = iota((8, LANES), 0) == segs[batch, block + PAIRS][:, 0:1]
            k_row = jnp.sum(jnp.where(chosen_doc, sink_rows[0], 0.0), axis=0, keepdims=True)
            v_row = jnp.sum(jnp.where(chosen_doc, sink_rows[1], 0.0), axis=0, keepdims=True)
            sink_seen = twice(mine[:, 0:1] == segcol[batch, block + WIN][:, 0:1])
            sink = jnp.sum(query * k_row, axis=1, keepdims=True) + sink_bias
            sink = jnp.where(sink_seen, sink, MASKED)
            peak = jnp.maximum(
                jnp.maximum(scores[0], scores[1]), jnp.maximum(scores[2], scores[3])
            )
            peak = jnp.maximum(jnp.max(peak, axis=1, keepdims=True), sink)
            weights = [jnp.exp(score - peak) for score in scores]
            sink_weight = jnp.exp(sink - peak)
            total = (weights[0] + weights[1]) + (weights[2] + weights[3])
            total = jnp.sum(total, axis=1, keepdims=True) + sink_weight
            mixed = sink_weight * v_row
            mixed = mixed + dot(jnp.where(causal, 0.0, weights[0]).astype(BF16), vb[batch, block])
            mixed = mixed + dot(
                jnp.where(causal, weights[0], 0.0).astype(BF16), vb[batch, block + WIN]
            )
            for near in range(1, WIN):
                mixed = mixed + dot(weights[near].astype(BF16), vb[batch, block + near])
            mixed = mixed / total
            ctx_out[batch, block] = jnp.where(
                lane_head[:TOK] == 0, mixed[:TOK], mixed[TOK:]
            ).astype(BF16)

            @pl.when(block == pair)
            def _():
                context_own(batch).start()

            @pl.when(block != pair)
            def _():
                context_copy(batch, block).start()

        def attend_late(turn, carry):
            attend(WIN + lax.rem(pair + turn, WIN))
            return carry

        def attend_early(turn, carry):
            attend(lax.rem(pair + turn, WIN))
            return carry

        lax.fori_loop(0, WIN, attend_late, 0, unroll=2)
        if not opening:
            relay()

        @pl.when(upper == 1)
        def _():
            for kind in range(2):
                halo_hop(batch, kind).wait_recv()

        lax.fori_loop(0, WIN, attend_early, 0, unroll=2)

    def target_of(group, dy, sign):
        y = lax.rem(me_y + EXP_Y + sign * dy, EXP_Y)
        z = lax.rem(me_z + EXP_Z + sign * plane_step(group), EXP_Z)
        return y * EXP_Z + z

    def beside(dy):
        return lax.rem(me_y + dy, EXP_Y) * EXP_Z + me_z

    def dispatch(batch, group, dy):
        slot = group * EXP_Y + dy
        rows = slice(0, SENT[batch])
        return remote(
            sbuf[batch].at[slot, rows],
            rbuf[batch].at[slot, rows],
            go_send.at[batch, slot],
            go_recv.at[batch, slot],
            exp=beside(dy) if batch == 1 else target_of(group, dy, 1),
        )

    def answer(batch, group, dy):
        slot = group * EXP_Y + dy
        rows = slice(0, SENT[batch])
        return remote(
            ybuf[batch].at[slot, rows],
            back[batch].at[slot, rows],
            back_send.at[batch, slot],
            back_recv.at[batch, slot],
            exp=beside(EXP_Y - dy) if batch == 1 else target_of(group, dy, -1),
        )

    gates = [None, None]

    def pick(batch, group, places, source):
        stride = STRIDE[batch]
        spot = (iota((EXP_Y * stride, TOK), 0) + group * EXP_Y * stride).astype(F32)
        hit = (spot == places[0]) | (spot == places[1])
        plan = jnp.where(hit, 1.0, 0.0).astype(BF16)
        for part in range(2):
            cols = slice(part * 512, (part + 1) * 512)
            sbuf[batch][group * EXP_Y : (group + 1) * EXP_Y, :, cols] = (
                dot(plan, source[:, cols]).astype(BF16).reshape(EXP_Y, stride, 512)
            )

    def spread(group):
        if group > 0:
            place_copies[group - 1].wait_recv()
            for half in range(2):
                if (group, half) not in ((1, 0), (2, 1)):
                    token_copy(group, half).wait_recv()
        places = [place_in[group, c : c + 1, :] for c in range(2)]
        pick(1, group, places, tok_in.at[group])
        for dy in range(1, EXP_Y):
            dispatch(1, group, dy).start()
        rbuf[1][group * EXP_Y] = sbuf[1][group * EXP_Y]

    def front(batch, opening):
        for step in range(1, PAIRS):
            source = lax.rem(pair + step, PAIRS)
            remote(
                ctx_out.at[batch, source],
                ctx_in.at[batch, :, lanes_of(source)],
                ctx_send.at[batch, source],
                ctx_recv.at[batch, source],
                seq=first_of_half + source,
            ).wait_recv()
        context_own(batch).wait()
        if opening:
            for copy in late[:3]:
                copy.wait()
        context = ctx_in[batch]
        for part in range(2):
            cols = slice(part * 512, (part + 1) * 512)
            hidden[batch, :, cols] = tok[batch, 0, :, cols].astype(F32) + dot(
                context, proj[:, cols]
            )
        value = hidden[batch]
        scale = lax.rsqrt(jnp.mean(value * value, axis=1, keepdims=True) + EPSILON)
        rows_value = (value * scale).astype(BF16)
        if batch == 1:
            tok_in[0] = rows_value
            for group, half in ((1, 0), (2, 1), (1, 1), (2, 0)):
                token_copy(group, half).start()
            spread(0)
            source = tok_in[0]
        else:
            normed[...] = rows_value
            for group in (3, 1, 2, 0):
                pick(batch, group, place_rows[0], normed)
                for dy in range(EXP_Y):
                    if group + dy > 0:
                        dispatch(batch, group, dy).start()
            rbuf[batch][0] = sbuf[batch][0]
            source = normed[...]
        logits = dot_t(source, router[...])
        picked = jnp.sum(differences[batch][:, :N_EXP] * logits, axis=1, keepdims=True)
        first = jax.nn.sigmoid(picked)
        gates[batch] = (first, 1.0 - first)
        if batch == 1:
            for c in range(2):
                gate_out[c : c + 1, :] = jnp.transpose(
                    jnp.broadcast_to(gates[batch][c], (TOK, TOK))
                )[0:1, :]
            gate_in[0] = gate_out[...]
            for copy in gate_copies:
                copy.start()

    def serve_all(batch, first, last):
        sent = SENT[batch]
        slots = 2 * EXP_Y
        count = slots * sent

        def serve(turn, carry):
            pair_of_groups = 1 - turn
            spots = pl.ds(pair_of_groups * slots, slots)
            for which in range(slots):
                group, dy = 2 * pair_of_groups + which // EXP_Y, which % EXP_Y
                if dy > 0:
                    dispatch(batch, group, dy).wait_recv()
                elif batch == 0:

                    @pl.when(group > 0)
                    def _():
                        dispatch(batch, group, dy).wait_recv()

            inputs = rbuf[batch][spots, 0:sent, :].astype(F32)
            inputs = inputs.reshape(count, D).astype(BF16)
            for low, high in ((0, 512), (512, 1024), (1024, FFW)):
                gate = dot(inputs, gate_w[:, low:high])
                up = dot(inputs, up_w[:, low:high])
                inner = 0.7978845608028654 * (gate + 0.044715 * (gate * gate * gate))
                active[0:count, low:high] = (0.5 * gate * (1.0 + jnp.tanh(inner)) * up).astype(
                    BF16
                )
            for part in range(2):
                cols = slice(part * 512, (part + 1) * 512)
                ybuf[batch][spots, 0:sent, cols] = (
                    dot(active[0:count], down_w[:, cols]).reshape(slots, sent, 512).astype(BF16)
                )
            for which in range(slots):
                group, dy = 2 * pair_of_groups + which // EXP_Y, which % EXP_Y
                if dy > 0:
                    answer(batch, group, dy).start()
                elif batch == 1:
                    back[1][group * EXP_Y, 0:sent] = ybuf[1][group * EXP_Y, 0:sent]
                else:

                    @pl.when(group > 0)
                    def _():
                        answer(batch, group, dy).start()

            return carry

        lax.fori_loop(first, last, serve, 0)
        if batch == 0 and last == 2:
            back[batch][0, 0:sent] = ybuf[batch][0, 0:sent]

    def blend(batch, group, places, weights):
        stride = STRIDE[batch]
        spot = (iota((TOK, EXP_Y * stride), 1) + group * EXP_Y * stride).astype(F32)
        mix = jnp.where(spot == places[0], weights[0], 0.0) + jnp.where(
            spot == places[1], weights[1], 0.0
        )
        coarse = mix.astype(BF16)
        fine = (mix - coarse.astype(F32)).astype(BF16)
        rows = back[batch][group * EXP_Y : (group + 1) * EXP_Y].reshape(EXP_Y * stride, D)
        both = dot(jnp.concatenate([coarse, fine], axis=0), rows)
        return both[:TOK] + both[TOK:]

    def plane_sum(group):
        for dy in range(1, EXP_Y):
            answer(1, group, dy).wait_recv()
        if group == 0:
            return blend(1, 0, place_cols[1], gates[1])
        gate_copies[group - 1].wait_recv()
        places = [turned(place_in[group, c : c + 1, :])[:, 0:1] for c in range(2)]
        weights = [turned(gate_in[group, c : c + 1, :])[:, 0:1] for c in range(2)]
        return blend(1, group, places, weights)

    half_rows = (slice(0, TOK // 2), slice(TOK // 2, TOK))

    def plane_sums():
        part_out[3] = plane_sum(3).astype(BF16)
        for half in range(2):
            far_copy(half).start()
        for group in (1, 2):
            total = plane_sum(group)
            near, far = half_rows[group - 1], half_rows[2 - group]
            part_out[group, far] = total[far].astype(BF16)
            part_copy(group, 2 - group).start()
            hidden_part[group - 1] = total[near]

    def pass_on():
        for group in (1, 2):
            near = half_rows[group - 1]
            far_copy(group - 1).wait_recv()
            total = hidden_part[group - 1] + red_in[group - 1].astype(F32)
            part_out[group, near] = total.astype(BF16)
            part_copy(group, group - 1).start()

    def finish_one():
        result = hidden[0]
        for group in range(EXP_Z):
            for dy in range(EXP_Y):
                if group + dy > 0:
                    answer(0, group, dy).wait_recv()
            result = result + blend(0, group, place_cols[0], gates[0])
        out_ref[0, 0] = result.astype(BF16)

    def finish_two():
        result = hidden[1] + plane_sum(0)
        for group in (1, 2):
            for half in range(2):
                part_copy(group, half).wait_recv()
        result = result + part_in[1].astype(F32) + part_in[2].astype(F32)
        out_ref[1, 0] = result.astype(BF16)

    prepare(1, True)
    attention(1, True)
    prepare(0, False)
    front(1, True)
    attention(0, False)
    front(0, False)
    spread(1)
    spread(2)
    spread(3)
    for copy in late[3:]:
        copy.wait()
    serve_all(1, 0, 2)
    plane_sums()
    serve_all(0, 0, 1)
    pass_on()
    serve_all(0, 1, 2)
    finish_one()
    finish_two()

    for batch in range(2):
        for group in range(EXP_Z):
            for dy in range(EXP_Y):
                if dy > 0 or (batch == 0 and group > 0):
                    dispatch(batch, group, dy).wait_send()
                    answer(batch, group, dy).wait_send()
        for step in range(1, PAIRS):
            context_copy(batch, lax.rem(pair + step, PAIRS)).wait_send()

    for group in range(1, EXP_Z):
        place_copies[group - 1].wait_send()
        gate_copies[group - 1].wait_send()
        for half in range(2):
            token_copy(group, half).wait_send()
            if group < 3:
                part_copy(group, half).wait_send()
    for half in range(2):
        far_copy(half).wait_send()

    @pl.when(upper == 0)
    def _():
        seg_hop.wait_send()
        for batch in range(2):
            sink_hop(batch).wait_send()
            for kind in range(2):
                halo_hop(batch, kind).wait_send()


def local(
    tokens,
    queries,
    key_rows,
    value_rows,
    segments,
    bias_table,
    out_proj,
    router,
    gate_weight,
    up_weight,
    down_weight,
    old_table,
    new_table,
    routes_one,
    routes_two,
):
    any_spec = pl.BlockSpec(memory_space=pl.ANY)
    vmem = pltpu.VMEM
    dma = pltpu.SemaphoreType.DMA
    buffers = [vmem((N_EXP, stride, D), BF16) for stride in STRIDE]
    return pl.pallas_call(
        layer_kernel,
        out_shape=jax.ShapeDtypeStruct((2, 1, TOK, D), BF16),
        in_specs=[any_spec] * 15,
        out_specs=pl.BlockSpec(memory_space=pltpu.VMEM),
        scratch_shapes=[
            vmem((N_EXP, NBUCK), F32),
            vmem((2, 2, TOK), I32),
            vmem((2, 1, N_EXP), I32),
            vmem((2, LANES), I32),
            vmem((N_EXP, D), BF16),
            vmem((2, 1, TOK, D), BF16),
            vmem((D, D), BF16),
            vmem((D, FFW), BF16),
            vmem((D, FFW), BF16),
            vmem((FFW, D), BF16),
            vmem((2, N_SEQ, 1, TOK), I32),
            vmem((2, PAIRS, TOK, LANES), BF16),
            vmem((2, PAIRS + WIN, TOK, LANES), BF16),
            vmem((2, PAIRS + WIN, TOK, LANES), BF16),
            vmem((2, N_SEQ, TOK, TOK), I32),
            vmem((WIN, 2 * TOK, TOK), F32),
            vmem((2, 2, 8, LANES), F32),
            vmem((2, 2, 8, LANES), F32),
            vmem((2, 8, LANES), F32),
            vmem((2, PAIRS, TOK, LANES), BF16),
            vmem((2, TOK, D), BF16),
            vmem((2, TOK, D), F32),
            vmem((TOK, D), BF16),
            *buffers,
            *buffers,
            *buffers,
            *buffers,
            vmem((2 * EXP_Y * SENT[1], FFW), BF16),
            dma((11,)),
            dma((2, 3, PAIRS)),
            dma((2, 3, PAIRS)),
            dma((2, 3)),
            dma((PAIRS,)),
            dma((PAIRS,)),
            dma(()),
            dma((5,)),
            dma((5,)),
            dma((2,)),
            dma((2,)),
            dma((2, PAIRS)),
            dma((2, PAIRS)),
            dma((2,)),
            dma((2, N_EXP)),
            dma((2, N_EXP)),
            dma((2, N_EXP)),
            dma((2, N_EXP)),
            vmem((EXP_Z, TOK, D), BF16),
            vmem((EXP_Z, 2, TOK), F32),
            vmem((2, TOK), F32),
            dma((EXP_Z, 2)),
            dma((EXP_Z, 2)),
            dma((EXP_Z,)),
            dma((EXP_Z,)),
            vmem((EXP_Z, 2, TOK), F32),
            vmem((2, TOK), F32),
            dma((EXP_Z,)),
            dma((EXP_Z,)),
            vmem((EXP_Z, TOK, D), BF16),
            vmem((EXP_Z, TOK, D), BF16),
            vmem((2, TOK // 2, D), BF16),
            dma((EXP_Z, 2)),
            dma((EXP_Z, 2)),
            dma((2,)),
            dma((2,)),
            vmem((2, TOK // 2, D), F32),
        ],
        compiler_params=pltpu.CompilerParams(
            collective_id=0, has_side_effects=True, vmem_limit_bytes=56 << 20
        ),
        name="layer",
    )(
        bias_table,
        segments,
        queries,
        key_rows,
        value_rows,
        tokens,
        out_proj,
        router.T,
        jnp.swapaxes(routes_one, 1, 2),
        jnp.swapaxes(routes_two, 1, 2),
        old_table[None],
        new_table[None],
        gate_weight,
        up_weight,
        down_weight,
    )


def solution(mesh):
    placed = (
        P(None, "exp", "seq", None),
        P(None, "exp", "seq", None),
        P(None, "exp", "seq", None),
        P(None, "exp", "seq", None),
        P(None, "exp", "seq"),
        P(),
        P(),
        P(),
        P("exp", None, None),
        P("exp", None, None),
        P("exp", None, None),
        P(),
        P(),
        P("exp", "seq", None),
        P("exp", "seq", None),
    )
    return jax.shard_map(
        local, mesh=mesh, in_specs=placed, out_specs=P(None, "exp", "seq", None), check_vma=False
    )
```

```python
import jax
import jax.numpy as jnp
from jax import lax
from jax.experimental import pallas as pl
from jax.experimental.pallas import tpu as pltpu
from jax.sharding import PartitionSpec as P

MESH = pl.DeviceIdType.MESH
BF16 = jnp.bfloat16
F32 = jnp.float32
I32 = jnp.int32

N_SEQ = 16
N_EXP = 16
EXP_Y = 4
EXP_Z = 4
TOK = 128
D = 1024
FFW = 1408
NBUCK = 32
WIN = 4
PAIRS = 8
LANES = 128
HALF = 64
CAP = 20
STRIDE = (48, 48)
SENT = (40, 40)
WIDTH = (512, 1024)
PACK = 32
SINK_BUCKET = 31

EPSILON = 1e-06
MASKED = -1e30


def iota(shape, dim):
    return lax.broadcasted_iota(I32, shape, dim)


def dot(a, b):
    return jnp.dot(a, b, preferred_element_type=F32)


def dot_t(a, b):
    return lax.dot_general(a, b, (((1,), (1,)), ((), ())), preferred_element_type=F32)


def turned(row):
    return jnp.transpose(jnp.broadcast_to(row, (LANES, LANES)))


def remote(src, dst, send, recv, **device):
    return pltpu.make_async_remote_copy(
        src_ref=src,
        dst_ref=dst,
        send_sem=send,
        recv_sem=recv,
        device_id=device,
        device_id_type=MESH,
    )


def bias_of_distance(distance, values):
    result = jnp.broadcast_to(values[0], distance.shape)
    for bucket in range(1, 10):
        result = jnp.where(distance >= (1 << (bucket - 1)), values[bucket], result)
    return result


def plane_step(group):
    return group + (group // 2) * (1 - 2 * lax.rem(group, 2))


def layer_kernel(
    bias_hbm,
    seg_hbm,
    q_hbm,
    k_hbm,
    v_hbm,
    tok_hbm,
    proj_hbm,
    router_hbm,
    one_hbm,
    two_hbm,
    old_hbm,
    new_hbm,
    gate_hbm,
    up_hbm,
    down_hbm,
    out_ref,
    table,
    routes,
    held,
    tabs,
    router,
    tok,
    proj,
    gate_w,
    up_w,
    down_w,
    segs,
    qb,
    kb,
    vb,
    segcol,
    bias,
    sink_out,
    sink_in,
    sink_rows,
    ctx_out,
    ctx_in,
    hidden,
    normed,
    sbuf_one,
    sbuf_two,
    rbuf_one,
    rbuf_two,
    ybuf_one,
    ybuf_two,
    back_one,
    back_two,
    active,
    load_sem,
    qkv_send,
    qkv_recv,
    qkv_own,
    seg_send,
    seg_recv,
    seg_own,
    hop_send,
    hop_recv,
    sink_send,
    sink_recv,
    ctx_send,
    ctx_recv,
    ctx_own,
    go_send,
    go_recv,
    back_send,
    back_recv,
    tok_in,
    place_in,
    place_out,
    tok_send,
    tok_recv,
    place_send,
    place_recv,
    gate_in,
    gate_out,
    gate_send,
    gate_recv,
    part_out,
    part_in,
    red_in,
    part_send,
    part_recv,
    red_send,
    red_recv,
    hidden_part,
):
    me = lax.axis_index("seq")
    my_exp = lax.axis_index("exp")
    upper, pair = me // PAIRS, lax.rem(me, PAIRS)
    me_y, me_z = my_exp // EXP_Z, lax.rem(my_exp, EXP_Z)
    first_of_half = upper * PAIRS
    across = lax.rem(me + PAIRS, N_SEQ)
    sbuf, rbuf = (sbuf_one, sbuf_two), (rbuf_one, rbuf_two)
    ybuf, back = (ybuf_one, ybuf_two), (back_one, back_two)

    early = [
        pltpu.make_async_copy(src, dst, load_sem.at[i])
        for i, (src, dst) in enumerate(
            (
                (old_hbm, held.at[0]),
                (new_hbm, held.at[1]),
                (one_hbm.at[0], routes.at[0]),
                (two_hbm.at[0], routes.at[1]),
                (bias_hbm, table),
            )
        )
    ]
    late = [
        pltpu.make_async_copy(src, dst, load_sem.at[i + 5])
        for i, (src, dst) in enumerate(
            (
                (router_hbm, router),
                (tok_hbm, tok),
                (proj_hbm, proj),
                (gate_hbm.at[0], gate_w),
                (up_hbm.at[0], up_w),
                (down_hbm.at[0], down_w),
            )
        )
    ]
    for copy in early:
        copy.start()

    for batch in range(2):
        low = STRIDE[batch] - 16
        back[batch][:, low:, :] = jnp.zeros((N_EXP, 16, WIDTH[batch]), BF16)
    rbuf[0][:, STRIDE[0] - 16 :, :] = jnp.zeros((N_EXP, 16, WIDTH[0]), BF16)

    @pl.when(upper == 0)
    def _():
        for batch in range(2):
            kb[batch, 0:WIN] = jnp.zeros((WIN, TOK, LANES), BF16)
            vb[batch, 0:WIN] = jnp.zeros((WIN, TOK, LANES), BF16)
            segs[batch, 0:PAIRS] = jnp.full((PAIRS, 1, TOK), -1, I32)
            sink_in[batch] = jnp.zeros((2, 8, LANES), F32)

    barrier = pltpu.get_barrier_semaphore()
    for step in range(1, PAIRS):
        pl.semaphore_signal(
            barrier,
            inc=1,
            device_id={"seq": first_of_half + lax.rem(pair + step, PAIRS)},
            device_id_type=MESH,
        )
    pl.semaphore_signal(barrier, inc=1, device_id={"seq": across}, device_id_type=MESH)
    for step in range(1, N_EXP):
        pl.semaphore_signal(
            barrier,
            inc=1,
            device_id={"exp": lax.rem(my_exp + step, N_EXP)},
            device_id_type=MESH,
        )
    pl.semaphore_wait(barrier, PAIRS + N_EXP - 1)

    def lanes_of(which):
        return pl.ds(pl.multiple_of(which * LANES, LANES), LANES)

    def qkv_parts(batch, target):
        lanes = lanes_of(target)
        return (
            (k_hbm.at[batch, 0, :, lanes], kb.at[batch, pair + WIN]),
            (v_hbm.at[batch, 0, :, lanes], vb.at[batch, pair + WIN]),
            (q_hbm.at[batch, 0, :, lanes], qb.at[batch, pair]),
        )

    def qkv_copies(batch):
        copies = []
        for step in range(1, PAIRS):
            target = lax.rem(pair + step, PAIRS)
            for kind, (src, dst) in enumerate(qkv_parts(batch, target)):
                copies.append(
                    remote(
                        src,
                        dst,
                        qkv_send.at[batch, kind, step],
                        qkv_recv.at[batch, kind, step],
                        seq=first_of_half + target,
                    )
                )
        for kind, (src, dst) in enumerate(qkv_parts(batch, pair)):
            copies.append(pltpu.make_async_copy(src, dst, qkv_own.at[batch, kind]))
        return copies

    qkv = [qkv_copies(batch) for batch in range(2)]
    seg_copies = [
        remote(
            seg_hbm,
            segs.at[:, PAIRS + pair],
            seg_send.at[step],
            seg_recv.at[step],
            seq=first_of_half + lax.rem(pair + step, PAIRS),
        )
        for step in range(1, PAIRS)
    ]
    seg_copies.append(pltpu.make_async_copy(seg_hbm, segs.at[:, PAIRS + pair], seg_own))
    seg_hop = remote(
        segs.at[:, PAIRS : 2 * PAIRS],
        segs.at[:, 0:PAIRS],
        hop_send.at[4],
        hop_recv.at[4],
        seq=across,
    )

    def halo_hop(batch, kind):
        block = (kb, vb)[kind]
        return remote(
            block.at[batch, PAIRS : PAIRS + WIN],
            block.at[batch, 0:WIN],
            hop_send.at[2 * batch + kind],
            hop_recv.at[2 * batch + kind],
            seq=across,
        )

    def sink_hop(batch):
        return remote(
            sink_out.at[batch],
            sink_in.at[batch],
            sink_send.at[batch],
            sink_recv.at[batch],
            seq=across,
        )

    for copy in seg_copies:
        copy.start()
    for copy in qkv[1]:
        copy.start()
    for copy in late:
        copy.start()
    for copy in early:
        copy.wait()

    qi = iota((TOK, TOK), 0)
    kj = iota((TOK, TOK), 1)
    for head in range(2):
        head_row = table[pl.ds(2 * pair + head, 1), :]
        values = [head_row[:, bucket : bucket + 1] for bucket in range(10)]
        rows = slice(head * TOK, (head + 1) * TOK)
        merged = jnp.where(kj <= qi, qi - kj, qi - kj + WIN * TOK)
        bias[0, rows, :] = bias_of_distance(merged, values)
        for block in range(1, WIN):
            bias[block, rows, :] = bias_of_distance(qi - kj + (WIN - block) * TOK, values)
    sink_bias = jnp.where(
        iota((2 * TOK, 1), 0) < TOK,
        table[pl.ds(2 * pair, 1), :][:, SINK_BUCKET : SINK_BUCKET + 1],
        table[pl.ds(2 * pair + 1, 1), :][:, SINK_BUCKET : SINK_BUCKET + 1],
    )

    lane = iota((LANES, LANES), 1)
    row = iota((LANES, LANES), 0)
    tabs[...] = jnp.full((2, LANES), -1, I32)
    tabs[0:1, 0:N_EXP] = held[0]
    tabs[1:2, 0:N_EXP] = held[1]
    steps_y = lax.rem(row // EXP_Z - me_y + 2 * EXP_Y * EXP_Y, EXP_Y)
    steps_z = lax.rem(lax.rem(row, EXP_Z) - me_z + EXP_Z, EXP_Z)
    groups = steps_z + (steps_z // 2) * (1 - 2 * lax.rem(steps_z, 2))
    slot_of_row = (groups * EXP_Y + steps_y).astype(F32)
    holds = turned(tabs[0:1, :]) == lane
    slot_of_expert = jnp.sum(jnp.where(holds, slot_of_row, 0.0), axis=0, keepdims=True)
    new_row = tabs[1:2, :]
    new_col = turned(new_row)
    served = new_col == lane
    serving = jnp.where(served, 1.0, 0.0).astype(BF16)
    slot_two = jnp.sum(jnp.where(served, slot_of_expert, 0.0), axis=1, keepdims=True)
    again = jnp.where((new_col == new_row) & (lane < row), 1.0, 0.0)
    again = jnp.sum(again, axis=1, keepdims=True)
    base_two = jnp.transpose(
        jnp.broadcast_to(slot_two * STRIDE[1] + again * CAP, (LANES, LANES))
    )[0:1, :]
    bases = (slot_of_expert * STRIDE[0], base_two)
    lower = jnp.where(row > lane, 1.0, 0.0).astype(BF16)
    place_cols, place_rows, differences = [], [], []
    for batch in range(2):
        member = [
            jnp.where(turned(routes[batch, c : c + 1, :]) == lane, 1.0, 0.0) for c in range(2)
        ]
        counts = [dot(lower, m.astype(BF16)) for m in member]
        counts[1] = counts[1] + jnp.sum(member[0], axis=0, keepdims=True)
        cols = [
            jnp.sum(m * (c + bases[batch]), axis=1, keepdims=True)
            for m, c in zip(member, counts)
        ]
        place_cols.append(cols)
        place_rows.append(
            [jnp.transpose(jnp.broadcast_to(col, (TOK, TOK)))[0:1, :] for col in cols]
        )
        difference = member[0] - member[1]
        if batch == 1:
            difference = dot(difference.astype(BF16), serving)
        differences.append(difference)
    for c in range(2):
        place_out[c : c + 1, :] = place_rows[1][c]
    place_in[0] = place_out[...]

    def plane(step):
        return me_y * EXP_Z + lax.rem(me_z + step, EXP_Z)

    place_copies = [
        remote(
            place_out,
            place_in.at[group],
            place_send.at[group],
            place_recv.at[group],
            exp=plane(step),
        )
        for group, step in ((1, 1), (2, 3), (3, 2))
    ]
    for copy in place_copies:
        copy.start()
    gate_copies = [
        remote(
            gate_out,
            gate_in.at[group],
            gate_send.at[group],
            gate_recv.at[group],
            exp=plane(step),
        )
        for group, step in ((1, 1), (2, 3), (3, 2))
    ]

    def part_copy(group, half):
        rows = slice(half * (TOK // 2), (half + 1) * (TOK // 2))
        return remote(
            part_out.at[group, rows],
            part_in.at[group, rows],
            part_send.at[group, half],
            part_recv.at[group, half],
            exp=plane((3, 1)[group - 1]),
        )

    def far_copy(half):
        rows = slice(half * (TOK // 2), (half + 1) * (TOK // 2))
        return remote(
            part_out.at[3, rows],
            red_in.at[half],
            red_send.at[half],
            red_recv.at[half],
            exp=plane((3, 1)[half]),
        )

    def token_copy(group, half):
        rows = slice(half * (TOK // 2), (half + 1) * (TOK // 2))
        origin = 1 + half if group == 3 else 0
        step = (1, 3)[half] if group == 3 else (1, 3)[group - 1]
        return remote(
            tok_in.at[origin, rows],
            tok_in.at[group, rows],
            tok_send.at[group, half],
            tok_recv.at[group, half],
            exp=plane(step),
        )

    def relay():
        for half in range(2):
            token_copy(1 + half, half).wait_recv()
            token_copy(3, half).start()

    lane_head = iota((2 * TOK, LANES), 1) // HALF
    row_head = iota((2 * TOK, LANES), 0) // TOK
    own_half = lane_head == row_head
    causal = lax.rem(iota((2 * TOK, TOK), 0), TOK) >= iota((2 * TOK, TOK), 1)

    def twice(value):
        return jnp.concatenate([value, value], axis=0)

    def context_copy(batch, block):
        return remote(
            ctx_out.at[batch, block],
            ctx_in.at[batch, :, lanes_of(pair)],
            ctx_send.at[batch, block],
            ctx_recv.at[batch, pair],
            seq=first_of_half + block,
        )

    def context_own(batch):
        return pltpu.make_async_copy(
            ctx_out.at[batch, pair], ctx_in.at[batch, :, lanes_of(pair)], ctx_own.at[batch]
        )

    def prepare(batch, opening):
        if opening:
            for copy in seg_copies:
                copy.wait()

            @pl.when(upper == 0)
            def _():
                seg_hop.start()

        for copy in qkv[batch]:
            copy.wait()

        @pl.when(upper == 0)
        def _():
            for kind in range(2):
                halo_hop(batch, kind).start()

        if opening:
            for copy in qkv[0]:
                copy.start()

            @pl.when(upper == 1)
            def _():
                seg_hop.wait_recv()

        def columns(block, before):
            line = segs[batch, block]
            segcol[block] = turned(line)
            document = iota((8, TOK), 0)
            return before + jnp.where((line < document) & (line >= 0), 1, 0)

        ahead = lax.fori_loop(0, 2 * PAIRS, columns, jnp.zeros((8, TOK), I32))
        starts = jnp.sum(ahead, axis=1, keepdims=True)

        def sinks(block, sums):
            k_sum, v_sum = sums
            spot = (upper * PAIRS + block) * TOK + iota((8, TOK), 1)
            pick = jnp.where(spot == starts, 1.0, 0.0).astype(BF16)
            return (
                k_sum + dot(pick, kb[batch, block + WIN]),
                v_sum + dot(pick, vb[batch, block + WIN]),
            )

        zero = jnp.zeros((8, LANES), F32)
        k_sink, v_sink = lax.fori_loop(0, PAIRS, sinks, (zero, zero))
        sink_out[batch, 0] = k_sink
        sink_out[batch, 1] = v_sink

        @pl.when(upper == 0)
        def _():
            sink_hop(batch).start()

    def attention(batch, opening):
        @pl.when(upper == 1)
        def _():
            sink_hop(batch).wait_recv()

        sink_rows[0] = sink_out[batch, 0] + sink_in[batch, 0]
        sink_rows[1] = sink_out[batch, 1] + sink_in[batch, 1]

        def attend(block):
            query = twice(qb[batch, block].astype(F32) * 0.125)
            query = jnp.where(own_half, query, 0.0)
            query_rows = query.astype(BF16)
            mine = segcol[block + PAIRS]
            pieces = []
            for near in range(WIN + 1):
                raw = dot_t(query_rows, kb[batch, block + near])
                same = twice(mine == segs[batch, block + near + WIN])
                pieces.append((raw, same))
            merged = jnp.where(causal, pieces[WIN][0], pieces[0][0])
            merged_same = jnp.where(
                causal, pieces[WIN][1].astype(I32), pieces[0][1].astype(I32)
            )
            scores = [jnp.where(merged_same > 0, merged + bias[0], MASKED)]
            for near in range(1, WIN):
                raw, same = pieces[near]
                scores.append(jnp.where(same, raw + bias[near], MASKED))
            chosen_doc = iota((8, LANES), 0) == segs[batch, block + PAIRS][:, 0:1]
            k_row = jnp.sum(jnp.where(chosen_doc, sink_rows[0], 0.0), axis=0, keepdims=True)
            v_row = jnp.sum(jnp.where(chosen_doc, sink_rows[1], 0.0), axis=0, keepdims=True)
            sink_seen = twice(mine[:, 0:1] == segcol[block + WIN][:, 0:1])
            sink = jnp.sum(query * k_row, axis=1, keepdims=True) + sink_bias
            sink = jnp.where(sink_seen, sink, MASKED)
            peak = jnp.maximum(
                jnp.maximum(scores[0], scores[1]), jnp.maximum(scores[2], scores[3])
            )
            peak = jnp.maximum(jnp.max(peak, axis=1, keepdims=True), sink)
            weights = [jnp.exp(score - peak) for score in scores]
            sink_weight = jnp.exp(sink - peak)
            total = (weights[0] + weights[1]) + (weights[2] + weights[3])
            total = jnp.sum(total, axis=1, keepdims=True) + sink_weight
            mixed = sink_weight * v_row
            mixed = mixed + dot(jnp.where(causal, 0.0, weights[0]).astype(BF16), vb[batch, block])
            mixed = mixed + dot(
                jnp.where(causal, weights[0], 0.0).astype(BF16), vb[batch, block + WIN]
            )
            for near in range(1, WIN):
                mixed = mixed + dot(weights[near].astype(BF16), vb[batch, block + near])
            mixed = mixed / total
            ctx_out[batch, block] = jnp.where(
                lane_head[:TOK] == 0, mixed[:TOK], mixed[TOK:]
            ).astype(BF16)

            @pl.when(block == pair)
            def _():
                context_own(batch).start()

            @pl.when(block != pair)
            def _():
                context_copy(batch, block).start()

        def attend_late(turn, carry):
            attend(WIN + lax.rem(pair + turn, WIN))
            return carry

        def attend_early(turn, carry):
            attend(lax.rem(pair + turn, WIN))
            return carry

        lax.fori_loop(0, WIN, attend_late, 0)
        if not opening:
            relay()

        @pl.when(upper == 1)
        def _():
            for kind in range(2):
                halo_hop(batch, kind).wait_recv()

        lax.fori_loop(0, WIN, attend_early, 0)

    def target_of(group, dy, sign):
        y = lax.rem(me_y + EXP_Y + sign * dy, EXP_Y)
        z = lax.rem(me_z + EXP_Z + sign * plane_step(group), EXP_Z)
        return y * EXP_Z + z

    def beside(dy):
        return lax.rem(me_y + dy, EXP_Y) * EXP_Z + me_z

    def dispatch(batch, group, dy):
        slot = group * EXP_Y + dy
        rows = slice(0, SENT[batch])
        return remote(
            sbuf[batch].at[slot, rows],
            rbuf[batch].at[slot, rows],
            go_send.at[batch, slot],
            go_recv.at[batch, slot],
            exp=beside(dy) if batch == 1 else target_of(group, dy, 1),
        )

    def answer(batch, group, dy):
        slot = group * EXP_Y + dy
        rows = slice(0, SENT[batch])
        return remote(
            ybuf[batch].at[slot, rows],
            back[batch].at[slot, rows],
            back_send.at[batch, slot],
            back_recv.at[batch, slot],
            exp=beside(EXP_Y - dy) if batch == 1 else target_of(group, dy, -1),
        )

    gates = [None, None]

    def pick(batch, group, places, source):
        stride = STRIDE[batch]
        spot = (iota((EXP_Y * stride, TOK), 0) + group * EXP_Y * stride).astype(F32)
        hit = (spot == places[0]) | (spot == places[1])
        plan = jnp.where(hit, 1.0, 0.0).astype(BF16)
        if batch == 0:
            hit = (spot == places[0] + CAP) | (spot == places[1] + CAP)
            other = jnp.where(hit, 1.0, 0.0).astype(BF16)
            halves = dot(plan, source[:, : WIDTH[0]]) + dot(other, source[:, WIDTH[0] :])
            sbuf[0][group * EXP_Y : (group + 1) * EXP_Y] = halves.astype(BF16).reshape(
                EXP_Y, stride, WIDTH[0]
            )
            return
        for part in range(2):
            cols = slice(part * 512, (part + 1) * 512)
            sbuf[batch][group * EXP_Y : (group + 1) * EXP_Y, :, cols] = (
                dot(plan, source[:, cols]).astype(BF16).reshape(EXP_Y, stride, 512)
            )

    def spread(group):
        if group > 0:
            place_copies[group - 1].wait_recv()
            for half in range(2):
                if (group, half) not in ((1, 0), (2, 1)):
                    token_copy(group, half).wait_recv()
        places = [place_in[group, c : c + 1, :] for c in range(2)]
        pick(1, group, places, tok_in.at[group])
        for dy in range(1, EXP_Y):
            dispatch(1, group, dy).start()
        rbuf[1][group * EXP_Y] = sbuf[1][group * EXP_Y]

    def front(batch, opening):
        for step in range(1, PAIRS):
            source = lax.rem(pair + step, PAIRS)
            remote(
                ctx_out.at[batch, source],
                ctx_in.at[batch, :, lanes_of(source)],
                ctx_send.at[batch, source],
                ctx_recv.at[batch, source],
                seq=first_of_half + source,
            ).wait_recv()
        context_own(batch).wait()
        if opening:
            for copy in late[:3]:
                copy.wait()
        context = ctx_in[batch]
        for part in range(2):
            cols = slice(part * 512, (part + 1) * 512)
            hidden[batch, :, cols] = tok[batch, 0, :, cols].astype(F32) + dot(
                context, proj[:, cols]
            )
        value = hidden[batch]
        scale = lax.rsqrt(jnp.mean(value * value, axis=1, keepdims=True) + EPSILON)
        rows_value = (value * scale).astype(BF16)
        if batch == 1:
            tok_in[0] = rows_value
            for group, half in ((1, 0), (2, 1), (1, 1), (2, 0)):
                token_copy(group, half).start()
            spread(0)
            source = tok_in[0]
        else:
            normed[...] = rows_value
            for group in (3, 1, 2, 0):
                pick(batch, group, place_rows[0], normed)
                for dy in range(EXP_Y):
                    if group + dy > 0:
                        dispatch(batch, group, dy).start()
            rbuf[batch][0] = sbuf[batch][0]
            source = normed[...]
        logits = dot_t(source, router[...])
        picked = jnp.sum(differences[batch][:, :N_EXP] * logits, axis=1, keepdims=True)
        first = jax.nn.sigmoid(picked)
        gates[batch] = (first, 1.0 - first)
        if batch == 1:
            for c in range(2):
                gate_out[c : c + 1, :] = jnp.transpose(
                    jnp.broadcast_to(gates[batch][c], (TOK, TOK))
                )[0:1, :]
            gate_in[0] = gate_out[...]
            for copy in gate_copies:
                copy.start()

    def serve_all(batch, low, high):
        stride = STRIDE[batch]
        count = EXP_Y * (stride if batch == 1 else PACK)
        if batch == 0:
            inner_row = iota((PACK, EXP_Y * stride), 0)
            inner_col = iota((PACK, EXP_Y * stride), 1)
            outer_row = iota((stride, EXP_Y * PACK), 0)
            outer_col = iota((stride, EXP_Y * PACK), 1)
            unpack, pack = [], []
            for side in range(2):
                near, far = [], []
                for dy in range(EXP_Y):
                    hit = inner_col == inner_row + (dy * stride + side * CAP)
                    near.append(jnp.where(hit & (inner_row < CAP), 1.0, 0.0))
                    hit = outer_col == outer_row + (dy * PACK - side * CAP)
                    inside = (outer_row >= side * CAP) & (outer_row < (side + 1) * CAP)
                    far.append(jnp.where(hit & inside, 1.0, 0.0))
                unpack.append(jnp.concatenate(near, axis=0).astype(BF16))
                pack.append(jnp.concatenate(far, axis=0).astype(BF16))

        def serve(turn, carry):
            group = lax.rem(turn + 1, EXP_Z)
            for dy in range(EXP_Y):
                if dy == 0 and batch == 1:
                    continue
                if dy == 0:

                    @pl.when(group > 0)
                    def _():
                        dispatch(batch, group, dy).wait_recv()

                else:
                    dispatch(batch, group, dy).wait_recv()
            arrived = rbuf[batch][pl.ds(group * EXP_Y, EXP_Y)].reshape(
                EXP_Y * stride, WIDTH[batch]
            )
            if batch == 0:
                inputs = jnp.concatenate(
                    [dot(unpack[side], arrived).astype(BF16) for side in range(2)], axis=1
                )
            else:
                inputs = arrived
            for low, high in ((0, 512), (512, 1024), (1024, FFW)):
                gate = dot(inputs, gate_w[:, low:high])
                up = dot(inputs, up_w[:, low:high])
                inner = 0.7978845608028654 * (gate + 0.044715 * (gate * gate * gate))
                active[0:count, low:high] = (0.5 * gate * (1.0 + jnp.tanh(inner)) * up).astype(
                    BF16
                )
            if batch == 0:
                outs = [
                    dot(active[0:count], down_w[:, side * 512 : (side + 1) * 512]).astype(BF16)
                    for side in range(2)
                ]
                halves = dot(pack[0], outs[0]) + dot(pack[1], outs[1])
                ybuf[0][pl.ds(group * EXP_Y, EXP_Y)] = halves.astype(BF16).reshape(
                    EXP_Y, stride, WIDTH[0]
                )
            for part in range(2 * batch):
                cols = slice(part * 512, (part + 1) * 512)
                ybuf[batch][pl.ds(group * EXP_Y, EXP_Y), :, cols] = (
                    dot(active[0:count], down_w[:, cols])
                    .astype(BF16)
                    .reshape(EXP_Y, stride, 512)
                )
            for dy in range(EXP_Y):
                if dy == 0 and batch == 1:
                    back[1][group * EXP_Y] = ybuf[1][group * EXP_Y]
                elif dy == 0:

                    @pl.when(group > 0)
                    def _():
                        answer(batch, group, dy).start()

                else:
                    answer(batch, group, dy).start()
            return carry

        lax.fori_loop(low, high, serve, 0)
        if batch == 0 and high == EXP_Z:
            back[batch][0] = ybuf[batch][0]

    def blend(batch, group, places, weights):
        stride = STRIDE[batch]
        spot = (iota((TOK, EXP_Y * stride), 1) + group * EXP_Y * stride).astype(F32)
        shifts = (0, CAP) if batch == 0 else (0,)
        terms = []
        for shift in shifts:
            mix = jnp.where(spot == places[0] + shift, weights[0], 0.0) + jnp.where(
                spot == places[1] + shift, weights[1], 0.0
            )
            coarse = mix.astype(BF16)
            terms += [coarse, (mix - coarse.astype(F32)).astype(BF16)]
        rows = back[batch][group * EXP_Y : (group + 1) * EXP_Y].reshape(
            EXP_Y * stride, WIDTH[batch]
        )
        both = dot(jnp.concatenate(terms, axis=0), rows)
        sums = [
            both[2 * side * TOK : (2 * side + 1) * TOK]
            + both[(2 * side + 1) * TOK : (2 * side + 2) * TOK]
            for side in range(len(shifts))
        ]
        return sums[0] if batch == 1 else jnp.concatenate(sums, axis=1)

    def plane_sum(group):
        for dy in range(1, EXP_Y):
            answer(1, group, dy).wait_recv()
        if group == 0:
            return blend(1, 0, place_cols[1], gates[1])
        gate_copies[group - 1].wait_recv()
        places = [turned(place_in[group, c : c + 1, :])[:, 0:1] for c in range(2)]
        weights = [turned(gate_in[group, c : c + 1, :])[:, 0:1] for c in range(2)]
        return blend(1, group, places, weights)

    half_rows = (slice(0, TOK // 2), slice(TOK // 2, TOK))

    def plane_sums():
        part_out[3] = plane_sum(3).astype(BF16)
        for half in range(2):
            far_copy(half).start()
        for group in (1, 2):
            total = plane_sum(group)
            near, far = half_rows[group - 1], half_rows[2 - group]
            part_out[group, far] = total[far].astype(BF16)
            part_copy(group, 2 - group).start()
            hidden_part[group - 1] = total[near]

    def pass_on():
        for group in (1, 2):
            near = half_rows[group - 1]
            far_copy(group - 1).wait_recv()
            total = hidden_part[group - 1] + red_in[group - 1].astype(F32)
            part_out[group, near] = total.astype(BF16)
            part_copy(group, group - 1).start()

    def finish_one():
        result = hidden[0]
        for group in range(EXP_Z):
            for dy in range(EXP_Y):
                if group + dy > 0:
                    answer(0, group, dy).wait_recv()
            result = result + blend(0, group, place_cols[0], gates[0])
        out_ref[0, 0] = result.astype(BF16)

    def finish_two():
        result = hidden[1] + plane_sum(0)
        for group in (1, 2):
            for half in range(2):
                part_copy(group, half).wait_recv()
        result = result + part_in[1].astype(F32) + part_in[2].astype(F32)
        out_ref[1, 0] = result.astype(BF16)

    prepare(1, True)
    attention(1, True)
    prepare(0, False)
    front(1, True)
    attention(0, False)
    spread(1)
    spread(2)
    front(0, False)
    spread(3)
    for copy in late[3:]:
        copy.wait()
    serve_all(1, 0, EXP_Z)
    plane_sums()
    serve_all(0, 0, 2)
    pass_on()
    serve_all(0, 2, EXP_Z)
    finish_one()
    finish_two()

    for batch in range(2):
        for group in range(EXP_Z):
            for dy in range(EXP_Y):
                if dy > 0 or (batch == 0 and group > 0):
                    dispatch(batch, group, dy).wait_send()
                    answer(batch, group, dy).wait_send()
        for step in range(1, PAIRS):
            context_copy(batch, lax.rem(pair + step, PAIRS)).wait_send()

    for group in range(1, EXP_Z):
        place_copies[group - 1].wait_send()
        gate_copies[group - 1].wait_send()
        for half in range(2):
            token_copy(group, half).wait_send()
            if group < 3:
                part_copy(group, half).wait_send()
    for half in range(2):
        far_copy(half).wait_send()

    @pl.when(upper == 0)
    def _():
        seg_hop.wait_send()
        for batch in range(2):
            sink_hop(batch).wait_send()
            for kind in range(2):
                halo_hop(batch, kind).wait_send()


def local(
    tokens,
    queries,
    key_rows,
    value_rows,
    segments,
    bias_table,
    out_proj,
    router,
    gate_weight,
    up_weight,
    down_weight,
    old_table,
    new_table,
    routes_one,
    routes_two,
):
    any_spec = pl.BlockSpec(memory_space=pl.ANY)
    vmem = pltpu.VMEM
    dma = pltpu.SemaphoreType.DMA
    buffers = [vmem((N_EXP, stride, width), BF16) for stride, width in zip(STRIDE, WIDTH)]
    return pl.pallas_call(
        layer_kernel,
        out_shape=jax.ShapeDtypeStruct((2, 1, TOK, D), BF16),
        in_specs=[any_spec] * 15,
        out_specs=pl.BlockSpec(memory_space=pltpu.VMEM),
        scratch_shapes=[
            vmem((N_EXP, NBUCK), F32),
            vmem((2, 2, TOK), I32),
            vmem((2, 1, N_EXP), I32),
            vmem((2, LANES), I32),
            vmem((N_EXP, D), BF16),
            vmem((2, 1, TOK, D), BF16),
            vmem((D, D), BF16),
            vmem((D, FFW), BF16),
            vmem((D, FFW), BF16),
            vmem((FFW, D), BF16),
            vmem((2, N_SEQ, 1, TOK), I32),
            vmem((2, PAIRS, TOK, LANES), BF16),
            vmem((2, PAIRS + WIN, TOK, LANES), BF16),
            vmem((2, PAIRS + WIN, TOK, LANES), BF16),
            vmem((N_SEQ, TOK, TOK), I32),
            vmem((WIN, 2 * TOK, TOK), F32),
            vmem((2, 2, 8, LANES), F32),
            vmem((2, 2, 8, LANES), F32),
            vmem((2, 8, LANES), F32),
            vmem((2, PAIRS, TOK, LANES), BF16),
            vmem((2, TOK, D), BF16),
            vmem((2, TOK, D), F32),
            vmem((TOK, D), BF16),
            *buffers,
            *buffers,
            *buffers,
            *buffers,
            vmem((EXP_Y * STRIDE[1], FFW), BF16),
            dma((11,)),
            dma((2, 3, PAIRS)),
            dma((2, 3, PAIRS)),
            dma((2, 3)),
            dma((PAIRS,)),
            dma((PAIRS,)),
            dma(()),
            dma((5,)),
            dma((5,)),
            dma((2,)),
            dma((2,)),
            dma((2, PAIRS)),
            dma((2, PAIRS)),
            dma((2,)),
            dma((2, N_EXP)),
            dma((2, N_EXP)),
            dma((2, N_EXP)),
            dma((2, N_EXP)),
            vmem((EXP_Z, TOK, D), BF16),
            vmem((EXP_Z, 2, TOK), F32),
            vmem((2, TOK), F32),
            dma((EXP_Z, 2)),
            dma((EXP_Z, 2)),
            dma((EXP_Z,)),
            dma((EXP_Z,)),
            vmem((EXP_Z, 2, TOK), F32),
            vmem((2, TOK), F32),
            dma((EXP_Z,)),
            dma((EXP_Z,)),
            vmem((EXP_Z, TOK, D), BF16),
            vmem((EXP_Z, TOK, D), BF16),
            vmem((2, TOK // 2, D), BF16),
            dma((EXP_Z, 2)),
            dma((EXP_Z, 2)),
            dma((2,)),
            dma((2,)),
            vmem((2, TOK // 2, D), F32),
        ],
        compiler_params=pltpu.CompilerParams(
            collective_id=0, has_side_effects=True, vmem_limit_bytes=56 << 20
        ),
        name="layer",
    )(
        bias_table,
        segments,
        queries,
        key_rows,
        value_rows,
        tokens,
        out_proj,
        router.T,
        jnp.swapaxes(routes_one, 1, 2),
        jnp.swapaxes(routes_two, 1, 2),
        old_table[None],
        new_table[None],
        gate_weight,
        up_weight,
        down_weight,
    )


def solution(mesh):
    placed = (
        P(None, "exp", "seq", None),
        P(None, "exp", "seq", None),
        P(None, "exp", "seq", None),
        P(None, "exp", "seq", None),
        P(None, "exp", "seq"),
        P(),
        P(),
        P(),
        P("exp", None, None),
        P("exp", None, None),
        P("exp", None, None),
        P(),
        P(),
        P("exp", "seq", None),
        P("exp", "seq", None),
    )
    return jax.shard_map(
        local, mesh=mesh, in_specs=placed, out_specs=P(None, "exp", "seq", None), check_vma=False
    )
```

```python
import jax
import jax.numpy as jnp
from jax import lax
from jax.experimental import pallas as pl
from jax.experimental.pallas import tpu as pltpu
from jax.sharding import PartitionSpec as P

MESH = pl.DeviceIdType.MESH
BF16 = jnp.bfloat16
F32 = jnp.float32
I32 = jnp.int32

N_SEQ = 16
N_EXP = 16
EXP_Y = 4
EXP_Z = 4
TOK = 128
D = 1024
FFW = 1408
NBUCK = 32
WIN = 4
PAIRS = 8
LANES = 128
HALF = 64
CAP = 20
STRIDE = (48, 48)
SENT = (40, 40)
WIDTH = (512, 1024)
PACK = 32
SINK_BUCKET = 31

EPSILON = 1e-06
MASKED = -1e30


def iota(shape, dim):
    return lax.broadcasted_iota(I32, shape, dim)


def dot(a, b):
    return jnp.dot(a, b, preferred_element_type=F32)


def dot_t(a, b):
    return lax.dot_general(a, b, (((1,), (1,)), ((), ())), preferred_element_type=F32)


def turned(row):
    return jnp.transpose(jnp.broadcast_to(row, (LANES, LANES)))


def remote(src, dst, send, recv, **device):
    return pltpu.make_async_remote_copy(
        src_ref=src,
        dst_ref=dst,
        send_sem=send,
        recv_sem=recv,
        device_id=device,
        device_id_type=MESH,
    )


def bias_of_distance(distance, values):
    result = jnp.broadcast_to(values[0], distance.shape)
    for bucket in range(1, 10):
        result = jnp.where(distance >= (1 << (bucket - 1)), values[bucket], result)
    return result


def plane_step(group):
    return group + (group // 2) * (1 - 2 * lax.rem(group, 2))


def layer_kernel(
    bias_hbm,
    seg_hbm,
    q_hbm,
    k_hbm,
    v_hbm,
    tok_hbm,
    proj_hbm,
    router_hbm,
    one_hbm,
    two_hbm,
    old_hbm,
    new_hbm,
    gate_hbm,
    up_hbm,
    down_hbm,
    out_ref,
    table,
    routes,
    held,
    tabs,
    router,
    tok,
    proj,
    gate_w,
    up_w,
    down_w,
    segs,
    qb,
    kb,
    vb,
    segcol,
    bias,
    sink_out,
    sink_in,
    sink_rows,
    ctx_out,
    ctx_in,
    hidden,
    normed,
    sbuf_one,
    sbuf_two,
    rbuf_one,
    rbuf_two,
    ybuf_one,
    ybuf_two,
    back_one,
    back_two,
    active,
    load_sem,
    qkv_send,
    qkv_recv,
    qkv_own,
    seg_send,
    seg_recv,
    seg_own,
    hop_send,
    hop_recv,
    sink_send,
    sink_recv,
    ctx_send,
    ctx_recv,
    ctx_own,
    go_send,
    go_recv,
    back_send,
    back_recv,
    tok_in,
    place_in,
    place_out,
    tok_send,
    tok_recv,
    place_send,
    place_recv,
    gate_in,
    gate_out,
    gate_send,
    gate_recv,
    part_out,
    part_in,
    red_in,
    part_send,
    part_recv,
    red_send,
    red_recv,
    hidden_part,
):
    me = lax.axis_index("seq")
    my_exp = lax.axis_index("exp")
    upper, pair = me // PAIRS, lax.rem(me, PAIRS)
    me_y, me_z = my_exp // EXP_Z, lax.rem(my_exp, EXP_Z)
    first_of_half = upper * PAIRS
    across = lax.rem(me + PAIRS, N_SEQ)
    sbuf, rbuf = (sbuf_one, sbuf_two), (rbuf_one, rbuf_two)
    ybuf, back = (ybuf_one, ybuf_two), (back_one, back_two)

    early = [
        pltpu.make_async_copy(src, dst, load_sem.at[i])
        for i, (src, dst) in enumerate(
            (
                (old_hbm, held.at[0]),
                (new_hbm, held.at[1]),
                (one_hbm.at[0], routes.at[0]),
                (two_hbm.at[0], routes.at[1]),
                (bias_hbm, table),
            )
        )
    ]
    late = [
        pltpu.make_async_copy(src, dst, load_sem.at[i + 5])
        for i, (src, dst) in enumerate(
            (
                (router_hbm, router),
                (tok_hbm, tok),
                (proj_hbm, proj),
                (gate_hbm.at[0], gate_w),
                (up_hbm.at[0], up_w),
                (down_hbm.at[0], down_w),
            )
        )
    ]
    for copy in early:
        copy.start()

    for batch in range(2):
        low = STRIDE[batch] - 16
        back[batch][:, low:, :] = jnp.zeros((N_EXP, 16, WIDTH[batch]), BF16)
    rbuf[0][:, STRIDE[0] - 16 :, :] = jnp.zeros((N_EXP, 16, WIDTH[0]), BF16)

    @pl.when(upper == 0)
    def _():
        for batch in range(2):
            kb[batch, 0:WIN] = jnp.zeros((WIN, TOK, LANES), BF16)
            vb[batch, 0:WIN] = jnp.zeros((WIN, TOK, LANES), BF16)
            segs[batch, 0:PAIRS] = jnp.full((PAIRS, 1, TOK), -1, I32)
            sink_in[batch] = jnp.zeros((2, 8, LANES), F32)

    barrier = pltpu.get_barrier_semaphore()
    for step in range(1, PAIRS):
        pl.semaphore_signal(
            barrier,
            inc=1,
            device_id={"seq": first_of_half + lax.rem(pair + step, PAIRS)},
            device_id_type=MESH,
        )
    pl.semaphore_signal(barrier, inc=1, device_id={"seq": across}, device_id_type=MESH)
    for step in range(1, N_EXP):
        pl.semaphore_signal(
            barrier,
            inc=1,
            device_id={"exp": lax.rem(my_exp + step, N_EXP)},
            device_id_type=MESH,
        )
    pl.semaphore_wait(barrier, PAIRS + N_EXP - 1)

    def lanes_of(which):
        return pl.ds(pl.multiple_of(which * LANES, LANES), LANES)

    def qkv_parts(batch, target):
        lanes = lanes_of(target)
        return (
            (k_hbm.at[batch, 0, :, lanes], kb.at[batch, pair + WIN]),
            (v_hbm.at[batch, 0, :, lanes], vb.at[batch, pair + WIN]),
            (q_hbm.at[batch, 0, :, lanes], qb.at[batch, pair]),
        )

    def qkv_copies(batch):
        copies = []
        for step in range(1, PAIRS):
            target = lax.rem(pair + step, PAIRS)
            for kind, (src, dst) in enumerate(qkv_parts(batch, target)):
                copies.append(
                    remote(
                        src,
                        dst,
                        qkv_send.at[batch, kind, step],
                        qkv_recv.at[batch, kind, step],
                        seq=first_of_half + target,
                    )
                )
        for kind, (src, dst) in enumerate(qkv_parts(batch, pair)):
            copies.append(pltpu.make_async_copy(src, dst, qkv_own.at[batch, kind]))
        return copies

    qkv = [qkv_copies(batch) for batch in range(2)]
    seg_copies = [
        remote(
            seg_hbm,
            segs.at[:, PAIRS + pair],
            seg_send.at[step],
            seg_recv.at[step],
            seq=first_of_half + lax.rem(pair + step, PAIRS),
        )
        for step in range(1, PAIRS)
    ]
    seg_copies.append(pltpu.make_async_copy(seg_hbm, segs.at[:, PAIRS + pair], seg_own))
    seg_hop = remote(
        segs.at[:, PAIRS : 2 * PAIRS],
        segs.at[:, 0:PAIRS],
        hop_send.at[4],
        hop_recv.at[4],
        seq=across,
    )

    def halo_hop(batch, kind):
        block = (kb, vb)[kind]
        return remote(
            block.at[batch, PAIRS : PAIRS + WIN],
            block.at[batch, 0:WIN],
            hop_send.at[2 * batch + kind],
            hop_recv.at[2 * batch + kind],
            seq=across,
        )

    def sink_hop(batch):
        return remote(
            sink_out.at[batch],
            sink_in.at[batch],
            sink_send.at[batch],
            sink_recv.at[batch],
            seq=across,
        )

    for copy in seg_copies:
        copy.start()
    for copy in qkv[1]:
        copy.start()
    for copy in late:
        copy.start()
    for copy in early:
        copy.wait()

    qi = iota((TOK, TOK), 0)
    kj = iota((TOK, TOK), 1)
    for head in range(2):
        head_row = table[pl.ds(2 * pair + head, 1), :]
        values = [head_row[:, bucket : bucket + 1] for bucket in range(10)]
        rows = slice(head * TOK, (head + 1) * TOK)
        merged = jnp.where(kj <= qi, qi - kj, qi - kj + WIN * TOK)
        bias[0, rows, :] = bias_of_distance(merged, values)
        for block in range(1, WIN):
            bias[block, rows, :] = bias_of_distance(qi - kj + (WIN - block) * TOK, values)
    sink_bias = jnp.where(
        iota((2 * TOK, 1), 0) < TOK,
        table[pl.ds(2 * pair, 1), :][:, SINK_BUCKET : SINK_BUCKET + 1],
        table[pl.ds(2 * pair + 1, 1), :][:, SINK_BUCKET : SINK_BUCKET + 1],
    )

    lane = iota((LANES, LANES), 1)
    row = iota((LANES, LANES), 0)
    tabs[...] = jnp.full((2, LANES), -1, I32)
    tabs[0:1, 0:N_EXP] = held[0]
    tabs[1:2, 0:N_EXP] = held[1]
    steps_y = lax.rem(row // EXP_Z - me_y + 2 * EXP_Y * EXP_Y, EXP_Y)
    steps_z = lax.rem(lax.rem(row, EXP_Z) - me_z + EXP_Z, EXP_Z)
    groups = steps_z + (steps_z // 2) * (1 - 2 * lax.rem(steps_z, 2))
    slot_of_row = (groups * EXP_Y + steps_y).astype(F32)
    holds = turned(tabs[0:1, :]) == lane
    slot_of_expert = jnp.sum(jnp.where(holds, slot_of_row, 0.0), axis=0, keepdims=True)
    new_row = tabs[1:2, :]
    new_col = turned(new_row)
    served = new_col == lane
    serving = jnp.where(served, 1.0, 0.0).astype(BF16)
    slot_two = jnp.sum(jnp.where(served, slot_of_expert, 0.0), axis=1, keepdims=True)
    again = jnp.where((new_col == new_row) & (lane < row), 1.0, 0.0)
    again = jnp.sum(again, axis=1, keepdims=True)
    base_two = jnp.transpose(
        jnp.broadcast_to(slot_two * STRIDE[1] + again * CAP, (LANES, LANES))
    )[0:1, :]
    bases = (slot_of_expert * STRIDE[0], base_two)
    lower = jnp.where(row > lane, 1.0, 0.0).astype(BF16)
    place_cols, place_rows, differences = [], [], []
    for batch in range(2):
        member = [
            jnp.where(turned(routes[batch, c : c + 1, :]) == lane, 1.0, 0.0) for c in range(2)
        ]
        counts = [dot(lower, m.astype(BF16)) for m in member]
        counts[1] = counts[1] + jnp.sum(member[0], axis=0, keepdims=True)
        cols = [
            jnp.sum(m * (c + bases[batch]), axis=1, keepdims=True)
            for m, c in zip(member, counts)
        ]
        place_cols.append(cols)
        place_rows.append(
            [jnp.transpose(jnp.broadcast_to(col, (TOK, TOK)))[0:1, :] for col in cols]
        )
        difference = member[0] - member[1]
        if batch == 1:
            difference = dot(difference.astype(BF16), serving)
        differences.append(difference)
    for c in range(2):
        place_out[c : c + 1, :] = place_rows[1][c]
    place_in[0] = place_out[...]

    def plane(step):
        return me_y * EXP_Z + lax.rem(me_z + step, EXP_Z)

    place_copies = [
        remote(
            place_out,
            place_in.at[group],
            place_send.at[group],
            place_recv.at[group],
            exp=plane(step),
        )
        for group, step in ((1, 1), (2, 3), (3, 2))
    ]
    for copy in place_copies:
        copy.start()
    gate_copies = [
        remote(
            gate_out,
            gate_in.at[group],
            gate_send.at[group],
            gate_recv.at[group],
            exp=plane(step),
        )
        for group, step in ((1, 1), (2, 3), (3, 2))
    ]

    def part_copy(group, half):
        rows = slice(half * (TOK // 2), (half + 1) * (TOK // 2))
        return remote(
            part_out.at[group, rows],
            part_in.at[group, rows],
            part_send.at[group, half],
            part_recv.at[group, half],
            exp=plane((3, 1)[group - 1]),
        )

    def far_copy(half):
        rows = slice(half * (TOK // 2), (half + 1) * (TOK // 2))
        return remote(
            part_out.at[3, rows],
            red_in.at[half],
            red_send.at[half],
            red_recv.at[half],
            exp=plane((3, 1)[half]),
        )

    def token_copy(group, half):
        rows = slice(half * (TOK // 2), (half + 1) * (TOK // 2))
        origin = 1 + half if group == 3 else 0
        step = (1, 3)[half] if group == 3 else (1, 3)[group - 1]
        return remote(
            tok_in.at[origin, rows],
            tok_in.at[group, rows],
            tok_send.at[group, half],
            tok_recv.at[group, half],
            exp=plane(step),
        )

    def relay():
        for half in range(2):
            token_copy(1 + half, half).wait_recv()
            token_copy(3, half).start()

    lane_head = iota((2 * TOK, LANES), 1) // HALF
    row_head = iota((2 * TOK, LANES), 0) // TOK
    own_half = lane_head == row_head
    causal = lax.rem(iota((2 * TOK, TOK), 0), TOK) >= iota((2 * TOK, TOK), 1)

    def twice(value):
        return jnp.concatenate([value, value], axis=0)

    def context_copy(batch, block):
        return remote(
            ctx_out.at[batch, block],
            ctx_in.at[batch, :, lanes_of(pair)],
            ctx_send.at[batch, block],
            ctx_recv.at[batch, pair],
            seq=first_of_half + block,
        )

    def context_own(batch):
        return pltpu.make_async_copy(
            ctx_out.at[batch, pair], ctx_in.at[batch, :, lanes_of(pair)], ctx_own.at[batch]
        )

    def prepare(batch, opening):
        if opening:
            for copy in seg_copies:
                copy.wait()

            @pl.when(upper == 0)
            def _():
                seg_hop.start()

        for copy in qkv[batch]:
            copy.wait()

        @pl.when(upper == 0)
        def _():
            for kind in range(2):
                halo_hop(batch, kind).start()

        if opening:
            for copy in qkv[0]:
                copy.start()

            @pl.when(upper == 1)
            def _():
                seg_hop.wait_recv()

    def find_starts(batch):
        def columns(block, before):
            line = segs[batch, block]
            segcol[block] = turned(line)
            document = iota((8, TOK), 0)
            return before + jnp.where((line < document) & (line >= 0), 1, 0)

        ahead = lax.fori_loop(0, 2 * PAIRS, columns, jnp.zeros((8, TOK), I32))
        starts = jnp.sum(ahead, axis=1, keepdims=True)

        def sinks(block, sums):
            k_sum, v_sum = sums
            spot = (upper * PAIRS + block) * TOK + iota((8, TOK), 1)
            pick = jnp.where(spot == starts, 1.0, 0.0).astype(BF16)
            return (
                k_sum + dot(pick, kb[batch, block + WIN]),
                v_sum + dot(pick, vb[batch, block + WIN]),
            )

        zero = jnp.zeros((8, LANES), F32)
        k_sink, v_sink = lax.fori_loop(0, PAIRS, sinks, (zero, zero))
        sink_out[batch, 0] = k_sink
        sink_out[batch, 1] = v_sink

        @pl.when(upper == 0)
        def _():
            sink_hop(batch).start()

    def attention(batch, opening):
        @pl.when(upper == 1)
        def _():
            sink_hop(batch).wait_recv()

        sink_rows[0] = sink_out[batch, 0] + sink_in[batch, 0]
        sink_rows[1] = sink_out[batch, 1] + sink_in[batch, 1]

        def attend(block):
            query = twice(qb[batch, block].astype(F32) * 0.125)
            query = jnp.where(own_half, query, 0.0)
            query_rows = query.astype(BF16)
            mine = segcol[block + PAIRS]
            pieces = []
            for near in range(WIN + 1):
                raw = dot_t(query_rows, kb[batch, block + near])
                same = twice(mine == segs[batch, block + near + WIN])
                pieces.append((raw, same))
            merged = jnp.where(causal, pieces[WIN][0], pieces[0][0])
            merged_same = jnp.where(
                causal, pieces[WIN][1].astype(I32), pieces[0][1].astype(I32)
            )
            scores = [jnp.where(merged_same > 0, merged + bias[0], MASKED)]
            for near in range(1, WIN):
                raw, same = pieces[near]
                scores.append(jnp.where(same, raw + bias[near], MASKED))
            chosen_doc = iota((8, LANES), 0) == segs[batch, block + PAIRS][:, 0:1]
            k_row = jnp.sum(jnp.where(chosen_doc, sink_rows[0], 0.0), axis=0, keepdims=True)
            v_row = jnp.sum(jnp.where(chosen_doc, sink_rows[1], 0.0), axis=0, keepdims=True)
            sink_seen = twice(mine[:, 0:1] == segcol[block + WIN][:, 0:1])
            sink = jnp.sum(query * k_row, axis=1, keepdims=True) + sink_bias
            sink = jnp.where(sink_seen, sink, MASKED)
            peak = jnp.maximum(
                jnp.maximum(scores[0], scores[1]), jnp.maximum(scores[2], scores[3])
            )
            peak = jnp.maximum(jnp.max(peak, axis=1, keepdims=True), sink)
            weights = [jnp.exp(score - peak) for score in scores]
            sink_weight = jnp.exp(sink - peak)
            total = (weights[0] + weights[1]) + (weights[2] + weights[3])
            total = jnp.sum(total, axis=1, keepdims=True) + sink_weight
            mixed = sink_weight * v_row
            mixed = mixed + dot(jnp.where(causal, 0.0, weights[0]).astype(BF16), vb[batch, block])
            mixed = mixed + dot(
                jnp.where(causal, weights[0], 0.0).astype(BF16), vb[batch, block + WIN]
            )
            for near in range(1, WIN):
                mixed = mixed + dot(weights[near].astype(BF16), vb[batch, block + near])
            mixed = mixed / total
            ctx_out[batch, block] = jnp.where(
                lane_head[:TOK] == 0, mixed[:TOK], mixed[TOK:]
            ).astype(BF16)

            @pl.when(block == pair)
            def _():
                context_own(batch).start()

            @pl.when(block != pair)
            def _():
                context_copy(batch, block).start()

        def attend_late(turn, carry):
            attend(WIN + lax.rem(pair + turn, WIN))
            return carry

        def attend_early(turn, carry):
            attend(lax.rem(pair + turn, WIN))
            return carry

        lax.fori_loop(0, WIN, attend_late, 0)
        if not opening:
            relay()

        @pl.when(upper == 1)
        def _():
            for kind in range(2):
                halo_hop(batch, kind).wait_recv()

        lax.fori_loop(0, WIN, attend_early, 0)

    def target_of(group, dy, sign):
        y = lax.rem(me_y + EXP_Y + sign * dy, EXP_Y)
        z = lax.rem(me_z + EXP_Z + sign * plane_step(group), EXP_Z)
        return y * EXP_Z + z

    def beside(dy):
        return lax.rem(me_y + dy, EXP_Y) * EXP_Z + me_z

    def dispatch(batch, group, dy):
        slot = group * EXP_Y + dy
        rows = slice(0, SENT[batch])
        return remote(
            sbuf[batch].at[slot, rows],
            rbuf[batch].at[slot, rows],
            go_send.at[batch, slot],
            go_recv.at[batch, slot],
            exp=beside(dy) if batch == 1 else target_of(group, dy, 1),
        )

    def answer(batch, group, dy):
        slot = group * EXP_Y + dy
        rows = slice(0, SENT[batch])
        return remote(
            ybuf[batch].at[slot, rows],
            back[batch].at[slot, rows],
            back_send.at[batch, slot],
            back_recv.at[batch, slot],
            exp=beside(EXP_Y - dy) if batch == 1 else target_of(group, dy, -1),
        )

    gates = [None, None]

    def pick(batch, group, places, source):
        stride = STRIDE[batch]
        spot = (iota((EXP_Y * stride, TOK), 0) + group * EXP_Y * stride).astype(F32)
        hit = (spot == places[0]) | (spot == places[1])
        plan = jnp.where(hit, 1.0, 0.0).astype(BF16)
        if batch == 0:
            hit = (spot == places[0] + CAP) | (spot == places[1] + CAP)
            other = jnp.where(hit, 1.0, 0.0).astype(BF16)
            halves = dot(plan, source[:, : WIDTH[0]]) + dot(other, source[:, WIDTH[0] :])
            sbuf[0][group * EXP_Y : (group + 1) * EXP_Y] = halves.astype(BF16).reshape(
                EXP_Y, stride, WIDTH[0]
            )
            return
        for part in range(2):
            cols = slice(part * 512, (part + 1) * 512)
            sbuf[batch][group * EXP_Y : (group + 1) * EXP_Y, :, cols] = (
                dot(plan, source[:, cols]).astype(BF16).reshape(EXP_Y, stride, 512)
            )

    def spread(group):
        if group > 0:
            place_copies[group - 1].wait_recv()
            for half in range(2):
                if (group, half) not in ((1, 0), (2, 1)):
                    token_copy(group, half).wait_recv()
        places = [place_in[group, c : c + 1, :] for c in range(2)]
        pick(1, group, places, tok_in.at[group])
        for dy in range(1, EXP_Y):
            dispatch(1, group, dy).start()
        rbuf[1][group * EXP_Y] = sbuf[1][group * EXP_Y]

    def front(batch, opening):
        for step in range(1, PAIRS):
            source = lax.rem(pair + step, PAIRS)
            remote(
                ctx_out.at[batch, source],
                ctx_in.at[batch, :, lanes_of(source)],
                ctx_send.at[batch, source],
                ctx_recv.at[batch, source],
                seq=first_of_half + source,
            ).wait_recv()
        context_own(batch).wait()
        if opening:
            for copy in late[:3]:
                copy.wait()
        context = ctx_in[batch]
        for part in range(2):
            cols = slice(part * 512, (part + 1) * 512)
            hidden[batch, :, cols] = tok[batch, 0, :, cols].astype(F32) + dot(
                context, proj[:, cols]
            )
        value = hidden[batch]
        scale = lax.rsqrt(jnp.mean(value * value, axis=1, keepdims=True) + EPSILON)
        rows_value = (value * scale).astype(BF16)
        if batch == 1:
            tok_in[0] = rows_value
            prepare(0, False)
            for group, half in ((1, 0), (2, 1), (1, 1), (2, 0)):
                token_copy(group, half).start()
            find_starts(0)
            spread(0)
            source = tok_in[0]
        else:
            normed[...] = rows_value
            for group in (3, 1, 2, 0):
                pick(batch, group, place_rows[0], normed)
                for dy in range(EXP_Y):
                    if group + dy > 0:
                        dispatch(batch, group, dy).start()
            rbuf[batch][0] = sbuf[batch][0]
            source = normed[...]
        logits = dot_t(source, router[...])
        picked = jnp.sum(differences[batch][:, :N_EXP] * logits, axis=1, keepdims=True)
        first = jax.nn.sigmoid(picked)
        gates[batch] = (first, 1.0 - first)
        if batch == 1:
            for c in range(2):
                gate_out[c : c + 1, :] = jnp.transpose(
                    jnp.broadcast_to(gates[batch][c], (TOK, TOK))
                )[0:1, :]
            gate_in[0] = gate_out[...]
            for copy in gate_copies:
                copy.start()

    def serve_all(batch, low, high):
        stride = STRIDE[batch]
        count = EXP_Y * (stride if batch == 1 else PACK)
        if batch == 0:
            inner_row = iota((PACK, EXP_Y * stride), 0)
            inner_col = iota((PACK, EXP_Y * stride), 1)
            outer_row = iota((stride, EXP_Y * PACK), 0)
            outer_col = iota((stride, EXP_Y * PACK), 1)
            unpack, pack = [], []
            for side in range(2):
                near, far = [], []
                for dy in range(EXP_Y):
                    hit = inner_col == inner_row + (dy * stride + side * CAP)
                    near.append(jnp.where(hit & (inner_row < CAP), 1.0, 0.0))
                    hit = outer_col == outer_row + (dy * PACK - side * CAP)
                    inside = (outer_row >= side * CAP) & (outer_row < (side + 1) * CAP)
                    far.append(jnp.where(hit & inside, 1.0, 0.0))
                unpack.append(jnp.concatenate(near, axis=0).astype(BF16))
                pack.append(jnp.concatenate(far, axis=0).astype(BF16))

        def serve(turn, carry):
            group = lax.rem(turn + 1, EXP_Z)
            for dy in range(EXP_Y):
                if dy == 0 and batch == 1:
                    continue
                if dy == 0:

                    @pl.when(group > 0)
                    def _():
                        dispatch(batch, group, dy).wait_recv()

                else:
                    dispatch(batch, group, dy).wait_recv()
            arrived = rbuf[batch][pl.ds(group * EXP_Y, EXP_Y)].reshape(
                EXP_Y * stride, WIDTH[batch]
            )
            if batch == 0:
                inputs = jnp.concatenate(
                    [dot(unpack[side], arrived).astype(BF16) for side in range(2)], axis=1
                )
            else:
                inputs = arrived
            for low, high in ((0, 512), (512, 1024), (1024, FFW)):
                gate = dot(inputs, gate_w[:, low:high])
                up = dot(inputs, up_w[:, low:high])
                inner = 0.7978845608028654 * (gate + 0.044715 * (gate * gate * gate))
                active[0:count, low:high] = (0.5 * gate * (1.0 + jnp.tanh(inner)) * up).astype(
                    BF16
                )
            if batch == 0:
                outs = [
                    dot(active[0:count], down_w[:, side * 512 : (side + 1) * 512]).astype(BF16)
                    for side in range(2)
                ]
                halves = dot(pack[0], outs[0]) + dot(pack[1], outs[1])
                ybuf[0][pl.ds(group * EXP_Y, EXP_Y)] = halves.astype(BF16).reshape(
                    EXP_Y, stride, WIDTH[0]
                )
            for part in range(2 * batch):
                cols = slice(part * 512, (part + 1) * 512)
                ybuf[batch][pl.ds(group * EXP_Y, EXP_Y), :, cols] = (
                    dot(active[0:count], down_w[:, cols])
                    .astype(BF16)
                    .reshape(EXP_Y, stride, 512)
                )
            for dy in range(EXP_Y):
                if dy == 0 and batch == 1:
                    back[1][group * EXP_Y] = ybuf[1][group * EXP_Y]
                elif dy == 0:

                    @pl.when(group > 0)
                    def _():
                        answer(batch, group, dy).start()

                else:
                    answer(batch, group, dy).start()
            return carry

        lax.fori_loop(low, high, serve, 0)
        if batch == 0 and high == EXP_Z:
            back[batch][0] = ybuf[batch][0]

    def blend(batch, group, places, weights):
        stride = STRIDE[batch]
        spot = (iota((TOK, EXP_Y * stride), 1) + group * EXP_Y * stride).astype(F32)
        shifts = (0, CAP) if batch == 0 else (0,)
        terms = []
        for shift in shifts:
            mix = jnp.where(spot == places[0] + shift, weights[0], 0.0) + jnp.where(
                spot == places[1] + shift, weights[1], 0.0
            )
            coarse = mix.astype(BF16)
            terms += [coarse, (mix - coarse.astype(F32)).astype(BF16)]
        rows = back[batch][group * EXP_Y : (group + 1) * EXP_Y].reshape(
            EXP_Y * stride, WIDTH[batch]
        )
        both = dot(jnp.concatenate(terms, axis=0), rows)
        sums = [
            both[2 * side * TOK : (2 * side + 1) * TOK]
            + both[(2 * side + 1) * TOK : (2 * side + 2) * TOK]
            for side in range(len(shifts))
        ]
        return sums[0] if batch == 1 else jnp.concatenate(sums, axis=1)

    def plane_sum(group):
        for dy in range(1, EXP_Y):
            answer(1, group, dy).wait_recv()
        if group == 0:
            return blend(1, 0, place_cols[1], gates[1])
        gate_copies[group - 1].wait_recv()
        places = [turned(place_in[group, c : c + 1, :])[:, 0:1] for c in range(2)]
        weights = [turned(gate_in[group, c : c + 1, :])[:, 0:1] for c in range(2)]
        return blend(1, group, places, weights)

    half_rows = (slice(0, TOK // 2), slice(TOK // 2, TOK))

    def plane_sums():
        part_out[3] = plane_sum(3).astype(BF16)
        for half in range(2):
            far_copy(half).start()
        for group in (1, 2):
            total = plane_sum(group)
            near, far = half_rows[group - 1], half_rows[2 - group]
            part_out[group, far] = total[far].astype(BF16)
            part_copy(group, 2 - group).start()
            hidden_part[group - 1] = total[near]

    def pass_on():
        for group in (1, 2):
            near = half_rows[group - 1]
            far_copy(group - 1).wait_recv()
            total = hidden_part[group - 1] + red_in[group - 1].astype(F32)
            part_out[group, near] = total.astype(BF16)
            part_copy(group, group - 1).start()

    def finish_one():
        result = hidden[0]
        for group in range(EXP_Z):
            for dy in range(EXP_Y):
                if group + dy > 0:
                    answer(0, group, dy).wait_recv()
            result = result + blend(0, group, place_cols[0], gates[0])
        out_ref[0, 0] = result.astype(BF16)

    def finish_two():
        result = hidden[1] + plane_sum(0)
        for group in (1, 2):
            for half in range(2):
                part_copy(group, half).wait_recv()
        result = result + part_in[1].astype(F32) + part_in[2].astype(F32)
        out_ref[1, 0] = result.astype(BF16)

    prepare(1, True)
    find_starts(1)
    attention(1, True)
    front(1, True)
    attention(0, False)
    spread(1)
    spread(2)
    front(0, False)
    spread(3)
    for copy in late[3:]:
        copy.wait()
    serve_all(1, 0, EXP_Z)
    plane_sums()
    serve_all(0, 0, 2)
    pass_on()
    serve_all(0, 2, EXP_Z)
    finish_one()
    finish_two()

    for batch in range(2):
        for group in range(EXP_Z):
            for dy in range(EXP_Y):
                if dy > 0 or (batch == 0 and group > 0):
                    dispatch(batch, group, dy).wait_send()
                    answer(batch, group, dy).wait_send()
        for step in range(1, PAIRS):
            context_copy(batch, lax.rem(pair + step, PAIRS)).wait_send()

    for group in range(1, EXP_Z):
        place_copies[group - 1].wait_send()
        gate_copies[group - 1].wait_send()
        for half in range(2):
            token_copy(group, half).wait_send()
            if group < 3:
                part_copy(group, half).wait_send()
    for half in range(2):
        far_copy(half).wait_send()

    @pl.when(upper == 0)
    def _():
        seg_hop.wait_send()
        for batch in range(2):
            sink_hop(batch).wait_send()
            for kind in range(2):
                halo_hop(batch, kind).wait_send()


def local(
    tokens,
    queries,
    key_rows,
    value_rows,
    segments,
    bias_table,
    out_proj,
    router,
    gate_weight,
    up_weight,
    down_weight,
    old_table,
    new_table,
    routes_one,
    routes_two,
):
    any_spec = pl.BlockSpec(memory_space=pl.ANY)
    vmem = pltpu.VMEM
    dma = pltpu.SemaphoreType.DMA
    buffers = [vmem((N_EXP, stride, width), BF16) for stride, width in zip(STRIDE, WIDTH)]
    return pl.pallas_call(
        layer_kernel,
        out_shape=jax.ShapeDtypeStruct((2, 1, TOK, D), BF16),
        in_specs=[any_spec] * 15,
        out_specs=pl.BlockSpec(memory_space=pltpu.VMEM),
        scratch_shapes=[
            vmem((N_EXP, NBUCK), F32),
            vmem((2, 2, TOK), I32),
            vmem((2, 1, N_EXP), I32),
            vmem((2, LANES), I32),
            vmem((N_EXP, D), BF16),
            vmem((2, 1, TOK, D), BF16),
            vmem((D, D), BF16),
            vmem((D, FFW), BF16),
            vmem((D, FFW), BF16),
            vmem((FFW, D), BF16),
            vmem((2, N_SEQ, 1, TOK), I32),
            vmem((2, PAIRS, TOK, LANES), BF16),
            vmem((2, PAIRS + WIN, TOK, LANES), BF16),
            vmem((2, PAIRS + WIN, TOK, LANES), BF16),
            vmem((N_SEQ, TOK, TOK), I32),
            vmem((WIN, 2 * TOK, TOK), F32),
            vmem((2, 2, 8, LANES), F32),
            vmem((2, 2, 8, LANES), F32),
            vmem((2, 8, LANES), F32),
            vmem((2, PAIRS, TOK, LANES), BF16),
            vmem((2, TOK, D), BF16),
            vmem((2, TOK, D), F32),
            vmem((TOK, D), BF16),
            *buffers,
            *buffers,
            *buffers,
            *buffers,
            vmem((EXP_Y * STRIDE[1], FFW), BF16),
            dma((11,)),
            dma((2, 3, PAIRS)),
            dma((2, 3, PAIRS)),
            dma((2, 3)),
            dma((PAIRS,)),
            dma((PAIRS,)),
            dma(()),
            dma((5,)),
            dma((5,)),
            dma((2,)),
            dma((2,)),
            dma((2, PAIRS)),
            dma((2, PAIRS)),
            dma((2,)),
            dma((2, N_EXP)),
            dma((2, N_EXP)),
            dma((2, N_EXP)),
            dma((2, N_EXP)),
            vmem((EXP_Z, TOK, D), BF16),
            vmem((EXP_Z, 2, TOK), F32),
            vmem((2, TOK), F32),
            dma((EXP_Z, 2)),
            dma((EXP_Z, 2)),
            dma((EXP_Z,)),
            dma((EXP_Z,)),
            vmem((EXP_Z, 2, TOK), F32),
            vmem((2, TOK), F32),
            dma((EXP_Z,)),
            dma((EXP_Z,)),
            vmem((EXP_Z, TOK, D), BF16),
            vmem((EXP_Z, TOK, D), BF16),
            vmem((2, TOK // 2, D), BF16),
            dma((EXP_Z, 2)),
            dma((EXP_Z, 2)),
            dma((2,)),
            dma((2,)),
            vmem((2, TOK // 2, D), F32),
        ],
        compiler_params=pltpu.CompilerParams(
            collective_id=0, has_side_effects=True, vmem_limit_bytes=56 << 20
        ),
        name="layer",
    )(
        bias_table,
        segments,
        queries,
        key_rows,
        value_rows,
        tokens,
        out_proj,
        router.T,
        jnp.swapaxes(routes_one, 1, 2),
        jnp.swapaxes(routes_two, 1, 2),
        old_table[None],
        new_table[None],
        gate_weight,
        up_weight,
        down_weight,
    )


def solution(mesh):
    placed = (
        P(None, "exp", "seq", None),
        P(None, "exp", "seq", None),
        P(None, "exp", "seq", None),
        P(None, "exp", "seq", None),
        P(None, "exp", "seq"),
        P(),
        P(),
        P(),
        P("exp", None, None),
        P("exp", None, None),
        P("exp", None, None),
        P(),
        P(),
        P("exp", "seq", None),
        P("exp", "seq", None),
    )
    return jax.shard_map(
        local, mesh=mesh, in_specs=placed, out_specs=P(None, "exp", "seq", None), check_vma=False
    )
```

```python
import jax
import jax.numpy as jnp
from jax import lax
from jax.experimental import pallas as pl
from jax.experimental.pallas import tpu as pltpu
from jax.sharding import PartitionSpec as P

MESH = pl.DeviceIdType.MESH
BF16 = jnp.bfloat16
F32 = jnp.float32
I32 = jnp.int32

N_SEQ = 16
N_EXP = 16
EXP_Y = 4
EXP_Z = 4
TOK = 128
D = 1024
FFW = 1408
NBUCK = 32
WIN = 4
PAIRS = 8
LANES = 128
HALF = 64
CAP = 20
STRIDE = (48, 48)
SENT = (40, 40)
WIDTH = (512, 1024)
PACK = 32
SINK_BUCKET = 31

EPSILON = 1e-06
MASKED = -1e30


def iota(shape, dim):
    return lax.broadcasted_iota(I32, shape, dim)


def dot(a, b):
    return jnp.dot(a, b, preferred_element_type=F32)


def dot_t(a, b):
    return lax.dot_general(a, b, (((1,), (1,)), ((), ())), preferred_element_type=F32)


def turned(row):
    return jnp.transpose(jnp.broadcast_to(row, (LANES, LANES)))


def remote(src, dst, send, recv, **device):
    return pltpu.make_async_remote_copy(
        src_ref=src,
        dst_ref=dst,
        send_sem=send,
        recv_sem=recv,
        device_id=device,
        device_id_type=MESH,
    )


def bias_of_distance(distance, values):
    result = jnp.broadcast_to(values[0], distance.shape)
    for bucket in range(1, 10):
        result = jnp.where(distance >= (1 << (bucket - 1)), values[bucket], result)
    return result


def plane_step(group):
    return group + (group // 2) * (1 - 2 * lax.rem(group, 2))


def layer_kernel(
    bias_hbm,
    seg_hbm,
    q_hbm,
    k_hbm,
    v_hbm,
    tok_hbm,
    proj_hbm,
    router_hbm,
    one_hbm,
    two_hbm,
    old_hbm,
    new_hbm,
    gate_hbm,
    up_hbm,
    down_hbm,
    out_ref,
    table,
    routes,
    held,
    tabs,
    router,
    tok,
    proj,
    gate_w,
    up_w,
    down_w,
    segs,
    qb,
    kb,
    vb,
    segcol,
    bias,
    sink_out,
    sink_in,
    sink_rows,
    ctx_out,
    ctx_in,
    hidden,
    normed,
    sbuf_one,
    sbuf_two,
    rbuf_one,
    rbuf_two,
    ybuf_one,
    ybuf_two,
    back_one,
    back_two,
    active,
    load_sem,
    qkv_send,
    qkv_recv,
    qkv_own,
    seg_send,
    seg_recv,
    seg_own,
    hop_send,
    hop_recv,
    sink_send,
    sink_recv,
    ctx_send,
    ctx_recv,
    ctx_own,
    go_send,
    go_recv,
    back_send,
    back_recv,
    tok_in,
    place_in,
    place_out,
    tok_send,
    tok_recv,
    place_send,
    place_recv,
    gate_in,
    gate_out,
    gate_send,
    gate_recv,
    part_out,
    part_in,
    red_in,
    part_send,
    part_recv,
    red_send,
    red_recv,
    hidden_part,
):
    me = lax.axis_index("seq")
    my_exp = lax.axis_index("exp")
    upper, pair = me // PAIRS, lax.rem(me, PAIRS)
    me_y, me_z = my_exp // EXP_Z, lax.rem(my_exp, EXP_Z)
    first_of_half = upper * PAIRS
    across = lax.rem(me + PAIRS, N_SEQ)
    sbuf, rbuf = (sbuf_one, sbuf_two), (rbuf_one, rbuf_two)
    ybuf, back = (ybuf_one, ybuf_two), (back_one, back_two)

    early = [
        pltpu.make_async_copy(src, dst, load_sem.at[i])
        for i, (src, dst) in enumerate(
            (
                (old_hbm, held.at[0]),
                (new_hbm, held.at[1]),
                (one_hbm.at[0], routes.at[0]),
                (two_hbm.at[0], routes.at[1]),
                (bias_hbm, table),
            )
        )
    ]
    late = [
        pltpu.make_async_copy(src, dst, load_sem.at[i + 5])
        for i, (src, dst) in enumerate(
            (
                (router_hbm, router),
                (tok_hbm, tok),
                (proj_hbm, proj),
                (gate_hbm.at[0], gate_w),
                (up_hbm.at[0], up_w),
                (down_hbm.at[0], down_w),
            )
        )
    ]
    for copy in early:
        copy.start()

    for batch in range(2):
        low = STRIDE[batch] - 16
        back[batch][:, low:, :] = jnp.zeros((N_EXP, 16, WIDTH[batch]), BF16)
    rbuf[0][:, STRIDE[0] - 16 :, :] = jnp.zeros((N_EXP, 16, WIDTH[0]), BF16)

    @pl.when(upper == 0)
    def _():
        for batch in range(2):
            kb[batch, 0:WIN] = jnp.zeros((WIN, TOK, LANES), BF16)
            vb[batch, 0:WIN] = jnp.zeros((WIN, TOK, LANES), BF16)
            segs[batch, 0:PAIRS] = jnp.full((PAIRS, 1, TOK), -1, I32)
            sink_in[batch] = jnp.zeros((2, 8, LANES), F32)

    barrier = pltpu.get_barrier_semaphore()
    for step in range(1, PAIRS):
        pl.semaphore_signal(
            barrier,
            inc=1,
            device_id={"seq": first_of_half + lax.rem(pair + step, PAIRS)},
            device_id_type=MESH,
        )
    pl.semaphore_signal(barrier, inc=1, device_id={"seq": across}, device_id_type=MESH)
    for step in range(1, N_EXP):
        pl.semaphore_signal(
            barrier,
            inc=1,
            device_id={"exp": lax.rem(my_exp + step, N_EXP)},
            device_id_type=MESH,
        )
    pl.semaphore_wait(barrier, PAIRS + N_EXP - 1)

    def lanes_of(which):
        return pl.ds(pl.multiple_of(which * LANES, LANES), LANES)

    def qkv_parts(batch, target):
        lanes = lanes_of(target)
        return (
            (k_hbm.at[batch, 0, :, lanes], kb.at[batch, pair + WIN]),
            (v_hbm.at[batch, 0, :, lanes], vb.at[batch, pair + WIN]),
            (q_hbm.at[batch, 0, :, lanes], qb.at[batch, pair]),
        )

    def qkv_copies(batch):
        copies = []
        for step in range(1, PAIRS):
            target = lax.rem(pair + step, PAIRS)
            for kind, (src, dst) in enumerate(qkv_parts(batch, target)):
                copies.append(
                    remote(
                        src,
                        dst,
                        qkv_send.at[batch, kind, step],
                        qkv_recv.at[batch, kind, step],
                        seq=first_of_half + target,
                    )
                )
        for kind, (src, dst) in enumerate(qkv_parts(batch, pair)):
            copies.append(pltpu.make_async_copy(src, dst, qkv_own.at[batch, kind]))
        return copies

    qkv = [qkv_copies(batch) for batch in range(2)]
    seg_copies = [
        remote(
            seg_hbm,
            segs.at[:, PAIRS + pair],
            seg_send.at[step],
            seg_recv.at[step],
            seq=first_of_half + lax.rem(pair + step, PAIRS),
        )
        for step in range(1, PAIRS)
    ]
    seg_copies.append(pltpu.make_async_copy(seg_hbm, segs.at[:, PAIRS + pair], seg_own))
    seg_hop = remote(
        segs.at[:, PAIRS : 2 * PAIRS],
        segs.at[:, 0:PAIRS],
        hop_send.at[4],
        hop_recv.at[4],
        seq=across,
    )

    def halo_hop(batch, kind):
        block = (kb, vb)[kind]
        return remote(
            block.at[batch, PAIRS : PAIRS + WIN],
            block.at[batch, 0:WIN],
            hop_send.at[2 * batch + kind],
            hop_recv.at[2 * batch + kind],
            seq=across,
        )

    def sink_hop(batch):
        return remote(
            sink_out.at[batch],
            sink_in.at[batch],
            sink_send.at[batch],
            sink_recv.at[batch],
            seq=across,
        )

    for copy in seg_copies:
        copy.start()
    for copy in qkv[1]:
        copy.start()
    for copy in late:
        copy.start()
    for copy in early:
        copy.wait()

    qi = iota((TOK, TOK), 0)
    kj = iota((TOK, TOK), 1)
    for head in range(2):
        head_row = table[pl.ds(2 * pair + head, 1), :]
        values = [head_row[:, bucket : bucket + 1] for bucket in range(10)]
        rows = slice(head * TOK, (head + 1) * TOK)
        merged = jnp.where(kj <= qi, qi - kj, qi - kj + WIN * TOK)
        bias[0, rows, :] = bias_of_distance(merged, values)
        for block in range(1, WIN):
            bias[block, rows, :] = bias_of_distance(qi - kj + (WIN - block) * TOK, values)
    sink_bias = jnp.where(
        iota((2 * TOK, 1), 0) < TOK,
        table[pl.ds(2 * pair, 1), :][:, SINK_BUCKET : SINK_BUCKET + 1],
        table[pl.ds(2 * pair + 1, 1), :][:, SINK_BUCKET : SINK_BUCKET + 1],
    )

    lane = iota((LANES, LANES), 1)
    row = iota((LANES, LANES), 0)
    tabs[...] = jnp.full((2, LANES), -1, I32)
    tabs[0:1, 0:N_EXP] = held[0]
    tabs[1:2, 0:N_EXP] = held[1]
    steps_y = lax.rem(row // EXP_Z - me_y + 2 * EXP_Y * EXP_Y, EXP_Y)
    steps_z = lax.rem(lax.rem(row, EXP_Z) - me_z + EXP_Z, EXP_Z)
    groups = steps_z + (steps_z // 2) * (1 - 2 * lax.rem(steps_z, 2))
    slot_of_row = (groups * EXP_Y + steps_y).astype(F32)
    holds = turned(tabs[0:1, :]) == lane
    slot_of_expert = jnp.sum(jnp.where(holds, slot_of_row, 0.0), axis=0, keepdims=True)
    new_row = tabs[1:2, :]
    new_col = turned(new_row)
    served = new_col == lane
    serving = jnp.where(served, 1.0, 0.0).astype(BF16)
    slot_two = jnp.sum(jnp.where(served, slot_of_expert, 0.0), axis=1, keepdims=True)
    again = jnp.where((new_col == new_row) & (lane < row), 1.0, 0.0)
    again = jnp.sum(again, axis=1, keepdims=True)
    base_two = jnp.transpose(
        jnp.broadcast_to(slot_two * STRIDE[1] + again * CAP, (LANES, LANES))
    )[0:1, :]
    bases = (slot_of_expert * STRIDE[0], base_two)
    lower = jnp.where(row > lane, 1.0, 0.0).astype(BF16)
    place_cols, place_rows, differences = [], [], []
    for batch in range(2):
        member = [
            jnp.where(turned(routes[batch, c : c + 1, :]) == lane, 1.0, 0.0) for c in range(2)
        ]
        counts = [dot(lower, m.astype(BF16)) for m in member]
        counts[1] = counts[1] + jnp.sum(member[0], axis=0, keepdims=True)
        cols = [
            jnp.sum(m * (c + bases[batch]), axis=1, keepdims=True)
            for m, c in zip(member, counts)
        ]
        place_cols.append(cols)
        place_rows.append(
            [jnp.transpose(jnp.broadcast_to(col, (TOK, TOK)))[0:1, :] for col in cols]
        )
        difference = member[0] - member[1]
        if batch == 1:
            difference = dot(difference.astype(BF16), serving)
        differences.append(difference)
    for c in range(2):
        place_out[c : c + 1, :] = place_rows[1][c]
    place_in[0] = place_out[...]

    def plane(step):
        return me_y * EXP_Z + lax.rem(me_z + step, EXP_Z)

    place_copies = [
        remote(
            place_out,
            place_in.at[group],
            place_send.at[group],
            place_recv.at[group],
            exp=plane(step),
        )
        for group, step in ((1, 1), (2, 3), (3, 2))
    ]
    for copy in place_copies:
        copy.start()
    gate_copies = [
        remote(
            gate_out,
            gate_in.at[group],
            gate_send.at[group],
            gate_recv.at[group],
            exp=plane(step),
        )
        for group, step in ((1, 1), (2, 3), (3, 2))
    ]

    def part_copy(group, half):
        rows = slice(half * (TOK // 2), (half + 1) * (TOK // 2))
        return remote(
            part_out.at[group, rows],
            part_in.at[group, rows],
            part_send.at[group, half],
            part_recv.at[group, half],
            exp=plane((3, 1)[group - 1]),
        )

    def far_copy(half):
        rows = slice(half * (TOK // 2), (half + 1) * (TOK // 2))
        return remote(
            part_out.at[3, rows],
            red_in.at[half],
            red_send.at[half],
            red_recv.at[half],
            exp=plane((3, 1)[half]),
        )

    def token_copy(group, half):
        rows = slice(half * (TOK // 2), (half + 1) * (TOK // 2))
        origin = 1 + half if group == 3 else 0
        step = (1, 3)[half] if group == 3 else (1, 3)[group - 1]
        return remote(
            tok_in.at[origin, rows],
            tok_in.at[group, rows],
            tok_send.at[group, half],
            tok_recv.at[group, half],
            exp=plane(step),
        )

    def relay():
        for half in range(2):
            token_copy(1 + half, half).wait_recv()
            token_copy(3, half).start()

    lane_head = iota((2 * TOK, LANES), 1) // HALF
    row_head = iota((2 * TOK, LANES), 0) // TOK
    own_half = lane_head == row_head
    causal = lax.rem(iota((2 * TOK, TOK), 0), TOK) >= iota((2 * TOK, TOK), 1)

    def twice(value):
        return jnp.concatenate([value, value], axis=0)

    def context_copy(batch, block):
        return remote(
            ctx_out.at[batch, block],
            ctx_in.at[batch, :, lanes_of(pair)],
            ctx_send.at[batch, block],
            ctx_recv.at[batch, pair],
            seq=first_of_half + block,
        )

    def context_own(batch):
        return pltpu.make_async_copy(
            ctx_out.at[batch, pair], ctx_in.at[batch, :, lanes_of(pair)], ctx_own.at[batch]
        )

    def prepare(batch, opening):
        if opening:
            for copy in seg_copies:
                copy.wait()

            @pl.when(upper == 0)
            def _():
                seg_hop.start()

        for copy in qkv[batch]:
            copy.wait()

        @pl.when(upper == 0)
        def _():
            for kind in range(2):
                halo_hop(batch, kind).start()

        if opening:
            for copy in qkv[0]:
                copy.start()

            @pl.when(upper == 1)
            def _():
                seg_hop.wait_recv()

    def find_starts(batch):
        def columns(block, before):
            line = segs[batch, block]
            segcol[block] = turned(line)
            document = iota((8, TOK), 0)
            return before + jnp.where((line < document) & (line >= 0), 1, 0)

        ahead = lax.fori_loop(0, 2 * PAIRS, columns, jnp.zeros((8, TOK), I32))
        starts = jnp.sum(ahead, axis=1, keepdims=True)

        def sinks(block, sums):
            k_sum, v_sum = sums
            spot = (upper * PAIRS + block) * TOK + iota((8, TOK), 1)
            pick = jnp.where(spot == starts, 1.0, 0.0).astype(BF16)
            return (
                k_sum + dot(pick, kb[batch, block + WIN]),
                v_sum + dot(pick, vb[batch, block + WIN]),
            )

        zero = jnp.zeros((8, LANES), F32)
        k_sink, v_sink = lax.fori_loop(0, PAIRS, sinks, (zero, zero))
        sink_out[batch, 0] = k_sink
        sink_out[batch, 1] = v_sink

        @pl.when(upper == 0)
        def _():
            sink_hop(batch).start()

    def attention(batch, opening):
        @pl.when(upper == 1)
        def _():
            sink_hop(batch).wait_recv()

        sink_rows[0] = sink_out[batch, 0] + sink_in[batch, 0]
        sink_rows[1] = sink_out[batch, 1] + sink_in[batch, 1]

        def attend(block):
            query = twice(qb[batch, block].astype(F32) * 0.125)
            query = jnp.where(own_half, query, 0.0)
            query_rows = query.astype(BF16)
            mine = segcol[block + PAIRS]
            pieces = []
            for near in range(WIN + 1):
                raw = dot_t(query_rows, kb[batch, block + near])
                same = twice(mine == segs[batch, block + near + WIN])
                pieces.append((raw, same))
            merged = jnp.where(causal, pieces[WIN][0], pieces[0][0])
            merged_same = jnp.where(
                causal, pieces[WIN][1].astype(I32), pieces[0][1].astype(I32)
            )
            scores = [jnp.where(merged_same > 0, merged + bias[0], MASKED)]
            for near in range(1, WIN):
                raw, same = pieces[near]
                scores.append(jnp.where(same, raw + bias[near], MASKED))
            chosen_doc = iota((8, LANES), 0) == segs[batch, block + PAIRS][:, 0:1]
            k_row = jnp.sum(jnp.where(chosen_doc, sink_rows[0], 0.0), axis=0, keepdims=True)
            v_row = jnp.sum(jnp.where(chosen_doc, sink_rows[1], 0.0), axis=0, keepdims=True)
            sink_seen = twice(mine[:, 0:1] == segcol[block + WIN][:, 0:1])
            sink = jnp.sum(query * k_row, axis=1, keepdims=True) + sink_bias
            sink = jnp.where(sink_seen, sink, MASKED)
            peak = jnp.maximum(
                jnp.maximum(scores[0], scores[1]), jnp.maximum(scores[2], scores[3])
            )
            peak = jnp.maximum(jnp.max(peak, axis=1, keepdims=True), sink)
            weights = [jnp.exp(score - peak) for score in scores]
            sink_weight = jnp.exp(sink - peak)
            total = (weights[0] + weights[1]) + (weights[2] + weights[3])
            total = jnp.sum(total, axis=1, keepdims=True) + sink_weight
            mixed = sink_weight * v_row
            mixed = mixed + dot(jnp.where(causal, 0.0, weights[0]).astype(BF16), vb[batch, block])
            mixed = mixed + dot(
                jnp.where(causal, weights[0], 0.0).astype(BF16), vb[batch, block + WIN]
            )
            for near in range(1, WIN):
                mixed = mixed + dot(weights[near].astype(BF16), vb[batch, block + near])
            mixed = mixed / total
            ctx_out[batch, block] = jnp.where(
                lane_head[:TOK] == 0, mixed[:TOK], mixed[TOK:]
            ).astype(BF16)

            @pl.when(block == pair)
            def _():
                context_own(batch).start()

            @pl.when(block != pair)
            def _():
                context_copy(batch, block).start()

        def attend_late(turn, carry):
            attend(WIN + lax.rem(pair + turn, WIN))
            return carry

        def attend_early(turn, carry):
            attend(lax.rem(pair + turn, WIN))
            return carry

        lax.fori_loop(0, WIN, attend_late, 0)
        if not opening:
            relay()

        @pl.when(upper == 1)
        def _():
            for kind in range(2):
                halo_hop(batch, kind).wait_recv()

        lax.fori_loop(0, WIN, attend_early, 0)

    def target_of(group, dy, sign):
        y = lax.rem(me_y + EXP_Y + sign * dy, EXP_Y)
        z = lax.rem(me_z + EXP_Z + sign * plane_step(group), EXP_Z)
        return y * EXP_Z + z

    def beside(dy):
        return lax.rem(me_y + dy, EXP_Y) * EXP_Z + me_z

    def dispatch(batch, group, dy):
        slot = group * EXP_Y + dy
        rows = slice(0, SENT[batch])
        return remote(
            sbuf[batch].at[slot, rows],
            rbuf[batch].at[slot, rows],
            go_send.at[batch, slot],
            go_recv.at[batch, slot],
            exp=beside(dy) if batch == 1 else target_of(group, dy, 1),
        )

    def answer(batch, group, dy):
        slot = group * EXP_Y + dy
        rows = slice(0, SENT[batch])
        return remote(
            ybuf[batch].at[slot, rows],
            back[batch].at[slot, rows],
            back_send.at[batch, slot],
            back_recv.at[batch, slot],
            exp=beside(EXP_Y - dy) if batch == 1 else target_of(group, dy, -1),
        )

    gates = [None, None]

    def pick(batch, group, places, source):
        stride = STRIDE[batch]
        spot = (iota((EXP_Y * stride, TOK), 0) + group * EXP_Y * stride).astype(F32)
        hit = (spot == places[0]) | (spot == places[1])
        plan = jnp.where(hit, 1.0, 0.0).astype(BF16)
        if batch == 0:
            hit = (spot == places[0] + CAP) | (spot == places[1] + CAP)
            other = jnp.where(hit, 1.0, 0.0).astype(BF16)
            halves = dot(plan, source[:, : WIDTH[0]]) + dot(other, source[:, WIDTH[0] :])
            sbuf[0][group * EXP_Y : (group + 1) * EXP_Y] = halves.astype(BF16).reshape(
                EXP_Y, stride, WIDTH[0]
            )
            return
        for part in range(2):
            cols = slice(part * 512, (part + 1) * 512)
            sbuf[batch][group * EXP_Y : (group + 1) * EXP_Y, :, cols] = (
                dot(plan, source[:, cols]).astype(BF16).reshape(EXP_Y, stride, 512)
            )

    def spread(group):
        if group > 0:
            place_copies[group - 1].wait_recv()
            for half in range(2):
                if (group, half) not in ((1, 0), (2, 1)):
                    token_copy(group, half).wait_recv()
        places = [place_in[group, c : c + 1, :] for c in range(2)]
        pick(1, group, places, tok_in.at[group])
        for dy in range(1, EXP_Y):
            dispatch(1, group, dy).start()
        rbuf[1][group * EXP_Y] = sbuf[1][group * EXP_Y]

    def front(batch, opening):
        for step in range(1, PAIRS):
            source = lax.rem(pair + step, PAIRS)
            remote(
                ctx_out.at[batch, source],
                ctx_in.at[batch, :, lanes_of(source)],
                ctx_send.at[batch, source],
                ctx_recv.at[batch, source],
                seq=first_of_half + source,
            ).wait_recv()
        context_own(batch).wait()
        if opening:
            for copy in late[:3]:
                copy.wait()
        context = ctx_in[batch]
        for part in range(2):
            cols = slice(part * 512, (part + 1) * 512)
            hidden[batch, :, cols] = tok[batch, 0, :, cols].astype(F32) + dot(
                context, proj[:, cols]
            )
        value = hidden[batch]
        scale = lax.rsqrt(jnp.mean(value * value, axis=1, keepdims=True) + EPSILON)
        rows_value = (value * scale).astype(BF16)
        if batch == 1:
            tok_in[0] = rows_value
            prepare(0, False)
            find_starts(0)
            for group, half in ((1, 0), (2, 1), (1, 1), (2, 0)):
                token_copy(group, half).start()
            spread(0)
            source = tok_in[0]
        else:
            normed[...] = rows_value
            for group in (3, 1, 2, 0):
                pick(batch, group, place_rows[0], normed)
                for dy in range(EXP_Y):
                    if group + dy > 0:
                        dispatch(batch, group, dy).start()
            rbuf[batch][0] = sbuf[batch][0]
            source = normed[...]
        logits = dot_t(source, router[...])
        picked = jnp.sum(differences[batch][:, :N_EXP] * logits, axis=1, keepdims=True)
        first = jax.nn.sigmoid(picked)
        gates[batch] = (first, 1.0 - first)
        if batch == 1:
            for c in range(2):
                gate_out[c : c + 1, :] = jnp.transpose(
                    jnp.broadcast_to(gates[batch][c], (TOK, TOK))
                )[0:1, :]
            gate_in[0] = gate_out[...]
            for copy in gate_copies:
                copy.start()

    def serve_all(batch, low, high):
        stride = STRIDE[batch]
        count = EXP_Y * (stride if batch == 1 else PACK)
        if batch == 0:
            inner_row = iota((PACK, EXP_Y * stride), 0)
            inner_col = iota((PACK, EXP_Y * stride), 1)
            outer_row = iota((stride, EXP_Y * PACK), 0)
            outer_col = iota((stride, EXP_Y * PACK), 1)
            unpack, pack = [], []
            for side in range(2):
                near, far = [], []
                for dy in range(EXP_Y):
                    hit = inner_col == inner_row + (dy * stride + side * CAP)
                    near.append(jnp.where(hit & (inner_row < CAP), 1.0, 0.0))
                    hit = outer_col == outer_row + (dy * PACK - side * CAP)
                    inside = (outer_row >= side * CAP) & (outer_row < (side + 1) * CAP)
                    far.append(jnp.where(hit & inside, 1.0, 0.0))
                unpack.append(jnp.concatenate(near, axis=0).astype(BF16))
                pack.append(jnp.concatenate(far, axis=0).astype(BF16))

        def serve(turn, carry):
            group = lax.rem(turn + 1, EXP_Z)
            for dy in range(EXP_Y):
                if dy == 0 and batch == 1:
                    continue
                if dy == 0:

                    @pl.when(group > 0)
                    def _():
                        dispatch(batch, group, dy).wait_recv()

                else:
                    dispatch(batch, group, dy).wait_recv()
            arrived = rbuf[batch][pl.ds(group * EXP_Y, EXP_Y)].reshape(
                EXP_Y * stride, WIDTH[batch]
            )
            if batch == 0:
                inputs = jnp.concatenate(
                    [dot(unpack[side], arrived).astype(BF16) for side in range(2)], axis=1
                )
            else:
                inputs = arrived
            for low, high in ((0, 512), (512, 1024), (1024, FFW)):
                gate = dot(inputs, gate_w[:, low:high])
                up = dot(inputs, up_w[:, low:high])
                inner = 0.7978845608028654 * (gate + 0.044715 * (gate * gate * gate))
                active[0:count, low:high] = (0.5 * gate * (1.0 + jnp.tanh(inner)) * up).astype(
                    BF16
                )
            if batch == 0:
                outs = [
                    dot(active[0:count], down_w[:, side * 512 : (side + 1) * 512]).astype(BF16)
                    for side in range(2)
                ]
                halves = dot(pack[0], outs[0]) + dot(pack[1], outs[1])
                ybuf[0][pl.ds(group * EXP_Y, EXP_Y)] = halves.astype(BF16).reshape(
                    EXP_Y, stride, WIDTH[0]
                )
            for part in range(2 * batch):
                cols = slice(part * 512, (part + 1) * 512)
                ybuf[batch][pl.ds(group * EXP_Y, EXP_Y), :, cols] = (
                    dot(active[0:count], down_w[:, cols])
                    .astype(BF16)
                    .reshape(EXP_Y, stride, 512)
                )
            for dy in range(EXP_Y):
                if dy == 0 and batch == 1:
                    back[1][group * EXP_Y] = ybuf[1][group * EXP_Y]
                elif dy == 0:

                    @pl.when(group > 0)
                    def _():
                        answer(batch, group, dy).start()

                else:
                    answer(batch, group, dy).start()
            return carry

        lax.fori_loop(low, high, serve, 0)
        if batch == 0 and high == EXP_Z:
            back[batch][0] = ybuf[batch][0]

    def blend(batch, group, places, weights):
        stride = STRIDE[batch]
        spot = (iota((TOK, EXP_Y * stride), 1) + group * EXP_Y * stride).astype(F32)
        shifts = (0, CAP) if batch == 0 else (0,)
        terms = []
        for shift in shifts:
            mix = jnp.where(spot == places[0] + shift, weights[0], 0.0) + jnp.where(
                spot == places[1] + shift, weights[1], 0.0
            )
            coarse = mix.astype(BF16)
            terms += [coarse, (mix - coarse.astype(F32)).astype(BF16)]
        rows = back[batch][group * EXP_Y : (group + 1) * EXP_Y].reshape(
            EXP_Y * stride, WIDTH[batch]
        )
        both = dot(jnp.concatenate(terms, axis=0), rows)
        sums = [
            both[2 * side * TOK : (2 * side + 1) * TOK]
            + both[(2 * side + 1) * TOK : (2 * side + 2) * TOK]
            for side in range(len(shifts))
        ]
        return sums[0] if batch == 1 else jnp.concatenate(sums, axis=1)

    def plane_sum(group):
        for dy in range(1, EXP_Y):
            answer(1, group, dy).wait_recv()
        if group == 0:
            return blend(1, 0, place_cols[1], gates[1])
        gate_copies[group - 1].wait_recv()
        places = [turned(place_in[group, c : c + 1, :])[:, 0:1] for c in range(2)]
        weights = [turned(gate_in[group, c : c + 1, :])[:, 0:1] for c in range(2)]
        return blend(1, group, places, weights)

    half_rows = (slice(0, TOK // 2), slice(TOK // 2, TOK))

    def plane_sums():
        part_out[3] = plane_sum(3).astype(BF16)
        for half in range(2):
            far_copy(half).start()
        for group in (1, 2):
            total = plane_sum(group)
            near, far = half_rows[group - 1], half_rows[2 - group]
            part_out[group, far] = total[far].astype(BF16)
            part_copy(group, 2 - group).start()
            hidden_part[group - 1] = total[near]

    def pass_on():
        for group in (1, 2):
            near = half_rows[group - 1]
            far_copy(group - 1).wait_recv()
            total = hidden_part[group - 1] + red_in[group - 1].astype(F32)
            part_out[group, near] = total.astype(BF16)
            part_copy(group, group - 1).start()

    def finish_one():
        result = hidden[0]
        for group in range(EXP_Z):
            for dy in range(EXP_Y):
                if group + dy > 0:
                    answer(0, group, dy).wait_recv()
            result = result + blend(0, group, place_cols[0], gates[0])
        out_ref[0, 0] = result.astype(BF16)

    def finish_two():
        result = hidden[1] + plane_sum(0)
        for group in (1, 2):
            for half in range(2):
                part_copy(group, half).wait_recv()
        result = result + part_in[1].astype(F32) + part_in[2].astype(F32)
        out_ref[1, 0] = result.astype(BF16)

    prepare(1, True)
    find_starts(1)
    attention(1, True)
    front(1, True)
    attention(0, False)
    spread(1)
    spread(2)
    front(0, False)
    spread(3)
    for copy in late[3:]:
        copy.wait()
    serve_all(1, 0, EXP_Z)
    plane_sums()
    serve_all(0, 0, 2)
    pass_on()
    serve_all(0, 2, EXP_Z)
    finish_one()
    finish_two()

    for batch in range(2):
        for group in range(EXP_Z):
            for dy in range(EXP_Y):
                if dy > 0 or (batch == 0 and group > 0):
                    dispatch(batch, group, dy).wait_send()
                    answer(batch, group, dy).wait_send()
        for step in range(1, PAIRS):
            context_copy(batch, lax.rem(pair + step, PAIRS)).wait_send()

    for group in range(1, EXP_Z):
        place_copies[group - 1].wait_send()
        gate_copies[group - 1].wait_send()
        for half in range(2):
            token_copy(group, half).wait_send()
            if group < 3:
                part_copy(group, half).wait_send()
    for half in range(2):
        far_copy(half).wait_send()

    @pl.when(upper == 0)
    def _():
        seg_hop.wait_send()
        for batch in range(2):
            sink_hop(batch).wait_send()
            for kind in range(2):
                halo_hop(batch, kind).wait_send()


def local(
    tokens,
    queries,
    key_rows,
    value_rows,
    segments,
    bias_table,
    out_proj,
    router,
    gate_weight,
    up_weight,
    down_weight,
    old_table,
    new_table,
    routes_one,
    routes_two,
):
    any_spec = pl.BlockSpec(memory_space=pl.ANY)
    vmem = pltpu.VMEM
    dma = pltpu.SemaphoreType.DMA
    buffers = [vmem((N_EXP, stride, width), BF16) for stride, width in zip(STRIDE, WIDTH)]
    return pl.pallas_call(
        layer_kernel,
        out_shape=jax.ShapeDtypeStruct((2, 1, TOK, D), BF16),
        in_specs=[any_spec] * 15,
        out_specs=pl.BlockSpec(memory_space=pltpu.VMEM),
        scratch_shapes=[
            vmem((N_EXP, NBUCK), F32),
            vmem((2, 2, TOK), I32),
            vmem((2, 1, N_EXP), I32),
            vmem((2, LANES), I32),
            vmem((N_EXP, D), BF16),
            vmem((2, 1, TOK, D), BF16),
            vmem((D, D), BF16),
            vmem((D, FFW), BF16),
            vmem((D, FFW), BF16),
            vmem((FFW, D), BF16),
            vmem((2, N_SEQ, 1, TOK), I32),
            vmem((2, PAIRS, TOK, LANES), BF16),
            vmem((2, PAIRS + WIN, TOK, LANES), BF16),
            vmem((2, PAIRS + WIN, TOK, LANES), BF16),
            vmem((N_SEQ, TOK, TOK), I32),
            vmem((WIN, 2 * TOK, TOK), F32),
            vmem((2, 2, 8, LANES), F32),
            vmem((2, 2, 8, LANES), F32),
            vmem((2, 8, LANES), F32),
            vmem((2, PAIRS, TOK, LANES), BF16),
            vmem((2, TOK, D), BF16),
            vmem((2, TOK, D), F32),
            vmem((TOK, D), BF16),
            *buffers,
            *buffers,
            *buffers,
            *buffers,
            vmem((EXP_Y * STRIDE[1], FFW), BF16),
            dma((11,)),
            dma((2, 3, PAIRS)),
            dma((2, 3, PAIRS)),
            dma((2, 3)),
            dma((PAIRS,)),
            dma((PAIRS,)),
            dma(()),
            dma((5,)),
            dma((5,)),
            dma((2,)),
            dma((2,)),
            dma((2, PAIRS)),
            dma((2, PAIRS)),
            dma((2,)),
            dma((2, N_EXP)),
            dma((2, N_EXP)),
            dma((2, N_EXP)),
            dma((2, N_EXP)),
            vmem((EXP_Z, TOK, D), BF16),
            vmem((EXP_Z, 2, TOK), F32),
            vmem((2, TOK), F32),
            dma((EXP_Z, 2)),
            dma((EXP_Z, 2)),
            dma((EXP_Z,)),
            dma((EXP_Z,)),
            vmem((EXP_Z, 2, TOK), F32),
            vmem((2, TOK), F32),
            dma((EXP_Z,)),
            dma((EXP_Z,)),
            vmem((EXP_Z, TOK, D), BF16),
            vmem((EXP_Z, TOK, D), BF16),
            vmem((2, TOK // 2, D), BF16),
            dma((EXP_Z, 2)),
            dma((EXP_Z, 2)),
            dma((2,)),
            dma((2,)),
            vmem((2, TOK // 2, D), F32),
        ],
        compiler_params=pltpu.CompilerParams(
            collective_id=0, has_side_effects=True, vmem_limit_bytes=56 << 20
        ),
        name="layer",
    )(
        bias_table,
        segments,
        queries,
        key_rows,
        value_rows,
        tokens,
        out_proj,
        router.T,
        jnp.swapaxes(routes_one, 1, 2),
        jnp.swapaxes(routes_two, 1, 2),
        old_table[None],
        new_table[None],
        gate_weight,
        up_weight,
        down_weight,
    )


def solution(mesh):
    placed = (
        P(None, "exp", "seq", None),
        P(None, "exp", "seq", None),
        P(None, "exp", "seq", None),
        P(None, "exp", "seq", None),
        P(None, "exp", "seq"),
        P(),
        P(),
        P(),
        P("exp", None, None),
        P("exp", None, None),
        P("exp", None, None),
        P(),
        P(),
        P("exp", "seq", None),
        P("exp", "seq", None),
    )
    return jax.shard_map(
        local, mesh=mesh, in_specs=placed, out_specs=P(None, "exp", "seq", None), check_vma=False
    )
```

```python
import jax
import jax.numpy as jnp
from jax import lax
from jax.experimental import pallas as pl
from jax.experimental.pallas import tpu as pltpu
from jax.sharding import PartitionSpec as P

MESH = pl.DeviceIdType.MESH
BF16 = jnp.bfloat16
F32 = jnp.float32
I32 = jnp.int32

N_SEQ = 16
N_EXP = 16
EXP_Y = 4
EXP_Z = 4
TOK = 128
D = 1024
FFW = 1408
NBUCK = 32
WIN = 4
PAIRS = 8
LANES = 128
HALF = 64
CAP = 20
STRIDE = (48, 48)
SENT = (40, 40)
WIDTH = (512, 1024)
PACK = 32
SINK_BUCKET = 31

EPSILON = 1e-06
MASKED = -1e30


def iota(shape, dim):
    return lax.broadcasted_iota(I32, shape, dim)


def dot(a, b):
    return jnp.dot(a, b, preferred_element_type=F32)


def dot_t(a, b):
    return lax.dot_general(a, b, (((1,), (1,)), ((), ())), preferred_element_type=F32)


def turned(row):
    return jnp.transpose(jnp.broadcast_to(row, (LANES, LANES)))


def remote(src, dst, send, recv, **device):
    return pltpu.make_async_remote_copy(
        src_ref=src,
        dst_ref=dst,
        send_sem=send,
        recv_sem=recv,
        device_id=device,
        device_id_type=MESH,
    )


def bias_of_distance(distance, values):
    result = jnp.broadcast_to(values[0], distance.shape)
    for bucket in range(1, 10):
        result = jnp.where(distance >= (1 << (bucket - 1)), values[bucket], result)
    return result


def plane_step(group):
    return group + (group // 2) * (1 - 2 * lax.rem(group, 2))


def layer_kernel(
    bias_hbm,
    seg_hbm,
    q_hbm,
    k_hbm,
    v_hbm,
    tok_hbm,
    proj_hbm,
    router_hbm,
    one_hbm,
    two_hbm,
    old_hbm,
    new_hbm,
    gate_hbm,
    up_hbm,
    down_hbm,
    out_ref,
    table,
    routes,
    held,
    tabs,
    router,
    tok,
    proj,
    gate_w,
    up_w,
    down_w,
    segs,
    qb,
    kb,
    vb,
    segcol,
    bias,
    sink_out,
    sink_in,
    sink_rows,
    ctx_out,
    ctx_in,
    hidden,
    normed,
    sbuf_one,
    sbuf_two,
    rbuf_one,
    rbuf_two,
    ybuf_one,
    ybuf_two,
    back_one,
    back_two,
    active,
    load_sem,
    qkv_send,
    qkv_recv,
    qkv_own,
    seg_send,
    seg_recv,
    seg_own,
    hop_send,
    hop_recv,
    sink_send,
    sink_recv,
    ctx_send,
    ctx_recv,
    ctx_own,
    go_send,
    go_recv,
    back_send,
    back_recv,
    tok_in,
    place_in,
    place_out,
    tok_send,
    tok_recv,
    place_send,
    place_recv,
    gate_in,
    gate_out,
    gate_send,
    gate_recv,
    part_out,
    part_in,
    red_in,
    part_send,
    part_recv,
    red_send,
    red_recv,
    hidden_part,
):
    me = lax.axis_index("seq")
    my_exp = lax.axis_index("exp")
    upper, pair = me // PAIRS, lax.rem(me, PAIRS)
    me_y, me_z = my_exp // EXP_Z, lax.rem(my_exp, EXP_Z)
    first_of_half = upper * PAIRS
    across = lax.rem(me + PAIRS, N_SEQ)
    sbuf, rbuf = (sbuf_one, sbuf_two), (rbuf_one, rbuf_two)
    ybuf, back = (ybuf_one, ybuf_two), (back_one, back_two)

    early = [
        pltpu.make_async_copy(src, dst, load_sem.at[i])
        for i, (src, dst) in enumerate(
            (
                (old_hbm, held.at[0]),
                (new_hbm, held.at[1]),
                (one_hbm.at[0], routes.at[0]),
                (two_hbm.at[0], routes.at[1]),
                (bias_hbm, table),
            )
        )
    ]
    late = [
        pltpu.make_async_copy(src, dst, load_sem.at[i + 5])
        for i, (src, dst) in enumerate(
            (
                (router_hbm, router),
                (tok_hbm, tok),
                (proj_hbm, proj),
                (gate_hbm.at[0], gate_w),
                (up_hbm.at[0], up_w),
                (down_hbm.at[0], down_w),
            )
        )
    ]
    for copy in early:
        copy.start()

    for batch in range(2):
        low = STRIDE[batch] - 16
        back[batch][:, low:, :] = jnp.zeros((N_EXP, 16, WIDTH[batch]), BF16)
    rbuf[0][:, STRIDE[0] - 16 :, :] = jnp.zeros((N_EXP, 16, WIDTH[0]), BF16)

    @pl.when(upper == 0)
    def _():
        for batch in range(2):
            kb[batch, 0:WIN] = jnp.zeros((WIN, TOK, LANES), BF16)
            vb[batch, 0:WIN] = jnp.zeros((WIN, TOK, LANES), BF16)
            segs[batch, 0:PAIRS] = jnp.full((PAIRS, 1, TOK), -1, I32)
            sink_in[batch] = jnp.zeros((2, 8, LANES), F32)

    barrier = pltpu.get_barrier_semaphore()
    for step in range(1, PAIRS):
        pl.semaphore_signal(
            barrier,
            inc=1,
            device_id={"seq": first_of_half + lax.rem(pair + step, PAIRS)},
            device_id_type=MESH,
        )
    pl.semaphore_signal(barrier, inc=1, device_id={"seq": across}, device_id_type=MESH)
    for step in range(1, N_EXP):
        pl.semaphore_signal(
            barrier,
            inc=1,
            device_id={"exp": lax.rem(my_exp + step, N_EXP)},
            device_id_type=MESH,
        )
    pl.semaphore_wait(barrier, PAIRS + N_EXP - 1)

    def lanes_of(which):
        return pl.ds(pl.multiple_of(which * LANES, LANES), LANES)

    def qkv_parts(batch, target):
        lanes = lanes_of(target)
        return (
            (k_hbm.at[batch, 0, :, lanes], kb.at[batch, pair + WIN]),
            (v_hbm.at[batch, 0, :, lanes], vb.at[batch, pair + WIN]),
            (q_hbm.at[batch, 0, :, lanes], qb.at[batch, pair]),
        )

    def qkv_copies(batch):
        copies = []
        for step in range(1, PAIRS):
            target = lax.rem(pair + step, PAIRS)
            for kind, (src, dst) in enumerate(qkv_parts(batch, target)):
                copies.append(
                    remote(
                        src,
                        dst,
                        qkv_send.at[batch, kind, step],
                        qkv_recv.at[batch, kind, step],
                        seq=first_of_half + target,
                    )
                )
        for kind, (src, dst) in enumerate(qkv_parts(batch, pair)):
            copies.append(pltpu.make_async_copy(src, dst, qkv_own.at[batch, kind]))
        return copies

    qkv = [qkv_copies(batch) for batch in range(2)]
    seg_copies = [
        remote(
            seg_hbm,
            segs.at[:, PAIRS + pair],
            seg_send.at[step],
            seg_recv.at[step],
            seq=first_of_half + lax.rem(pair + step, PAIRS),
        )
        for step in range(1, PAIRS)
    ]
    seg_copies.append(pltpu.make_async_copy(seg_hbm, segs.at[:, PAIRS + pair], seg_own))
    seg_hop = remote(
        segs.at[:, PAIRS : 2 * PAIRS],
        segs.at[:, 0:PAIRS],
        hop_send.at[4],
        hop_recv.at[4],
        seq=across,
    )

    def halo_hop(batch, kind):
        block = (kb, vb)[kind]
        return remote(
            block.at[batch, PAIRS : PAIRS + WIN],
            block.at[batch, 0:WIN],
            hop_send.at[2 * batch + kind],
            hop_recv.at[2 * batch + kind],
            seq=across,
        )

    def sink_hop(batch):
        return remote(
            sink_out.at[batch],
            sink_in.at[batch],
            sink_send.at[batch],
            sink_recv.at[batch],
            seq=across,
        )

    for copy in seg_copies:
        copy.start()
    for copy in qkv[1]:
        copy.start()
    for copy in late:
        copy.start()
    for copy in early:
        copy.wait()

    qi = iota((TOK, TOK), 0)
    kj = iota((TOK, TOK), 1)
    for head in range(2):
        head_row = table[pl.ds(2 * pair + head, 1), :]
        values = [head_row[:, bucket : bucket + 1] for bucket in range(10)]
        rows = slice(head * TOK, (head + 1) * TOK)
        merged = jnp.where(kj <= qi, qi - kj, qi - kj + WIN * TOK)
        bias[0, rows, :] = bias_of_distance(merged, values)
        for block in range(1, WIN):
            bias[block, rows, :] = bias_of_distance(qi - kj + (WIN - block) * TOK, values)
    sink_bias = jnp.where(
        iota((2 * TOK, 1), 0) < TOK,
        table[pl.ds(2 * pair, 1), :][:, SINK_BUCKET : SINK_BUCKET + 1],
        table[pl.ds(2 * pair + 1, 1), :][:, SINK_BUCKET : SINK_BUCKET + 1],
    )

    lane = iota((LANES, LANES), 1)
    row = iota((LANES, LANES), 0)
    tabs[...] = jnp.full((2, LANES), -1, I32)
    tabs[0:1, 0:N_EXP] = held[0]
    tabs[1:2, 0:N_EXP] = held[1]
    steps_y = lax.rem(row // EXP_Z - me_y + 2 * EXP_Y * EXP_Y, EXP_Y)
    steps_z = lax.rem(lax.rem(row, EXP_Z) - me_z + EXP_Z, EXP_Z)
    groups = steps_z + (steps_z // 2) * (1 - 2 * lax.rem(steps_z, 2))
    slot_of_row = (groups * EXP_Y + steps_y).astype(F32)
    holds = turned(tabs[0:1, :]) == lane
    slot_of_expert = jnp.sum(jnp.where(holds, slot_of_row, 0.0), axis=0, keepdims=True)
    new_row = tabs[1:2, :]
    new_col = turned(new_row)
    served = new_col == lane
    serving = jnp.where(served, 1.0, 0.0).astype(BF16)
    slot_two = jnp.sum(jnp.where(served, slot_of_expert, 0.0), axis=1, keepdims=True)
    again = jnp.where((new_col == new_row) & (lane < row), 1.0, 0.0)
    again = jnp.sum(again, axis=1, keepdims=True)
    base_two = jnp.transpose(
        jnp.broadcast_to(slot_two * STRIDE[1] + again * CAP, (LANES, LANES))
    )[0:1, :]
    bases = (slot_of_expert * STRIDE[0], base_two)
    lower = jnp.where(row > lane, 1.0, 0.0).astype(BF16)
    place_cols, place_rows, differences = [], [], []
    for batch in range(2):
        member = [
            jnp.where(turned(routes[batch, c : c + 1, :]) == lane, 1.0, 0.0) for c in range(2)
        ]
        counts = [dot(lower, m.astype(BF16)) for m in member]
        counts[1] = counts[1] + jnp.sum(member[0], axis=0, keepdims=True)
        cols = [
            jnp.sum(m * (c + bases[batch]), axis=1, keepdims=True)
            for m, c in zip(member, counts)
        ]
        place_cols.append(cols)
        place_rows.append(
            [jnp.transpose(jnp.broadcast_to(col, (TOK, TOK)))[0:1, :] for col in cols]
        )
        difference = member[0] - member[1]
        if batch == 1:
            difference = dot(difference.astype(BF16), serving)
        differences.append(difference)
    for c in range(2):
        place_out[c : c + 1, :] = place_rows[1][c]
    place_in[0] = place_out[...]

    def plane(step):
        return me_y * EXP_Z + lax.rem(me_z + step, EXP_Z)

    place_copies = [
        remote(
            place_out,
            place_in.at[group],
            place_send.at[group],
            place_recv.at[group],
            exp=plane(step),
        )
        for group, step in ((1, 1), (2, 3), (3, 2))
    ]
    for copy in place_copies:
        copy.start()
    gate_copies = [
        remote(
            gate_out,
            gate_in.at[group],
            gate_send.at[group],
            gate_recv.at[group],
            exp=plane(step),
        )
        for group, step in ((1, 1), (2, 3), (3, 2))
    ]

    def part_copy(group, half):
        rows = slice(half * (TOK // 2), (half + 1) * (TOK // 2))
        return remote(
            part_out.at[group, rows],
            part_in.at[group, rows],
            part_send.at[group, half],
            part_recv.at[group, half],
            exp=plane((3, 1)[group - 1]),
        )

    def far_copy(half):
        rows = slice(half * (TOK // 2), (half + 1) * (TOK // 2))
        return remote(
            part_out.at[3, rows],
            red_in.at[half],
            red_send.at[half],
            red_recv.at[half],
            exp=plane((3, 1)[half]),
        )

    def token_copy(group, half):
        rows = slice(half * (TOK // 2), (half + 1) * (TOK // 2))
        origin = 1 + half if group == 3 else 0
        step = (1, 3)[half] if group == 3 else (1, 3)[group - 1]
        return remote(
            tok_in.at[origin, rows],
            tok_in.at[group, rows],
            tok_send.at[group, half],
            tok_recv.at[group, half],
            exp=plane(step),
        )

    def relay():
        for half in range(2):
            token_copy(1 + half, half).wait_recv()
            token_copy(3, half).start()

    lane_head = iota((2 * TOK, LANES), 1) // HALF
    row_head = iota((2 * TOK, LANES), 0) // TOK
    own_half = lane_head == row_head
    causal = lax.rem(iota((2 * TOK, TOK), 0), TOK) >= iota((2 * TOK, TOK), 1)

    def twice(value):
        return jnp.concatenate([value, value], axis=0)

    def context_copy(batch, block):
        return remote(
            ctx_out.at[batch, block],
            ctx_in.at[batch, :, lanes_of(pair)],
            ctx_send.at[batch, block],
            ctx_recv.at[batch, pair],
            seq=first_of_half + block,
        )

    def context_own(batch):
        return pltpu.make_async_copy(
            ctx_out.at[batch, pair], ctx_in.at[batch, :, lanes_of(pair)], ctx_own.at[batch]
        )

    def prepare(batch, opening):
        if opening:
            for copy in seg_copies:
                copy.wait()

            @pl.when(upper == 0)
            def _():
                seg_hop.start()

        soon = 12 if opening else 0
        for copy in qkv[batch][:soon]:
            copy.wait()
        if opening:
            for copy in qkv[0]:
                copy.start()
        for copy in qkv[batch][soon:]:
            copy.wait()

        @pl.when(upper == 0)
        def _():
            for kind in range(2):
                halo_hop(batch, kind).start()

        if opening:

            @pl.when(upper == 1)
            def _():
                seg_hop.wait_recv()

        def columns(block, before):
            line = segs[batch, block]
            segcol[block] = turned(line)
            document = iota((8, TOK), 0)
            return before + jnp.where((line < document) & (line >= 0), 1, 0)

        ahead = lax.fori_loop(0, 2 * PAIRS, columns, jnp.zeros((8, TOK), I32))
        starts = jnp.sum(ahead, axis=1, keepdims=True)

        def sinks(block, sums):
            k_sum, v_sum = sums
            spot = (upper * PAIRS + block) * TOK + iota((8, TOK), 1)
            pick = jnp.where(spot == starts, 1.0, 0.0).astype(BF16)
            return (
                k_sum + dot(pick, kb[batch, block + WIN]),
                v_sum + dot(pick, vb[batch, block + WIN]),
            )

        zero = jnp.zeros((8, LANES), F32)
        k_sink, v_sink = lax.fori_loop(0, PAIRS, sinks, (zero, zero))
        sink_out[batch, 0] = k_sink
        sink_out[batch, 1] = v_sink

        @pl.when(upper == 0)
        def _():
            sink_hop(batch).start()

    def attention(batch, opening):
        @pl.when(upper == 1)
        def _():
            sink_hop(batch).wait_recv()

        sink_rows[0] = sink_out[batch, 0] + sink_in[batch, 0]
        sink_rows[1] = sink_out[batch, 1] + sink_in[batch, 1]

        def attend(block):
            query = twice(qb[batch, block].astype(F32) * 0.125)
            query = jnp.where(own_half, query, 0.0)
            query_rows = query.astype(BF16)
            mine = segcol[block + PAIRS]
            pieces = []
            for near in range(WIN + 1):
                raw = dot_t(query_rows, kb[batch, block + near])
                same = twice(mine == segs[batch, block + near + WIN])
                pieces.append((raw, same))
            merged = jnp.where(causal, pieces[WIN][0], pieces[0][0])
            merged_same = jnp.where(
                causal, pieces[WIN][1].astype(I32), pieces[0][1].astype(I32)
            )
            scores = [jnp.where(merged_same > 0, merged + bias[0], MASKED)]
            for near in range(1, WIN):
                raw, same = pieces[near]
                scores.append(jnp.where(same, raw + bias[near], MASKED))
            chosen_doc = iota((8, LANES), 0) == segs[batch, block + PAIRS][:, 0:1]
            k_row = jnp.sum(jnp.where(chosen_doc, sink_rows[0], 0.0), axis=0, keepdims=True)
            v_row = jnp.sum(jnp.where(chosen_doc, sink_rows[1], 0.0), axis=0, keepdims=True)
            sink_seen = twice(mine[:, 0:1] == segcol[block + WIN][:, 0:1])
            sink = jnp.sum(query * k_row, axis=1, keepdims=True) + sink_bias
            sink = jnp.where(sink_seen, sink, MASKED)
            peak = jnp.maximum(
                jnp.maximum(scores[0], scores[1]), jnp.maximum(scores[2], scores[3])
            )
            peak = jnp.maximum(jnp.max(peak, axis=1, keepdims=True), sink)
            weights = [jnp.exp(score - peak) for score in scores]
            sink_weight = jnp.exp(sink - peak)
            total = (weights[0] + weights[1]) + (weights[2] + weights[3])
            total = jnp.sum(total, axis=1, keepdims=True) + sink_weight
            mixed = sink_weight * v_row
            mixed = mixed + dot(jnp.where(causal, 0.0, weights[0]).astype(BF16), vb[batch, block])
            mixed = mixed + dot(
                jnp.where(causal, weights[0], 0.0).astype(BF16), vb[batch, block + WIN]
            )
            for near in range(1, WIN):
                mixed = mixed + dot(weights[near].astype(BF16), vb[batch, block + near])
            mixed = mixed / total
            ctx_out[batch, block] = jnp.where(
                lane_head[:TOK] == 0, mixed[:TOK], mixed[TOK:]
            ).astype(BF16)

            @pl.when(block == pair)
            def _():
                context_own(batch).start()

            @pl.when(block != pair)
            def _():
                context_copy(batch, block).start()

        def attend_late(turn, carry):
            attend(WIN + lax.rem(pair + turn, WIN))
            return carry

        def attend_early(turn, carry):
            attend(lax.rem(pair + turn, WIN))
            return carry

        lax.fori_loop(0, WIN, attend_late, 0)
        if not opening:
            relay()

        @pl.when(upper == 1)
        def _():
            for kind in range(2):
                halo_hop(batch, kind).wait_recv()

        lax.fori_loop(0, WIN, attend_early, 0)

    def target_of(group, dy, sign):
        y = lax.rem(me_y + EXP_Y + sign * dy, EXP_Y)
        z = lax.rem(me_z + EXP_Z + sign * plane_step(group), EXP_Z)
        return y * EXP_Z + z

    def beside(dy):
        return lax.rem(me_y + dy, EXP_Y) * EXP_Z + me_z

    def dispatch(batch, group, dy):
        slot = group * EXP_Y + dy
        rows = slice(0, SENT[batch])
        return remote(
            sbuf[batch].at[slot, rows],
            rbuf[batch].at[slot, rows],
            go_send.at[batch, slot],
            go_recv.at[batch, slot],
            exp=beside(dy) if batch == 1 else target_of(group, dy, 1),
        )

    def answer(batch, group, dy):
        slot = group * EXP_Y + dy
        rows = slice(0, SENT[batch])
        return remote(
            ybuf[batch].at[slot, rows],
            back[batch].at[slot, rows],
            back_send.at[batch, slot],
            back_recv.at[batch, slot],
            exp=beside(EXP_Y - dy) if batch == 1 else target_of(group, dy, -1),
        )

    gates = [None, None]

    def pick(batch, group, places, source):
        stride = STRIDE[batch]
        spot = (iota((EXP_Y * stride, TOK), 0) + group * EXP_Y * stride).astype(F32)
        hit = (spot == places[0]) | (spot == places[1])
        plan = jnp.where(hit, 1.0, 0.0).astype(BF16)
        if batch == 0:
            hit = (spot == places[0] + CAP) | (spot == places[1] + CAP)
            other = jnp.where(hit, 1.0, 0.0).astype(BF16)
            halves = dot(plan, source[:, : WIDTH[0]]) + dot(other, source[:, WIDTH[0] :])
            sbuf[0][group * EXP_Y : (group + 1) * EXP_Y] = halves.astype(BF16).reshape(
                EXP_Y, stride, WIDTH[0]
            )
            return
        for part in range(2):
            cols = slice(part * 512, (part + 1) * 512)
            sbuf[batch][group * EXP_Y : (group + 1) * EXP_Y, :, cols] = (
                dot(plan, source[:, cols]).astype(BF16).reshape(EXP_Y, stride, 512)
            )

    def spread(group):
        if group > 0:
            place_copies[group - 1].wait_recv()
            for half in range(2):
                if (group, half) not in ((1, 0), (2, 1)):
                    token_copy(group, half).wait_recv()
        places = [place_in[group, c : c + 1, :] for c in range(2)]
        pick(1, group, places, tok_in.at[group])
        for dy in range(1, EXP_Y):
            dispatch(1, group, dy).start()
        rbuf[1][group * EXP_Y] = sbuf[1][group * EXP_Y]

    def front(batch, opening):
        for step in range(1, PAIRS):
            source = lax.rem(pair + step, PAIRS)
            remote(
                ctx_out.at[batch, source],
                ctx_in.at[batch, :, lanes_of(source)],
                ctx_send.at[batch, source],
                ctx_recv.at[batch, source],
                seq=first_of_half + source,
            ).wait_recv()
        context_own(batch).wait()
        if opening:
            for copy in late[:3]:
                copy.wait()
        context = ctx_in[batch]
        for part in range(2):
            cols = slice(part * 512, (part + 1) * 512)
            hidden[batch, :, cols] = tok[batch, 0, :, cols].astype(F32) + dot(
                context, proj[:, cols]
            )
        value = hidden[batch]
        scale = lax.rsqrt(jnp.mean(value * value, axis=1, keepdims=True) + EPSILON)
        rows_value = (value * scale).astype(BF16)
        if batch == 1:
            tok_in[0] = rows_value
            for group, half in ((1, 0), (2, 1), (1, 1), (2, 0)):
                token_copy(group, half).start()
            spread(0)
            source = tok_in[0]
        else:
            normed[...] = rows_value
            for group in (3, 1, 2, 0):
                pick(batch, group, place_rows[0], normed)
                for dy in range(EXP_Y):
                    if group + dy > 0:
                        dispatch(batch, group, dy).start()
            rbuf[batch][0] = sbuf[batch][0]
            source = normed[...]
        logits = dot_t(source, router[...])
        picked = jnp.sum(differences[batch][:, :N_EXP] * logits, axis=1, keepdims=True)
        first = jax.nn.sigmoid(picked)
        gates[batch] = (first, 1.0 - first)
        if batch == 1:
            for c in range(2):
                gate_out[c : c + 1, :] = jnp.transpose(
                    jnp.broadcast_to(gates[batch][c], (TOK, TOK))
                )[0:1, :]
            gate_in[0] = gate_out[...]
            for copy in gate_copies:
                copy.start()

    def serve_all(batch, low, high):
        stride = STRIDE[batch]
        count = EXP_Y * (stride if batch == 1 else PACK)
        if batch == 0:
            inner_row = iota((PACK, EXP_Y * stride), 0)
            inner_col = iota((PACK, EXP_Y * stride), 1)
            outer_row = iota((stride, EXP_Y * PACK), 0)
            outer_col = iota((stride, EXP_Y * PACK), 1)
            unpack, pack = [], []
            for side in range(2):
                near, far = [], []
                for dy in range(EXP_Y):
                    hit = inner_col == inner_row + (dy * stride + side * CAP)
                    near.append(jnp.where(hit & (inner_row < CAP), 1.0, 0.0))
                    hit = outer_col == outer_row + (dy * PACK - side * CAP)
                    inside = (outer_row >= side * CAP) & (outer_row < (side + 1) * CAP)
                    far.append(jnp.where(hit & inside, 1.0, 0.0))
                unpack.append(jnp.concatenate(near, axis=0).astype(BF16))
                pack.append(jnp.concatenate(far, axis=0).astype(BF16))

        def serve(turn, carry):
            group = lax.rem(turn + 1, EXP_Z)
            for dy in range(EXP_Y):
                if dy == 0 and batch == 1:
                    continue
                if dy == 0:

                    @pl.when(group > 0)
                    def _():
                        dispatch(batch, group, dy).wait_recv()

                else:
                    dispatch(batch, group, dy).wait_recv()
            arrived = rbuf[batch][pl.ds(group * EXP_Y, EXP_Y)].reshape(
                EXP_Y * stride, WIDTH[batch]
            )
            if batch == 0:
                inputs = jnp.concatenate(
                    [dot(unpack[side], arrived).astype(BF16) for side in range(2)], axis=1
                )
            else:
                inputs = arrived
            for low, high in ((0, 512), (512, 1024), (1024, FFW)):
                gate = dot(inputs, gate_w[:, low:high])
                up = dot(inputs, up_w[:, low:high])
                inner = 0.7978845608028654 * (gate + 0.044715 * (gate * gate * gate))
                active[0:count, low:high] = (0.5 * gate * (1.0 + jnp.tanh(inner)) * up).astype(
                    BF16
                )
            if batch == 0:
                outs = [
                    dot(active[0:count], down_w[:, side * 512 : (side + 1) * 512]).astype(BF16)
                    for side in range(2)
                ]
                halves = dot(pack[0], outs[0]) + dot(pack[1], outs[1])
                ybuf[0][pl.ds(group * EXP_Y, EXP_Y)] = halves.astype(BF16).reshape(
                    EXP_Y, stride, WIDTH[0]
                )
            for part in range(2 * batch):
                cols = slice(part * 512, (part + 1) * 512)
                ybuf[batch][pl.ds(group * EXP_Y, EXP_Y), :, cols] = (
                    dot(active[0:count], down_w[:, cols])
                    .astype(BF16)
                    .reshape(EXP_Y, stride, 512)
                )
            for dy in range(EXP_Y):
                if dy == 0 and batch == 1:
                    back[1][group * EXP_Y] = ybuf[1][group * EXP_Y]
                elif dy == 0:

                    @pl.when(group > 0)
                    def _():
                        answer(batch, group, dy).start()

                else:
                    answer(batch, group, dy).start()
            return carry

        lax.fori_loop(low, high, serve, 0)
        if batch == 0 and high == EXP_Z:
            back[batch][0] = ybuf[batch][0]

    def blend(batch, group, places, weights):
        stride = STRIDE[batch]
        spot = (iota((TOK, EXP_Y * stride), 1) + group * EXP_Y * stride).astype(F32)
        shifts = (0, CAP) if batch == 0 else (0,)
        terms = []
        for shift in shifts:
            mix = jnp.where(spot == places[0] + shift, weights[0], 0.0) + jnp.where(
                spot == places[1] + shift, weights[1], 0.0
            )
            coarse = mix.astype(BF16)
            terms += [coarse, (mix - coarse.astype(F32)).astype(BF16)]
        rows = back[batch][group * EXP_Y : (group + 1) * EXP_Y].reshape(
            EXP_Y * stride, WIDTH[batch]
        )
        both = dot(jnp.concatenate(terms, axis=0), rows)
        sums = [
            both[2 * side * TOK : (2 * side + 1) * TOK]
            + both[(2 * side + 1) * TOK : (2 * side + 2) * TOK]
            for side in range(len(shifts))
        ]
        return sums[0] if batch == 1 else jnp.concatenate(sums, axis=1)

    def plane_sum(group):
        for dy in range(1, EXP_Y):
            answer(1, group, dy).wait_recv()
        if group == 0:
            return blend(1, 0, place_cols[1], gates[1])
        gate_copies[group - 1].wait_recv()
        places = [turned(place_in[group, c : c + 1, :])[:, 0:1] for c in range(2)]
        weights = [turned(gate_in[group, c : c + 1, :])[:, 0:1] for c in range(2)]
        return blend(1, group, places, weights)

    half_rows = (slice(0, TOK // 2), slice(TOK // 2, TOK))

    def plane_sums():
        part_out[3] = plane_sum(3).astype(BF16)
        for half in range(2):
            far_copy(half).start()
        for group in (1, 2):
            total = plane_sum(group)
            near, far = half_rows[group - 1], half_rows[2 - group]
            part_out[group, far] = total[far].astype(BF16)
            part_copy(group, 2 - group).start()
            hidden_part[group - 1] = total[near]

    def pass_on():
        for group in (1, 2):
            near = half_rows[group - 1]
            far_copy(group - 1).wait_recv()
            total = hidden_part[group - 1] + red_in[group - 1].astype(F32)
            part_out[group, near] = total.astype(BF16)
            part_copy(group, group - 1).start()

    def finish_one():
        result = hidden[0]
        for group in range(EXP_Z):
            for dy in range(EXP_Y):
                if group + dy > 0:
                    answer(0, group, dy).wait_recv()
            result = result + blend(0, group, place_cols[0], gates[0])
        out_ref[0, 0] = result.astype(BF16)

    def finish_two():
        result = hidden[1] + plane_sum(0)
        for group in (1, 2):
            for half in range(2):
                part_copy(group, half).wait_recv()
        result = result + part_in[1].astype(F32) + part_in[2].astype(F32)
        out_ref[1, 0] = result.astype(BF16)

    prepare(1, True)
    attention(1, True)
    prepare(0, False)
    front(1, True)
    attention(0, False)
    spread(1)
    spread(2)
    front(0, False)
    spread(3)
    for copy in late[3:]:
        copy.wait()
    serve_all(1, 0, EXP_Z)
    plane_sums()
    serve_all(0, 0, 2)
    pass_on()
    serve_all(0, 2, EXP_Z)
    finish_one()
    finish_two()

    for batch in range(2):
        for group in range(EXP_Z):
            for dy in range(EXP_Y):
                if dy > 0 or (batch == 0 and group > 0):
                    dispatch(batch, group, dy).wait_send()
                    answer(batch, group, dy).wait_send()
        for step in range(1, PAIRS):
            context_copy(batch, lax.rem(pair + step, PAIRS)).wait_send()

    for group in range(1, EXP_Z):
        place_copies[group - 1].wait_send()
        gate_copies[group - 1].wait_send()
        for half in range(2):
            token_copy(group, half).wait_send()
            if group < 3:
                part_copy(group, half).wait_send()
    for half in range(2):
        far_copy(half).wait_send()

    @pl.when(upper == 0)
    def _():
        seg_hop.wait_send()
        for batch in range(2):
            sink_hop(batch).wait_send()
            for kind in range(2):
                halo_hop(batch, kind).wait_send()


def local(
    tokens,
    queries,
    key_rows,
    value_rows,
    segments,
    bias_table,
    out_proj,
    router,
    gate_weight,
    up_weight,
    down_weight,
    old_table,
    new_table,
    routes_one,
    routes_two,
):
    any_spec = pl.BlockSpec(memory_space=pl.ANY)
    vmem = pltpu.VMEM
    dma = pltpu.SemaphoreType.DMA
    buffers = [vmem((N_EXP, stride, width), BF16) for stride, width in zip(STRIDE, WIDTH)]
    return pl.pallas_call(
        layer_kernel,
        out_shape=jax.ShapeDtypeStruct((2, 1, TOK, D), BF16),
        in_specs=[any_spec] * 15,
        out_specs=pl.BlockSpec(memory_space=pltpu.VMEM),
        scratch_shapes=[
            vmem((N_EXP, NBUCK), F32),
            vmem((2, 2, TOK), I32),
            vmem((2, 1, N_EXP), I32),
            vmem((2, LANES), I32),
            vmem((N_EXP, D), BF16),
            vmem((2, 1, TOK, D), BF16),
            vmem((D, D), BF16),
            vmem((D, FFW), BF16),
            vmem((D, FFW), BF16),
            vmem((FFW, D), BF16),
            vmem((2, N_SEQ, 1, TOK), I32),
            vmem((2, PAIRS, TOK, LANES), BF16),
            vmem((2, PAIRS + WIN, TOK, LANES), BF16),
            vmem((2, PAIRS + WIN, TOK, LANES), BF16),
            vmem((N_SEQ, TOK, TOK), I32),
            vmem((WIN, 2 * TOK, TOK), F32),
            vmem((2, 2, 8, LANES), F32),
            vmem((2, 2, 8, LANES), F32),
            vmem((2, 8, LANES), F32),
            vmem((2, PAIRS, TOK, LANES), BF16),
            vmem((2, TOK, D), BF16),
            vmem((2, TOK, D), F32),
            vmem((TOK, D), BF16),
            *buffers,
            *buffers,
            *buffers,
            *buffers,
            vmem((EXP_Y * STRIDE[1], FFW), BF16),
            dma((11,)),
            dma((2, 3, PAIRS)),
            dma((2, 3, PAIRS)),
            dma((2, 3)),
            dma((PAIRS,)),
            dma((PAIRS,)),
            dma(()),
            dma((5,)),
            dma((5,)),
            dma((2,)),
            dma((2,)),
            dma((2, PAIRS)),
            dma((2, PAIRS)),
            dma((2,)),
            dma((2, N_EXP)),
            dma((2, N_EXP)),
            dma((2, N_EXP)),
            dma((2, N_EXP)),
            vmem((EXP_Z, TOK, D), BF16),
            vmem((EXP_Z, 2, TOK), F32),
            vmem((2, TOK), F32),
            dma((EXP_Z, 2)),
            dma((EXP_Z, 2)),
            dma((EXP_Z,)),
            dma((EXP_Z,)),
            vmem((EXP_Z, 2, TOK), F32),
            vmem((2, TOK), F32),
            dma((EXP_Z,)),
            dma((EXP_Z,)),
            vmem((EXP_Z, TOK, D), BF16),
            vmem((EXP_Z, TOK, D), BF16),
            vmem((2, TOK // 2, D), BF16),
            dma((EXP_Z, 2)),
            dma((EXP_Z, 2)),
            dma((2,)),
            dma((2,)),
            vmem((2, TOK // 2, D), F32),
        ],
        compiler_params=pltpu.CompilerParams(
            collective_id=0, has_side_effects=True, vmem_limit_bytes=56 << 20
        ),
        name="layer",
    )(
        bias_table,
        segments,
        queries,
        key_rows,
        value_rows,
        tokens,
        out_proj,
        router.T,
        jnp.swapaxes(routes_one, 1, 2),
        jnp.swapaxes(routes_two, 1, 2),
        old_table[None],
        new_table[None],
        gate_weight,
        up_weight,
        down_weight,
    )


def solution(mesh):
    placed = (
        P(None, "exp", "seq", None),
        P(None, "exp", "seq", None),
        P(None, "exp", "seq", None),
        P(None, "exp", "seq", None),
        P(None, "exp", "seq"),
        P(),
        P(),
        P(),
        P("exp", None, None),
        P("exp", None, None),
        P("exp", None, None),
        P(),
        P(),
        P("exp", "seq", None),
        P("exp", "seq", None),
    )
    return jax.shard_map(
        local, mesh=mesh, in_specs=placed, out_specs=P(None, "exp", "seq", None), check_vma=False
    )
```
